32 devices in a mesh: dp: 4 (over y, x), seq: 8 (over z, core).
Axes of the slice: x: 2, y: 2, z: 4, core: 2. Of those that a mesh axis runs over, the one named last changes fastest.
Arguments:
- tokens: bfloat16 [4096, 1024], P(('dp', 'seq')), may hold values from -6 to 6
- w_query: bfloat16 [1024, 256], P(('dp', 'seq')), may hold values from -0.25 to 0.25
- w_key: bfloat16 [1024, 256], P(('dp', 'seq')), may hold values from -0.25 to 0.25
- w_value: bfloat16 [1024, 1024], P(('dp', 'seq')), may hold values from -0.1875 to 0.1875
- w_output: bfloat16 [1024, 1024], P(None, ('dp', 'seq')), may hold values from -1.5 to 1.5
- w_gate: bfloat16 [1024, 2752], P(('dp', 'seq')), may hold values from -0.1875 to 0.1875
- w_up: bfloat16 [1024, 2752], P(('dp', 'seq')), may hold values from -0.1875 to 0.1875
- w_down: bfloat16 [2752, 1024], P(None, ('dp', 'seq')), may hold values from -0.109375 to 0.109375
- norm_attn: bfloat16 [1024], P(('dp', 'seq')), may hold values from 0.099609375 to 1.8984375
- norm_mlp: bfloat16 [1024], P(('dp', 'seq')), may hold values from 0.099609375 to 1.8984375
- cotangent: bfloat16 [4096, 1024], P(('dp', 'seq')), may hold values from -6 to 6
Outputs:
- layer_out: bfloat16 [4096, 1024], P(('dp', 'seq'))
- grad_tokens: float32 [4096, 1024], P(('dp', 'seq'))
- grad_query: float32 [1024, 256], P(('dp', 'seq'))
- grad_key: float32 [1024, 256], P(('dp', 'seq'))
- grad_value: float32 [1024, 1024], P(('dp', 'seq'))
- grad_output: float32 [1024, 1024], P(None, ('dp', 'seq'))
- grad_gate: float32 [1024, 2752], P(('dp', 'seq'))
- grad_up: float32 [1024, 2752], P(('dp', 'seq'))
- grad_down: float32 [2752, 1024], P(None, ('dp', 'seq'))
- grad_norm_attn: float32 [1024], P(('dp', 'seq'))
- grad_norm_mlp: float32 [1024], P(('dp', 'seq'))
The draws below stay inside these ranges and needn't reach their ends.
All inputs are finite; a program needn't handle non-finite values.
Results may differ from the reference program's by a relative error of at most 0.02.
Values may be sent and summed in bfloat16 or wider, within the bound.
A program may use at most 192 MiB of HBM per device.

```python
import math
import jax
import jax.numpy as jnp
from jax import lax

D = 1024
FF = 2752
HEADS = 16
FEAT_DIM = 16
HEAD_V = 64
TOK_DEV = 128
TOKENS = 4096
N_DP = 4
N_SEQ = 8


def spiked(drawn, stream_key, source, target, shards_of, factor):
    def block_of(dim):
        return (jnp.arange(drawn.shape[dim]) // (drawn.shape[dim] // shards_of)).reshape((-1,) + (1,) * (drawn.ndim - 1 - dim))

    first = jax.random.permutation(stream_key, shards_of)[block_of(target)]
    other_side = (block_of(target) + shards_of // 2) % shards_of
    return jnp.where((block_of(source) == first) | (block_of(source) == other_side), factor * drawn, drawn)


def shard_levels(own_key, dims, cuts, least, top_value):
    def one(position, parts):
        heights = jax.random.uniform(jax.random.fold_in(jax.random.fold_in(own_key, 6), position), (parts,), jnp.float32, least / len(cuts), top_value / len(cuts))
        return jnp.repeat(jnp.exp(heights), dims[position] // parts).reshape((-1,) + (1,) * (len(dims) - position - 1))

    gain = one(*cuts[0])
    for cut in cuts[1:]:
        gain = gain * one(*cut)
    return gain


def scatter_about(stream_key, shape, deviation, bound, cuts=(), held_as=jnp.bfloat16):
    values = jax.random.normal(stream_key, shape, jnp.float32) * deviation
    if len(cuts) > 0:
        values = shard_levels(stream_key, shape, cuts, -0.22, 0.18) * values
    return jnp.clip(values, min=-bound, max=bound).astype(held_as)


def gaussian_with(stream_key, shape, deviation, most, split, heavy, held_as=jnp.bfloat16):
    drawn = deviation * jax.random.normal(stream_key, shape, jnp.float32)
    if split:
        drawn = drawn * shard_levels(stream_key, shape, split, -0.22, 0.18)
    return jnp.clip(spiked(drawn, jax.random.fold_in(stream_key, 3), *heavy), -most, most).astype(held_as)


def setup_inputs(seed: int = 0) -> dict:
    keys = jax.random.split(jax.random.key(seed), 12)
    tokens = gaussian_with(keys[0], (TOKENS, D), 1.0, 6.0, ((0, 32),), (0, 1, 32, 2.75))
    w_query = scatter_about(keys[1], (D, HEADS * FEAT_DIM), (D // 2) ** -0.5, 0.25, ((0, 32),))
    w_key = scatter_about(keys[2], (D, HEADS * FEAT_DIM), (D // 2) ** -0.5, 0.25, ((0, 32),))
    w_value = scatter_about(keys[3], (D, HEADS * HEAD_V), D ** -0.5, 0.1875, ((0, 32),))
    w_output = scatter_about(keys[4], (HEADS * HEAD_V, D), (D // 64) ** -0.5, 1.5, ((1, 32),))
    w_gate = scatter_about(keys[5], (D, FF), D ** -0.5, 0.1875, ((0, 32),))
    w_up = scatter_about(keys[6], (D, FF), D ** -0.5, 0.1875, ((0, 32),))
    w_down = scatter_about(keys[7], (FF, D), FF ** -0.5, 0.109375, ((1, 32),))
    norm_attn = jnp.clip(1.0 + 0.18 * jax.random.normal(keys[8], (D,), jnp.float32), 0.099609375, 1.8984375).astype(jnp.bfloat16)
    norm_mlp = jnp.clip(1.0 + 0.18 * jax.random.normal(keys[9], (D,), jnp.float32), 0.099609375, 1.8984375).astype(jnp.bfloat16)
    cotangent = gaussian_with(keys[10], (TOKENS, D), 1.0, 6.0, ((0, 32),), (0, 1, 32, 2.75))
    return {"tokens": tokens, "w_query": w_query, "w_key": w_key, "w_value": w_value, "w_output": w_output, "w_gate": w_gate, "w_up": w_up, "w_down": w_down, "norm_attn": norm_attn, "norm_mlp": norm_mlp, "cotangent": cotangent}


@jax.custom_vjp
def low(v):
    return lax.optimization_barrier(v.astype(jnp.bfloat16)).astype(jnp.float32)

@jax.custom_vjp
def low_back(v):
    return v

def low_keep(v):
    return (low(v), None)

def low_pass(kept, grad):
    return (grad,)

def back_keep(v):
    return (v, None)

def back_low(kept, grad):
    return (low(grad),)
low.defvjp(low_keep, low_pass)
low_back.defvjp(back_keep, back_low)
EPSILON = 1e-06
PRECISE = lax.Precision.HIGHEST

def product(operand, weight):
    return jnp.dot(operand, weight, precision=PRECISE)

def rms_norm(matrix, norm_gain):
    factor = lax.rsqrt(lax.optimization_barrier(jnp.mean(matrix * matrix, -1, keepdims=True)) + EPSILON)
    return matrix * factor * norm_gain

def features(source):
    width_in = source.shape[-1]
    constant = jnp.ones(source.shape[:-1] + (1,), jnp.float32)
    linear = source * width_in ** (-0.25)
    outer_prod = source[..., :, None] * source[..., None, :]
    square = outer_prod.reshape(source.shape[:-1] + (width_in * width_in,)) * (1.0 / (math.sqrt(2.0) * math.sqrt(width_in)))
    return jnp.concatenate([constant, linear, square], -1)

def split_heads(matrix, head_width):
    groups = matrix.shape[0] // TOK_DEV
    return matrix.reshape(groups, TOK_DEV, HEADS, head_width).transpose(0, 2, 1, 3)

def group_step(running, pieces):
    prefix, prefix_norm = running
    query_feat, key_feat, value_heads = pieces
    length = query_feat.shape[1]
    causal = (lax.broadcasted_iota(jnp.int32, (length, length), 0) >= lax.broadcasted_iota(jnp.int32, (length, length), 1)).astype(jnp.float32)
    scores = low_back(jnp.einsum('hif,hjf->hij', query_feat, key_feat, precision=PRECISE) * causal)
    numerator = low_back(jnp.einsum('hij,hjv->hiv', low(scores), value_heads, precision=PRECISE) + jnp.einsum('hif,hfv->hiv', query_feat, low(prefix), precision=PRECISE))
    denominator = lax.optimization_barrier(jnp.sum(scores, -1)) + jnp.einsum('hif,hf->hi', query_feat, prefix_norm, precision=PRECISE)
    group_state = low_back(jnp.einsum('hjf,hjv->hfv', key_feat, value_heads, precision=PRECISE))
    return ((prefix + group_state, prefix_norm + lax.optimization_barrier(jnp.sum(key_feat, 1))), numerator / denominator[..., None])

def layer(inputs, w_query, w_key, w_value, w_output, w_gate, w_up, w_down, norm_attn, norm_mlp):
    normed = low(rms_norm(inputs, norm_attn))
    queries = low(low_back(product(normed, w_query)))
    keys_low = low(low_back(product(normed, w_key)))
    values = low(low_back(product(normed, w_value)))
    query_feat = low(features(split_heads(queries, FEAT_DIM)))
    key_feat = low(features(split_heads(keys_low, FEAT_DIM)))
    value_heads = split_heads(values, HEAD_V)
    width_feat = query_feat.shape[-1]
    initial = (jnp.zeros((HEADS, width_feat, HEAD_V), jnp.float32), jnp.zeros((HEADS, width_feat), jnp.float32))
    _, attn_heads = lax.scan(jax.checkpoint(group_step), initial, (query_feat, key_feat, value_heads))
    attended = attn_heads.transpose(0, 2, 1, 3).reshape(inputs.shape[0], HEADS * HEAD_V)
    stream = inputs + low_back(product(low(low_back(attended)), w_output))
    normed_mlp = low(rms_norm(stream, norm_mlp))
    gate_pre = low_back(product(normed_mlp, w_gate))
    up_pre = low_back(product(normed_mlp, w_up))
    hidden = low(jax.nn.silu(gate_pre) * up_pre)
    return stream + low_back(product(hidden, w_down))

def reference(tokens, w_query, w_key, w_value, w_output, w_gate, w_up, w_down, norm_attn, norm_mlp, cotangent):
    weights = (w_query.astype(jnp.float32), w_key.astype(jnp.float32), w_value.astype(jnp.float32), w_output.astype(jnp.float32), w_gate.astype(jnp.float32), w_up.astype(jnp.float32), w_down.astype(jnp.float32), norm_attn.astype(jnp.float32), norm_mlp.astype(jnp.float32))
    length = TOK_DEV * N_SEQ
    inputs = tokens.astype(jnp.float32).reshape(N_DP, length, D)

    def forward(batch, *params):

        def single(sequence):
            return layer(sequence, *params)
        return lax.map(jax.checkpoint(single), batch)
    result, pullback = jax.vjp(forward, inputs, *weights)
    gradients = pullback(cotangent.astype(jnp.float32).reshape(N_DP, length, D))
    return (result.reshape(N_DP * length, D).astype(jnp.bfloat16), gradients[0].reshape(N_DP * length, D), gradients[1], gradients[2], gradients[3], gradients[4], gradients[5], gradients[6], gradients[7], gradients[8], gradients[9])
```

```python
import functools

import jax
import jax.numpy as jnp
from jax import lax
from jax.experimental import pallas as pl
from jax.experimental.pallas import tpu as pltpu
from jax.sharding import PartitionSpec as P

HEADS = 16
FEAT_DIM = 16
HEAD_V = 64
EPSILON = 1e-06
LANES = 128
MESH = pl.DeviceIdType.MESH
BF16 = jnp.bfloat16
F32 = jnp.float32


def round_up(size, unit):
    return -(-size // unit) * unit


def product(a, b):
    return jnp.dot(a, b, preferred_element_type=F32)


def product_nt(a, b):
    return lax.dot_general(a, b, (((1,), (1,)), ((), ())), preferred_element_type=F32)


def product_tn(a, b):
    return lax.dot_general(a, b, (((0,), (0,)), ((), ())), preferred_element_type=F32)


class Plan:
    def __init__(self, n_dp, n_seq, block, width, hidden):
        self.n_dp, self.n_seq, self.n_z = n_dp, n_seq, n_seq // 2
        self.block, self.width = block, width
        self.heads = HEADS // n_seq
        self.feat = self.heads * FEAT_DIM
        self.value = self.heads * HEAD_V
        self.unit = hidden // n_seq
        self.qk = round_up(2 * self.feat + 2, LANES)
        self.vp = round_up(self.value, LANES)
        self.fp = round_up(self.unit, LANES)
        self.rows = width // (n_dp * n_seq)
        self.band = width // n_dp
        self.at_v = self.qk
        self.at_o = self.at_v + self.vp
        self.at_gate = self.at_o + self.vp
        self.at_up = self.at_gate + self.fp
        self.at_down = self.at_up + self.fp
        self.cols = self.at_down + self.fp
        self.inline = self.rows % 16 == 0


def pack_weights(plan, w_query, w_key, w_value, w_output, w_gate, w_up, w_down, norm_attn, norm_mlp):
    s, r = plan.n_seq, plan.rows

    def cut(w, unit):
        return w.reshape(r, s, unit).transpose(1, 0, 2)

    def pad(parts, to):
        joined = jnp.concatenate(parts, -1) if len(parts) > 1 else parts[0]
        return jnp.pad(joined, ((0, 0), (0, 0), (0, to - joined.shape[-1])))

    gains = jnp.broadcast_to(jnp.stack([norm_attn, norm_mlp], -1), (s, r, 2))
    return jnp.concatenate(
        [
            pad([cut(w_query, plan.feat), cut(w_key, plan.feat), gains], plan.qk),
            pad([cut(w_value, plan.value)], plan.vp),
            pad([cut(w_output.T, plan.value)], plan.vp),
            pad([cut(w_gate, plan.unit)], plan.fp),
            pad([cut(w_up, plan.unit)], plan.fp),
            pad([cut(w_down.T, plan.unit)], plan.fp),
        ],
        -1,
    )


def unpack_grads(plan, owned):
    s, r = plan.n_seq, plan.rows

    def join(start, unit):
        return owned[:, :, start : start + unit].transpose(1, 0, 2).reshape(r, s * unit).astype(F32)

    at_gain = 2 * plan.feat
    gains = jnp.sum(owned[:, :, at_gain : at_gain + 2].astype(F32), 0)
    return (
        join(0, plan.feat),
        join(plan.feat, plan.feat),
        join(plan.at_v, plan.value),
        join(plan.at_o, plan.value).T,
        join(plan.at_gate, plan.unit),
        join(plan.at_up, plan.unit),
        join(plan.at_down, plan.unit).T,
        gains[:, 0],
        gains[:, 1],
    )


def layer_kernel(plan, *refs):
    p = plan
    (
        tok_ref, cot_ref, w_ref,
        out_ref, gtok_ref, grad_ref,
        TOK, NA, COT, NM, BM,
        W, G, GR, GS,
        Q, K, V, ATT, ATTF, DEN, BNUM, DQK, DV, DKF, DVF,
        H, BG, BU,
        PARTA, PARTB, SIB, CH, STREAM, BSTREAM,
        ag_send, ag_recv, sib_send, sib_recv, ch_send, ch_recv,
        w_send, w_recv, wd_send, wd_recv,
        g_send, g_recv, gz_send, gz_recv, local_sem,
    ) = refs
    dp, seq = lax.axis_index("dp"), lax.axis_index("seq")
    n_seq, n_z, n_dp, B, D = p.n_seq, p.n_z, p.n_dp, p.block, p.width
    z, core = seq // 2, seq % 2
    sibling = (dp, seq + 1 - 2 * core)
    above, below = (dp, seq + 2), (dp, seq - 2)
    is_top, is_bottom = z == n_z - 1, z == 0

    def remote(src, dst, send, recv, device):
        return pltpu.make_async_remote_copy(
            src_ref=src, dst_ref=dst, send_sem=send, recv_sem=recv,
            device_id=device, device_id_type=MESH,
        )

    def each_peer(count, mine, body):
        def one(i, carry):
            @pl.when(i != mine)
            def _():
                body(i)

            return carry

        lax.fori_loop(0, count, one, 0)

    def loop(count, body):
        def one(i, carry):
            body(i)
            return carry

        lax.fori_loop(0, count, one, 0)

    barrier = pltpu.get_barrier_semaphore()
    each_peer(n_seq, seq, lambda i: pl.semaphore_signal(barrier, inc=1, device_id=(dp, i), device_id_type=MESH))
    each_peer(n_dp, dp, lambda i: pl.semaphore_signal(barrier, inc=1, device_id=(i, seq), device_id_type=MESH))
    pl.semaphore_wait(barrier, n_seq - 1 + n_dp - 1)

    near = jnp.minimum(z, n_z - 1 - z)
    far_side = jnp.where(z < n_z - 1 - z, 1, -1)

    def order(k):
        step = (k + 1) // 2
        alternate = jnp.where(k % 2 == 1, -step, step)
        return z + jnp.where(k <= 2 * near, alternate, far_side * (k - near))

    def weight_cols(part):
        return pl.ds(0, p.at_gate) if part == 0 else pl.ds(p.at_gate, p.cols - p.at_gate)

    def piece_rows(d, s):
        return pl.ds(pl.multiple_of((d * n_seq + s) * p.rows, p.rows), p.rows)

    def band_rows(d):
        return pl.ds(pl.multiple_of(d * p.band, p.band), p.band)

    def piece_copy(part, s, mine):
        cols = weight_cols(part)
        src_of = seq if mine else s
        return remote(
            w_ref.at[s, :, cols], W.at[piece_rows(dp, src_of), cols],
            w_send.at[part, s], w_recv.at[part, src_of], (dp, s),
        )

    def band_copy(part, d, mine):
        cols = weight_cols(part)
        src_of = dp if mine else d
        return remote(
            W.at[band_rows(src_of), cols], W.at[band_rows(src_of), cols],
            wd_send.at[part, d], wd_recv.at[part, src_of], (d, seq),
        )

    def gather_copy(a, buf, j, way, device):
        return remote(buf.at[j], buf.at[j], ag_send.at[a, way, j], ag_recv.at[a, j], device)

    def gather_step(a, buf, k, on_block):
        def one(side):
            take = jnp.where(side == 0, k < n_z, k >= 1)

            @pl.when(take)
            def _():
                zk = order(k - side)
                j = 2 * zk + jnp.where(side == 0, core, 1 - core)

                @pl.when(j != seq)
                def _():
                    gather_copy(a, buf, j, 0, sibling).wait_recv()

                @pl.when(side == 0)
                def _():
                    @pl.when(jnp.logical_and(zk <= z, jnp.logical_not(is_top)))
                    def _():
                        gather_copy(a, buf, j, 0, above).start()

                    @pl.when(jnp.logical_and(zk >= z, jnp.logical_not(is_bottom)))
                    def _():
                        gather_copy(a, buf, j, 1, below).start()

                    gather_copy(a, buf, j, 2, sibling).start()

                if on_block is not None:
                    on_block(j)

        loop(2, one)

    def gather_drain(a, buf):
        def one(zk):
            j = 2 * zk + core

            @pl.when(jnp.logical_and(zk <= z, jnp.logical_not(is_top)))
            def _():
                gather_copy(a, buf, j, 0, above).wait_send()

            @pl.when(jnp.logical_and(zk >= z, jnp.logical_not(is_bottom)))
            def _():
                gather_copy(a, buf, j, 1, below).wait_send()

            gather_copy(a, buf, j, 2, sibling).wait_send()

        loop(n_z, one)

    def sibling_copy(i, part, zk):
        return remote(
            part.at[2 * zk + 1 - core], SIB.at[i % 3, zk], sib_send.at[i, zk], sib_recv.at[i, zk], sibling
        )

    def chain_copy(i, part, zk, up):
        slot = zk if up else jnp.where(zk == z - 1, n_z, zk)
        return remote(
            part.at[2 * zk + core], CH.at[i % 3, slot], ch_send.at[i, zk], ch_recv.at[i, slot],
            above if up else below,
        )

    def chain_wait(i, part, slot):
        remote(part.at[0], CH.at[i % 3, slot], ch_send.at[i, 0], ch_recv.at[i, slot], sibling).wait_recv()

    def sum_step(i, part, k, fill):
        @pl.when(k < n_z)
        def _():
            zk = order(n_z - 1 - k)
            if fill is not None:
                loop(2, lambda side: fill(2 * zk + jnp.where(side == 0, 1 - core, core)))
            sibling_copy(i, part, zk).start()

        @pl.when(jnp.logical_and(k >= 1, k <= n_z))
        def _():
            zk = order(n_z - k)
            j = 2 * zk + core
            remote(part.at[0], SIB.at[i % 3, zk], sib_send.at[i, zk], sib_recv.at[i, zk], sibling).wait_recv()

            @pl.when(zk != z)
            def _():
                first = jnp.where(zk > z, is_bottom, is_top)

                @pl.when(first)
                def _():
                    part[j] = (part[j].astype(F32) + SIB[i % 3, zk].astype(F32)).astype(BF16)

                @pl.when(jnp.logical_not(first))
                def _():
                    chain_wait(i, part, zk)
                    part[j] = (
                        part[j].astype(F32) + SIB[i % 3, zk].astype(F32) + CH[i % 3, zk].astype(F32)
                    ).astype(BF16)

                @pl.when(zk > z)
                def _():
                    chain_copy(i, part, zk, True).start()

                @pl.when(zk < z)
                def _():
                    chain_copy(i, part, zk, False).start()

    def sum_result(i, part, total):
        total[...] = part[seq].astype(F32) + SIB[i % 3, z].astype(F32)

        @pl.when(jnp.logical_not(is_bottom))
        def _():
            chain_wait(i, part, z)
            total[...] += CH[i % 3, z].astype(F32)

        @pl.when(jnp.logical_not(is_top))
        def _():
            chain_wait(i, part, n_z)
            total[...] += CH[i % 3, n_z].astype(F32)

    def sum_drain(i, part):
        def one(zk):
            sibling_copy(i, part, zk).wait_send()

            @pl.when(zk > z)
            def _():
                chain_copy(i, part, zk, True).wait_send()

            @pl.when(zk < z)
            def _():
                chain_copy(i, part, zk, False).wait_send()

        loop(n_z, one)

    if p.inline:
        each_peer(n_seq, seq, lambda s: piece_copy(0, s, True).start())
        own = pltpu.make_async_copy(w_ref.at[seq], W.at[piece_rows(dp, seq), :], local_sem.at[0])
        own.start()
        own.wait()
    else:
        own = pltpu.make_async_copy(w_ref, W, local_sem.at[0])
        own.start()
        own.wait()
    TOK[seq] = tok_ref[...]
    COT[seq] = cot_ref[...]
    loop(1, lambda k: gather_step(0, TOK, k, None))
    if p.inline:
        each_peer(n_seq, seq, lambda s: piece_copy(0, s, False).wait_recv())
        each_peer(n_dp, dp, lambda d: band_copy(0, d, True).start())
    loop(n_z, lambda k: gather_step(0, TOK, k + 1, None))
    if p.inline:
        each_peer(n_seq, seq, lambda s: piece_copy(1, s, True).start())
        each_peer(n_dp, dp, lambda d: band_copy(0, d, False).wait_recv())

    lane = lax.broadcasted_iota(jnp.int32, (1, p.qk), 1)
    vlane = lax.broadcasted_iota(jnp.int32, (1, p.vp), 1)
    feat_masks = [
        jnp.logical_and(lane >= h * FEAT_DIM, lane < (h + 1) * FEAT_DIM).astype(BF16) for h in range(p.heads)
    ]
    value_masks = [
        jnp.logical_and(vlane >= h * HEAD_V, vlane < (h + 1) * HEAD_V).astype(BF16) for h in range(p.heads)
    ]
    row = lax.broadcasted_iota(jnp.int32, (p.qk, p.qk), 0)
    col = lax.broadcasted_iota(jnp.int32, (p.qk, p.qk), 1)
    shift = jnp.logical_and(row == col + p.feat, col < p.feat).astype(F32).astype(BF16)
    at_gain = 2 * p.feat
    pick = lax.broadcasted_iota(jnp.int32, (16, p.qk), 0) + at_gain == lax.broadcasted_iota(
        jnp.int32, (16, p.qk), 1
    )
    gain_rows = product_nt(pick.astype(F32).astype(BF16), W[:, : p.qk])
    gain_attn, gain_mlp = gain_rows[0:1], gain_rows[1:2]
    scale = FEAT_DIM ** -0.5
    below_diag = lax.broadcasted_iota(jnp.int32, (B, B), 0) >= lax.broadcasted_iota(jnp.int32, (B, B), 1)

    def factor_of(x):
        return lax.rsqrt(jnp.mean(x * x, -1, keepdims=True) + EPSILON)

    def project(j):
        x = TOK[j].astype(F32)
        normed = (x * factor_of(x) * gain_attn).astype(BF16)
        NA[j] = normed
        qk = product(normed, W[:, : p.qk]).astype(BF16)
        Q[j] = qk
        K[j] = product(qk, shift).astype(BF16)
        V[j] = product(normed, W[:, p.at_v : p.at_o]).astype(BF16)

    loop(n_seq, project)

    def scores_of(query, key, allowed):
        t = product_nt(query, key) * scale
        s = jnp.where(allowed, 1.0 + t + 0.5 * t * t, 0.0)
        return t, s

    def attend(i):
        queries = Q[i]

        def inner(j, carry):
            num, sums = carry
            allowed = jnp.logical_or(below_diag, j < i)
            new_sums = []
            for h in range(p.heads):
                _, s = scores_of(queries * feat_masks[h], K[j], allowed)
                num = num + product(s.astype(BF16), V[j] * value_masks[h])
                new_sums.append(sums[h] + s)
            return num, tuple(new_sums)

        num, sums = lax.fori_loop(
            0, i + 1, inner,
            (jnp.zeros((B, p.vp), F32), tuple(jnp.zeros((B, B), F32) for _ in range(p.heads))),
        )
        den = jnp.ones((B, p.vp), F32)
        for h in range(p.heads):
            total = jnp.sum(sums[h], -1, keepdims=True)
            den = jnp.where(value_masks[h] > 0, total, den)
        att = num / den
        DEN[i] = den
        ATTF[i] = att
        ATT[i] = att.astype(BF16)
        PARTA[i] = product_nt(ATT[i], W[:, p.at_o : p.at_gate]).astype(BF16)

    def first_sum(k):
        sum_step(0, PARTA, k, attend)
        gather_step(1, COT, k, None)

    loop(n_z + 1, first_sum)
    sum_result(0, PARTA, STREAM)
    STREAM[...] += tok_ref[...].astype(F32)
    if p.inline:
        each_peer(n_seq, seq, lambda s: piece_copy(1, s, False).wait_recv())
        each_peer(n_dp, dp, lambda d: band_copy(1, d, True).start())

    stream = STREAM[...]
    NM[seq] = (stream * factor_of(stream) * gain_mlp).astype(BF16)
    loop(1, lambda k: gather_step(2, NM, k, None))
    sum_drain(0, PARTA)
    if p.inline:
        each_peer(n_dp, dp, lambda d: band_copy(1, d, False).wait_recv())

    def feed(j):
        normed = NM[j]
        gate = product(normed, W[:, p.at_gate : p.at_up])
        up = product(normed, W[:, p.at_up : p.at_down])
        back = product(COT[j], W[:, p.at_down : p.cols])
        sig = jax.nn.sigmoid(gate)
        act = gate * sig
        H[j] = (act * up).astype(BF16)
        BG[j] = (back * up * sig * (1.0 + gate * (1.0 - sig))).astype(BF16)
        BU[j] = (back * act).astype(BF16)
        PARTA[j] = (
            product_nt(BG[j], W[:, p.at_gate : p.at_up]) + product_nt(BU[j], W[:, p.at_up : p.at_down])
        ).astype(BF16)
        PARTB[j] = product_nt(H[j], W[:, p.at_down : p.cols]).astype(BF16)

    feed(seq)
    loop(n_z, lambda k: gather_step(2, NM, k + 1, feed))
    loop(n_z + 1, lambda k: sum_step(1, PARTA, k, None))
    sum_result(1, PARTA, BSTREAM)
    back_normed = BSTREAM[...]
    stream = STREAM[...]
    factor = factor_of(stream)
    n = stream * factor
    e = back_normed * gain_mlp
    BSTREAM[...] = cot_ref[...].astype(F32) + factor * (e - n * jnp.mean(e * n, -1, keepdims=True))
    BM[seq] = BSTREAM[...].astype(BF16)

    def all_rows(buf, d0, size):
        return buf[:, :, pl.ds(d0, size)].reshape(n_seq * B, size)

    def grad_tile(left, right, start, size):
        def one(i):
            d0 = pl.multiple_of(i * LANES, LANES)
            tile = product_tn(all_rows(left, d0, LANES), right[...].reshape(n_seq * B, size))
            G[pl.ds(d0, LANES), start : start + size] = tile.astype(BF16)

        loop(D // LANES, one)

    def back_of_weights(i):
        d0 = pl.multiple_of(i * LANES, LANES)
        rows = pl.ds(d0, LANES)
        normed = all_rows(NM, d0, LANES)
        tile_gate = product_tn(normed, BG[...].reshape(n_seq * B, p.fp))
        G[rows, p.at_gate : p.at_up] = tile_gate.astype(BF16)
        tile_up = product_tn(normed, BU[...].reshape(n_seq * B, p.fp))
        G[rows, p.at_up : p.at_down] = tile_up.astype(BF16)
        both = tile_gate * W[rows, p.at_gate : p.at_up].astype(F32) + tile_up * W[
            rows, p.at_up : p.at_down
        ].astype(F32)
        gain = W[rows, : p.qk].astype(F32)
        gain_grad = jnp.sum(both, -1, keepdims=True) / gain[:, at_gain + 1 : at_gain + 2]
        G[rows, : p.qk] = jnp.where(lane == at_gain + 1, gain_grad, 0.0).astype(BF16)

    def group_cols(part):
        return pl.ds(0, p.at_gate) if part == 0 else pl.ds(p.at_gate, p.cols - p.at_gate)

    def band_send(part, d, mine):
        cols = group_cols(part)
        src_of = dp if mine else d
        return remote(
            G.at[band_rows(d), cols], GR.at[src_of, :, cols], g_send.at[part, d], g_recv.at[part, src_of], (d, seq)
        )

    def piece_send(part, s, mine):
        cols = group_cols(part)
        src_of = seq if mine else s
        return remote(
            GS.at[pl.ds(pl.multiple_of(s * p.rows, p.rows), p.rows), cols], grad_ref.at[src_of, :, cols],
            gz_send.at[part, s], gz_recv.at[part, src_of], (dp, s),
        )

    def start_bands(part):
        if p.inline:
            each_peer(n_dp, dp, lambda d: band_send(part, d, True).start())

    def start_pieces(part):
        if not p.inline:
            return
        cols = group_cols(part)
        each_peer(n_dp, dp, lambda d: band_send(part, d, False).wait_recv())

        def one(i):
            rows = pl.ds(pl.multiple_of(i * p.rows, p.rows), p.rows)
            total = G[pl.ds(pl.multiple_of(dp * p.band + i * p.rows, p.rows), p.rows), cols].astype(F32)
            mine = total

            def add(d, acc):
                use = jnp.where(d == dp, 0.0, 1.0)
                return acc + use * jnp.where(d == dp, mine, GR[d, rows, cols].astype(F32))

            for step in range(1, n_dp):
                total = total + GR[lax.rem(dp + step, n_dp), rows, cols].astype(F32)
            GS[rows, cols] = total.astype(BF16)

        loop(n_seq, one)
        each_peer(n_seq, seq, lambda s: piece_send(part, s, True).start())
        grad_ref[seq, :, cols] = GS[pl.ds(pl.multiple_of(seq * p.rows, p.rows), p.rows), cols]

    loop(1, lambda k: gather_step(3, BM, k, None))
    loop(D // LANES, back_of_weights)
    grad_tile(COT, H, p.at_down, p.fp)
    start_bands(1)

    def back_heads(j):
        back = product(BM[j], W[:, p.at_o : p.at_gate]).astype(BF16).astype(F32)
        den = DEN[j]
        BNUM[j] = (back / den).astype(BF16)
        prod = back * ATTF[j]
        out = jnp.zeros((B, p.vp), F32)
        for h in range(p.heads):
            total = jnp.sum(prod * value_masks[h].astype(F32), -1, keepdims=True)
            out = jnp.where(value_masks[h] > 0, -total, out)
        ATTF[j] = out / den
        DKF[j] = jnp.zeros((B, p.qk), F32)
        DVF[j] = jnp.zeros((B, p.vp), F32)

    back_heads(seq)

    def third_sum(k):
        gather_step(3, BM, k + 1, back_heads)
        sum_step(2, PARTB, k, None)

    loop(n_z, third_sum)
    sum_step(2, PARTB, n_z, None)

    def attend_back(i):
        queries, numer, denom = Q[i], BNUM[i], ATTF[i]

        def inner(j, dq):
            allowed = jnp.logical_or(below_diag, j < i)
            dk, dv = DKF[j], DVF[j]
            for h in range(p.heads):
                qh, bh = queries * feat_masks[h], numer * value_masks[h]
                t, s = scores_of(qh, K[j], allowed)
                ds = product_nt(bh, V[j]) + denom[:, h * HEAD_V : h * HEAD_V + 1]
                dt = jnp.where(allowed, ds * (1.0 + t), 0.0).astype(BF16)
                dq = dq + product(dt, K[j] * feat_masks[h])
                dk = dk + product_tn(dt, qh)
                dv = dv + product_tn(s.astype(BF16), bh)
            DKF[j] = dk
            DVF[j] = dv
            return dq

        dq = lax.fori_loop(0, i + 1, inner, jnp.zeros((B, p.qk), F32))
        DQK[i] = (dq * scale).astype(BF16)

    loop(n_seq, attend_back)
    sum_drain(1, PARTA)

    def back_input(j):
        dk = (DKF[j] * scale).astype(BF16)
        qk = (DQK[j].astype(F32) + product_nt(dk, shift)).astype(BF16)
        DQK[j] = qk
        DV[j] = DVF[j].astype(BF16)
        PARTA[j] = (
            product_nt(qk, W[:, : p.qk]) + product_nt(DV[j], W[:, p.at_v : p.at_o])
        ).astype(BF16)

    loop(n_seq, back_input)
    loop(1, lambda k: sum_step(3, PARTA, k, None))

    def attention_weights(i):
        d0 = pl.multiple_of(i * LANES, LANES)
        rows = pl.ds(d0, LANES)
        normed = all_rows(NA, d0, LANES)
        tile_qk = product_tn(normed, DQK[...].reshape(n_seq * B, p.qk))
        tile_v = product_tn(normed, DV[...].reshape(n_seq * B, p.vp))
        G[rows, p.at_v : p.at_o] = tile_v.astype(BF16)
        tile_o = product_tn(all_rows(BM, d0, LANES), ATT[...].reshape(n_seq * B, p.vp))
        G[rows, p.at_o : p.at_gate] = tile_o.astype(BF16)
        own_qk = W[rows, : p.qk].astype(F32)
        gain_grad = (
            jnp.sum(jnp.where(lane < at_gain, tile_qk * own_qk, 0.0), -1, keepdims=True)
            + jnp.sum(tile_v * W[rows, p.at_v : p.at_o].astype(F32), -1, keepdims=True)
        ) / own_qk[:, at_gain : at_gain + 1]
        rest = jnp.where(lane == at_gain, gain_grad, G[rows, : p.qk].astype(F32))
        G[rows, : p.qk] = jnp.where(lane < at_gain, tile_qk, rest).astype(BF16)

    loop(D // LANES, attention_weights)
    start_bands(0)
    start_pieces(1)
    loop(n_z, lambda k: sum_step(3, PARTA, k + 1, None))
    start_pieces(0)

    sum_result(2, PARTB, gtok_ref)
    out_ref[...] = (STREAM[...] + gtok_ref[...]).astype(BF16)
    sum_result(3, PARTA, gtok_ref)
    x = tok_ref[...].astype(F32)
    factor = factor_of(x)
    m = x * factor
    f = gtok_ref[...] * gain_attn
    gtok_ref[...] = BSTREAM[...] + factor * (f - m * jnp.mean(f * m, -1, keepdims=True))

    if p.inline:
        for part in (1, 0):
            each_peer(n_seq, seq, lambda s: piece_send(part, s, False).wait_recv())
    else:
        done = pltpu.make_async_copy(G, grad_ref, local_sem.at[0])
        done.start()
        done.wait()

    gather_drain(0, TOK)
    gather_drain(1, COT)
    gather_drain(2, NM)
    gather_drain(3, BM)
    sum_drain(2, PARTB)
    sum_drain(3, PARTA)
    if p.inline:
        for part in (0, 1):
            each_peer(n_seq, seq, lambda s: piece_copy(part, s, True).wait_send())
            each_peer(n_dp, dp, lambda d: band_copy(part, d, True).wait_send())
            each_peer(n_dp, dp, lambda d: band_send(part, d, True).wait_send())
            each_peer(n_seq, seq, lambda s: piece_send(part, s, True).wait_send())


def run_layer(plan, tokens, cotangent, weights):
    p = plan
    n_seq, n_z, n_dp, B, D = p.n_seq, p.n_z, p.n_dp, p.block, p.width
    vmem = pl.BlockSpec(memory_space=pltpu.VMEM)
    grads = (n_seq, p.rows, p.cols) if p.inline else (D, p.cols)
    dma = pltpu.SemaphoreType.DMA

    def rows(width, kind=BF16):
        return pltpu.VMEM((n_seq, B, width), kind)

    band = p.band if p.inline else 16
    n_gr = n_dp if p.inline else 1
    return pl.pallas_call(
        functools.partial(layer_kernel, plan),
        out_shape=(
            jax.ShapeDtypeStruct((B, D), BF16),
            jax.ShapeDtypeStruct((B, D), F32),
            jax.ShapeDtypeStruct(grads, BF16),
        ),
        in_specs=[vmem] * 3,
        out_specs=(vmem, vmem, vmem if p.inline else pl.BlockSpec(memory_space=pl.ANY)),
        scratch_shapes=[
            rows(D), rows(D), rows(D), rows(D), rows(D),
            pltpu.VMEM((D, p.cols), BF16), pltpu.VMEM((D, p.cols), BF16),
            pltpu.VMEM((n_gr, band, p.cols), BF16), pltpu.VMEM((band, p.cols), BF16),
            rows(p.qk), rows(p.qk), rows(p.vp), rows(p.vp), rows(p.vp, F32), rows(p.vp, F32),
            rows(p.vp), rows(p.qk), rows(p.vp), rows(p.qk, F32), rows(p.vp, F32),
            rows(p.fp), rows(p.fp), rows(p.fp),
            rows(D), rows(D),
            pltpu.VMEM((3, n_z, B, D), BF16), pltpu.VMEM((3, n_z + 1, B, D), BF16),
            pltpu.VMEM((B, D), F32), pltpu.VMEM((B, D), F32),
            dma((4, 3, n_seq)), dma((4, n_seq)), dma((4, n_z)), dma((4, n_z)),
            dma((4, n_z)), dma((4, n_z + 1)),
            dma((2, n_seq)), dma((2, n_seq)), dma((2, n_dp)), dma((2, n_dp)),
            dma((2, n_dp)), dma((2, n_dp)), dma((2, n_seq)), dma((2, n_seq)), dma((1,)),
        ],
        compiler_params=pltpu.CompilerParams(
            collective_id=0, has_side_effects=True, vmem_limit_bytes=66_000_000
        ),
    )(tokens, cotangent, weights)


def on_device(tokens, w_query, w_key, w_value, w_output, w_gate, w_up, w_down, norm_attn, norm_mlp, cotangent):
    plan = Plan(
        lax.axis_size("dp"), lax.axis_size("seq"), tokens.shape[0], tokens.shape[1], w_gate.shape[1]
    )
    weights = pack_weights(
        plan, w_query, w_key, w_value, w_output, w_gate, w_up, w_down, norm_attn, norm_mlp
    )
    if not plan.inline:
        weights = lax.all_to_all(weights, "seq", split_axis=0, concat_axis=0, tiled=True)
        weights = lax.all_gather(weights, "dp").reshape(plan.width, plan.cols)
    layer_out, grad_tokens, grads = run_layer(plan, tokens, cotangent, weights)
    if not plan.inline:
        grads = lax.psum_scatter(grads, "dp", scatter_dimension=0, tiled=True)
        grads = grads.reshape(plan.n_seq, plan.rows, plan.cols)
        grads = lax.all_to_all(grads, "seq", split_axis=0, concat_axis=0, tiled=True)
    return (layer_out, grad_tokens) + unpack_grads(plan, grads)


def solution(mesh):
    rows, cols, vec = P(("dp", "seq"), None), P(None, ("dp", "seq")), P(("dp", "seq"))
    return jax.shard_map(
        on_device,
        mesh=mesh,
        in_specs=(rows, rows, rows, rows, cols, rows, rows, cols, vec, vec, rows),
        out_specs=(rows, rows, rows, rows, rows, cols, rows, rows, cols, vec, vec),
        check_vma=False,
    )
```

```python
import functools

import jax
import jax.numpy as jnp
from jax import lax
from jax.experimental import pallas as pl
from jax.experimental.pallas import tpu as pltpu
from jax.sharding import PartitionSpec as P

HEADS = 16
FEAT_DIM = 16
HEAD_V = 64
EPSILON = 1e-06
LANES = 128
MESH = pl.DeviceIdType.MESH
BF16 = jnp.bfloat16
F32 = jnp.float32


def round_up(size, unit):
    return -(-size // unit) * unit


def product(a, b):
    return jnp.dot(a, b, preferred_element_type=F32)


def product_nt(a, b):
    return lax.dot_general(a, b, (((1,), (1,)), ((), ())), preferred_element_type=F32)


def product_tn(a, b):
    return lax.dot_general(a, b, (((0,), (0,)), ((), ())), preferred_element_type=F32)


class Plan:
    def __init__(self, n_dp, n_seq, block, width, hidden):
        self.n_dp, self.n_seq, self.n_z = n_dp, n_seq, n_seq // 2
        self.block, self.width = block, width
        self.heads = HEADS // n_seq
        self.feat = self.heads * FEAT_DIM
        self.value = self.heads * HEAD_V
        self.unit = hidden // n_seq
        self.qk = round_up(2 * self.feat + 2, LANES)
        self.vp = round_up(self.value, LANES)
        self.fp = round_up(self.unit, LANES)
        self.rows = width // (n_dp * n_seq)
        self.band = width // n_dp
        self.at_v = self.qk
        self.at_gate = self.at_v + self.vp
        self.at_up = self.at_gate + self.fp
        self.at_down = self.at_up + self.fp
        self.cols = self.at_down + self.fp
        self.joined = n_seq * self.vp
        self.inline = self.rows % 16 == 0


def pack_weights(plan, w_query, w_key, w_value, w_gate, w_up, w_down, norm_attn, norm_mlp):
    s, r = plan.n_seq, plan.rows

    def cut(w, unit):
        return w.reshape(r, s, unit).transpose(1, 0, 2)

    def pad(parts, to):
        joined = jnp.concatenate(parts, -1) if len(parts) > 1 else parts[0]
        return jnp.pad(joined, ((0, 0), (0, 0), (0, to - joined.shape[-1])))

    gains = jnp.broadcast_to(jnp.stack([norm_attn, norm_mlp], -1), (s, r, 2))
    return jnp.concatenate(
        [
            pad([cut(w_query, plan.feat), cut(w_key, plan.feat), gains], plan.qk),
            pad([cut(w_value, plan.value)], plan.vp),
            pad([cut(w_gate, plan.unit)], plan.fp),
            pad([cut(w_up, plan.unit)], plan.fp),
            pad([cut(w_down.T, plan.unit)], plan.fp),
        ],
        -1,
    )


def pack_output(plan, w_output):
    heads = w_output.T.reshape(plan.rows, plan.n_seq, plan.value)
    return jnp.pad(heads, ((0, 0), (0, 0), (0, plan.vp - plan.value))).reshape(plan.rows, plan.joined)


def unpack_grads(plan, owned, owned_output):
    s, r = plan.n_seq, plan.rows

    def join(start, unit):
        return owned[:, :, start : start + unit].transpose(1, 0, 2).reshape(r, s * unit).astype(F32)

    at_gain = 2 * plan.feat
    gains = jnp.sum(owned[:, :, at_gain : at_gain + 2].astype(F32), 0)
    return (
        join(0, plan.feat),
        join(plan.feat, plan.feat),
        join(plan.at_v, plan.value),
        owned_output.reshape(r, s, plan.vp)[:, :, : plan.value].reshape(r, s * plan.value).T,
        join(plan.at_gate, plan.unit),
        join(plan.at_up, plan.unit),
        join(plan.at_down, plan.unit).T,
        gains[:, 0],
        gains[:, 1],
    )


def layer_kernel(plan, *refs):
    p = plan
    (
        tok_ref, cot_ref, w_ref, wo_ref,
        out_ref, gtok_ref, grad_ref, go_ref,
        TOK, NA, COT, NM, WO, GO, SO, DO, ZS, ZO, AO, BAT, BATT,
        W, G, GR, GS,
        Q, K, V, ATT, ATTF, DEN, BNUM, DQK, DV, DKF, DVF,
        H, BG, BU,
        PARTA, PARTB, SIB, CH, STREAM, BSTREAM,
        ag_send, ag_recv, sib_send, sib_recv, ch_send, ch_recv,
        w_send, w_recv, wd_send, wd_recv,
        g_send, g_recv, gz_send, gz_recv, local_sem,
        wo_send, wo_recv, wod_send, wod_recv, sl_send, sl_recv,
        go_send, go_recv, gd_send, gd_recv, at_send, at_recv, bt_send, bt_recv,
    ) = refs
    if not p.inline:
        GO = WO
    dp, seq = lax.axis_index("dp"), lax.axis_index("seq")
    n_seq, n_z, n_dp, B, D = p.n_seq, p.n_z, p.n_dp, p.block, p.width
    z, core = seq // 2, seq % 2
    sibling = (dp, seq + 1 - 2 * core)
    above, below = (dp, seq + 2), (dp, seq - 2)
    is_top, is_bottom = z == n_z - 1, z == 0

    def remote(src, dst, send, recv, device):
        return pltpu.make_async_remote_copy(
            src_ref=src, dst_ref=dst, send_sem=send, recv_sem=recv,
            device_id=device, device_id_type=MESH,
        )

    def each_peer(count, mine, body):
        def one(i, carry):
            @pl.when(i != mine)
            def _():
                body(i)

            return carry

        lax.fori_loop(0, count, one, 0)

    def loop(count, body):
        def one(i, carry):
            body(i)
            return carry

        lax.fori_loop(0, count, one, 0)

    barrier = pltpu.get_barrier_semaphore()
    each_peer(n_seq, seq, lambda i: pl.semaphore_signal(barrier, inc=1, device_id=(dp, i), device_id_type=MESH))
    each_peer(n_dp, dp, lambda i: pl.semaphore_signal(barrier, inc=1, device_id=(i, seq), device_id_type=MESH))
    pl.semaphore_wait(barrier, n_seq - 1 + n_dp - 1)

    near = jnp.minimum(z, n_z - 1 - z)
    far_side = jnp.where(z < n_z - 1 - z, 1, -1)

    def order(k):
        step = (k + 1) // 2
        alternate = jnp.where(k % 2 == 1, -step, step)
        return z + jnp.where(k <= 2 * near, alternate, far_side * (k - near))

    def weight_cols(part):
        return pl.ds(0, p.at_gate) if part == 0 else pl.ds(p.at_gate, p.cols - p.at_gate)

    def piece_rows(d, s):
        return pl.ds(pl.multiple_of((d * n_seq + s) * p.rows, p.rows), p.rows)

    def band_rows(d):
        return pl.ds(pl.multiple_of(d * p.band, p.band), p.band)

    def piece_copy(part, s, mine):
        cols = weight_cols(part)
        src_of = seq if mine else s
        return remote(
            w_ref.at[s, :, cols], W.at[piece_rows(dp, src_of), cols],
            w_send.at[part, s], w_recv.at[part, src_of], (dp, s),
        )

    def band_copy(part, d, mine):
        cols = weight_cols(part)
        src_of = dp if mine else d
        return remote(
            W.at[band_rows(src_of), cols], W.at[band_rows(src_of), cols],
            wd_send.at[part, d], wd_recv.at[part, src_of], (d, seq),
        )

    def gather_copy(a, buf, j, way, device):
        return remote(buf.at[j], buf.at[j], ag_send.at[a, way, j], ag_recv.at[a, j], device)

    def gather_step(a, buf, k, on_block):
        def one(side):
            take = jnp.where(side == 0, k < n_z, k >= 1)

            @pl.when(take)
            def _():
                zk = order(k - side)
                j = 2 * zk + jnp.where(side == 0, core, 1 - core)

                @pl.when(j != seq)
                def _():
                    gather_copy(a, buf, j, 0, sibling).wait_recv()

                @pl.when(side == 0)
                def _():
                    @pl.when(jnp.logical_and(zk <= z, jnp.logical_not(is_top)))
                    def _():
                        gather_copy(a, buf, j, 0, above).start()

                    @pl.when(jnp.logical_and(zk >= z, jnp.logical_not(is_bottom)))
                    def _():
                        gather_copy(a, buf, j, 1, below).start()

                    gather_copy(a, buf, j, 2, sibling).start()

                if on_block is not None:
                    on_block(j)

        loop(2, one)

    def gather_drain(a, buf):
        def one(zk):
            j = 2 * zk + core

            @pl.when(jnp.logical_and(zk <= z, jnp.logical_not(is_top)))
            def _():
                gather_copy(a, buf, j, 0, above).wait_send()

            @pl.when(jnp.logical_and(zk >= z, jnp.logical_not(is_bottom)))
            def _():
                gather_copy(a, buf, j, 1, below).wait_send()

            gather_copy(a, buf, j, 2, sibling).wait_send()

        loop(n_z, one)

    def sibling_copy(i, part, zk):
        return remote(
            part.at[2 * zk + 1 - core], SIB.at[i - 1, zk], sib_send.at[i, zk], sib_recv.at[i, zk], sibling
        )

    def chain_copy(i, part, zk, up):
        slot = zk if up else jnp.where(zk == z - 1, n_z, zk)
        return remote(
            part.at[2 * zk + core], CH.at[i - 1, slot], ch_send.at[i, zk], ch_recv.at[i, slot],
            above if up else below,
        )

    def chain_wait(i, part, slot):
        remote(part.at[0], CH.at[i - 1, slot], ch_send.at[i, 0], ch_recv.at[i, slot], sibling).wait_recv()

    def far(k):
        return order(n_z - 1 - k)

    def sum_step(i, part, k):
        zk = far(k)
        j = 2 * zk + core
        remote(part.at[0], SIB.at[i - 1, zk], sib_send.at[i, zk], sib_recv.at[i, zk], sibling).wait_recv()

        @pl.when(zk != z)
        def _():
            first = jnp.where(zk > z, is_bottom, is_top)

            @pl.when(first)
            def _():
                part[j] = (part[j].astype(F32) + SIB[i - 1, zk].astype(F32)).astype(BF16)

            @pl.when(jnp.logical_not(first))
            def _():
                chain_wait(i, part, zk)
                part[j] = (
                    part[j].astype(F32) + SIB[i - 1, zk].astype(F32) + CH[i - 1, zk].astype(F32)
                ).astype(BF16)

            @pl.when(zk > z)
            def _():
                chain_copy(i, part, zk, True).start()

            @pl.when(zk < z)
            def _():
                chain_copy(i, part, zk, False).start()

    def sum_result(i, part, total):
        total[...] = part[seq].astype(F32) + SIB[i - 1, z].astype(F32)

        @pl.when(jnp.logical_not(is_bottom))
        def _():
            chain_wait(i, part, z)
            total[...] += CH[i - 1, z].astype(F32)

        @pl.when(jnp.logical_not(is_top))
        def _():
            chain_wait(i, part, n_z)
            total[...] += CH[i - 1, n_z].astype(F32)

    def sum_drain(i, part):
        def one(zk):
            sibling_copy(i, part, zk).wait_send()

            @pl.when(zk > z)
            def _():
                chain_copy(i, part, zk, True).wait_send()

            @pl.when(zk < z)
            def _():
                chain_copy(i, part, zk, False).wait_send()

        loop(n_z, one)

    def slab_copy(zk, mine):
        src_of = z if mine else zk
        return remote(
            wo_ref, WO.at[dp, src_of, core], wo_send.at[zk], wo_recv.at[src_of], (dp, 2 * zk + core)
        )

    def slab_band(d, mine):
        src_of = dp if mine else d
        return remote(
            WO.at[src_of, :, core], WO.at[src_of, :, core], wod_send.at[d], wod_recv.at[src_of], (d, seq)
        )

    def slab_half(which):
        return remote(WO.at[:, :, which], WO.at[:, :, which], sl_send.at[0], sl_recv.at[0], sibling)

    def slab_sum_half():
        return remote(GO.at[:, :, 1 - core], SO, sl_send.at[1], sl_recv.at[1], sibling)

    def slab_sum_band(d, mine):
        src_of = dp if mine else d
        return remote(GO.at[d, :, core], DO.at[src_of], gd_send.at[d], gd_recv.at[src_of], (d, seq))

    def slab_sum(zk, mine):
        src_of = z if mine else zk
        return remote(ZS.at[zk], ZO.at[src_of], go_send.at[zk], go_recv.at[src_of], (dp, 2 * zk + core))

    def lanes_of(s):
        return pl.ds(pl.multiple_of(s * p.vp, p.vp), p.vp)

    def attended_copy(s, mine):
        src_of = seq if mine else s
        return remote(ATT.at[s], AO.at[:, lanes_of(src_of)], at_send.at[s], at_recv.at[src_of], (dp, s))

    def back_copy(s, mine):
        src_of = seq if mine else s
        return remote(BAT.at[:, lanes_of(s)], BATT.at[src_of], bt_send.at[s], bt_recv.at[src_of], (dp, s))

    if p.inline:
        each_peer(n_seq, seq, lambda s: piece_copy(0, s, True).start())
        own = pltpu.make_async_copy(w_ref.at[seq], W.at[piece_rows(dp, seq), :], local_sem.at[0])
        own.start()
        own.wait()
        own = pltpu.make_async_copy(wo_ref, WO.at[dp, z, core], local_sem.at[0])
        own.start()
        own.wait()
    else:
        own = pltpu.make_async_copy(w_ref, W, local_sem.at[0])
        own.start()
        own.wait()
        own = pltpu.make_async_copy(wo_ref, WO.at[0, 0, 0], local_sem.at[0])
        own.start()
        own.wait()
    TOK[seq] = tok_ref[...]
    COT[seq] = cot_ref[...]
    loop(1, lambda k: gather_step(0, TOK, k, None))
    if p.inline:
        each_peer(n_seq, seq, lambda s: piece_copy(0, s, False).wait_recv())
        each_peer(n_dp, dp, lambda d: band_copy(0, d, True).start())
    loop(1, lambda k: gather_step(0, TOK, k + 1, None))
    if p.inline:
        each_peer(n_z, z, lambda zk: slab_copy(zk, True).start())
    loop(n_z - 3, lambda k: gather_step(0, TOK, k + 2, None))
    if p.inline:
        each_peer(n_dp, dp, lambda d: band_copy(0, d, False).wait_recv())

    lane = lax.broadcasted_iota(jnp.int32, (1, p.qk), 1)
    vlane = lax.broadcasted_iota(jnp.int32, (1, p.vp), 1)
    feat_masks = [
        jnp.logical_and(lane >= h * FEAT_DIM, lane < (h + 1) * FEAT_DIM).astype(BF16) for h in range(p.heads)
    ]
    value_masks = [
        jnp.logical_and(vlane >= h * HEAD_V, vlane < (h + 1) * HEAD_V).astype(BF16) for h in range(p.heads)
    ]
    spare = (vlane >= p.value).astype(F32)
    row = lax.broadcasted_iota(jnp.int32, (p.qk, p.qk), 0)
    col = lax.broadcasted_iota(jnp.int32, (p.qk, p.qk), 1)
    shift = jnp.logical_and(row == col + p.feat, col < p.feat).astype(F32).astype(BF16)
    at_gain = 2 * p.feat
    pick = lax.broadcasted_iota(jnp.int32, (16, p.qk), 0) + at_gain == lax.broadcasted_iota(
        jnp.int32, (16, p.qk), 1
    )
    gain_rows = product_nt(pick.astype(F32).astype(BF16), W[:, : p.qk])
    gain_attn, gain_mlp = gain_rows[0:1], gain_rows[1:2]
    scale = FEAT_DIM ** -0.5
    one_lane = (lane == p.qk - 1).astype(F32)
    C = 2 * B
    below_diag = lax.broadcasted_iota(jnp.int32, (C, C), 0) >= lax.broadcasted_iota(jnp.int32, (C, C), 1)

    def factor_of(x):
        return lax.rsqrt(jnp.mean(x * x, -1, keepdims=True) + EPSILON)

    def project(j):
        x = TOK[j].astype(F32)
        normed = (x * factor_of(x) * gain_attn).astype(BF16)
        NA[j] = normed
        qk = product(normed, W[:, : p.qk]).astype(BF16)
        Q[j] = (qk.astype(F32) * scale).astype(BF16)
        K[j] = (product(qk, shift) + one_lane).astype(BF16)
        V[j] = product(normed, W[:, p.at_v : p.at_gate]).astype(BF16)

    loop(n_z - 1, lambda k: project(2 * order(k) + core))
    loop(n_z - 2, lambda k: project(2 * order(k) + 1 - core))
    loop(1, lambda k: gather_step(0, TOK, k + n_z - 1, project))
    if p.inline:
        each_peer(n_seq, seq, lambda s: piece_copy(1, s, True).start())
        each_peer(n_z, z, lambda zk: slab_copy(zk, False).wait_recv())
        each_peer(n_dp, dp, lambda d: slab_band(d, True).start())
    loop(1, lambda k: gather_step(0, TOK, k + n_z, project))

    def chip_rows(buf, i):
        return buf[pl.ds(2 * i, 2)].reshape(C, buf.shape[-1])

    def store_rows(buf, i, value):
        buf[pl.ds(2 * i, 2)] = value.reshape(2, B, value.shape[-1]).astype(buf.dtype)

    def one_plus_t(query, key):
        return product_nt(query, key)

    def query_of(queries, h):
        return queries * feat_masks[h] + one_lane.astype(BF16)

    def attend(i):
        queries = chip_rows(Q, i)

        def inner(j, acc, diagonal):
            keys, values = chip_rows(K, j), chip_rows(V, j)
            for h in range(p.heads):
                u = product_nt(query_of(queries, h), keys)
                s = 0.5 * u * u + 0.5
                if diagonal:
                    s = jnp.where(below_diag, s, 0.0)
                ones = jnp.broadcast_to(value_masks[h], (C, p.vp))
                acc = acc + product(s.astype(BF16), jnp.concatenate([values * value_masks[h], ones], -1))
            return acc

        acc = lax.fori_loop(0, i, lambda j, acc: inner(j, acc, False), jnp.zeros((C, 2 * p.vp), F32))
        acc = inner(i, acc, True)
        den = acc[:, p.vp :] + spare
        att = acc[:, : p.vp] / den
        store_rows(DEN, i, den)
        store_rows(ATTF, i, att)
        store_rows(ATT, i, att)

        def give(side):
            @pl.when(2 * i + side != seq)
            def _():
                attended_copy(2 * i + side, True).start()

        loop(2, give)

    loop(n_z, lambda k: attend(far(k)))
    loop(1, lambda k: gather_step(1, COT, k, None))
    AO[:, lanes_of(seq)] = ATT[seq]
    if p.inline:
        each_peer(n_seq, seq, lambda s: piece_copy(1, s, False).wait_recv())
        each_peer(n_dp, dp, lambda d: slab_band(d, False).wait_recv())
        slab_half(core).start()
        each_peer(n_dp, dp, lambda d: band_copy(1, d, True).start())
    each_peer(n_seq, seq, lambda s: attended_copy(s, False).wait_recv())
    if p.inline:
        slab_half(1 - core).wait_recv()
    STREAM[...] = tok_ref[...].astype(F32) + product_nt(AO[...], WO[...].reshape(D, p.joined))

    stream = STREAM[...]
    NM[seq] = (stream * factor_of(stream) * gain_mlp).astype(BF16)
    loop(1, lambda k: gather_step(2, NM, k, None))
    loop(1, lambda k: gather_step(1, COT, k + 1, None))
    if p.inline:
        each_peer(n_dp, dp, lambda d: band_copy(1, d, False).wait_recv())

    def feed(j):
        normed = NM[j]
        gate = product(normed, W[:, p.at_gate : p.at_up])
        up = product(normed, W[:, p.at_up : p.at_down])
        back = product(COT[j], W[:, p.at_down : p.cols])
        sig = jax.nn.sigmoid(gate)
        act = gate * sig
        H[j] = (act * up).astype(BF16)
        BG[j] = (back * up * sig * (1.0 + gate * (1.0 - sig))).astype(BF16)
        BU[j] = (back * act).astype(BF16)
        PARTA[j] = (
            product_nt(BG[j], W[:, p.at_gate : p.at_up]) + product_nt(BU[j], W[:, p.at_up : p.at_down])
        ).astype(BF16)
        PARTB[j] = product_nt(H[j], W[:, p.at_down : p.cols]).astype(BF16)

        @pl.when(j % 2 != core)
        def _():
            sibling_copy(1, PARTA, j // 2).start()
            sibling_copy(2, PARTB, j // 2).start()

    feed(seq)

    def feed_step(k):
        @pl.when(k + 2 <= n_z)
        def _():
            gather_step(1, COT, k + 2, None)

        gather_step(2, NM, k + 1, feed)

    loop(n_z, feed_step)
    def all_rows(buf, d0, size):
        return buf[:, :, pl.ds(d0, size)].reshape(n_seq * B, size)

    def back_of_weights(i):
        d0 = pl.multiple_of(i * LANES, LANES)
        rows = pl.ds(d0, LANES)
        normed = all_rows(NM, d0, LANES)
        tile_gate = product_tn(normed, BG[...].reshape(n_seq * B, p.fp))
        G[rows, p.at_gate : p.at_up] = tile_gate.astype(BF16)
        tile_up = product_tn(normed, BU[...].reshape(n_seq * B, p.fp))
        G[rows, p.at_up : p.at_down] = tile_up.astype(BF16)
        tile_down = product_tn(all_rows(COT, d0, LANES), H[...].reshape(n_seq * B, p.fp))
        G[rows, p.at_down : p.cols] = tile_down.astype(BF16)
        both = tile_gate * W[rows, p.at_gate : p.at_up].astype(F32) + tile_up * W[
            rows, p.at_up : p.at_down
        ].astype(F32)
        gain = W[rows, : p.qk].astype(F32)
        gain_grad = jnp.sum(both, -1, keepdims=True) / gain[:, at_gain + 1 : at_gain + 2]
        G[rows, : p.qk] = jnp.where(lane == at_gain + 1, gain_grad, 0.0).astype(BF16)

    def group_cols(part):
        return pl.ds(0, p.at_gate) if part == 0 else pl.ds(p.at_gate, p.cols - p.at_gate)

    def band_send(part, d, mine):
        cols = group_cols(part)
        src_of = dp if mine else d
        return remote(
            G.at[band_rows(d), cols], GR.at[src_of, :, cols], g_send.at[part, d], g_recv.at[part, src_of], (d, seq)
        )

    def piece_send(part, s, mine):
        cols = group_cols(part)
        src_of = seq if mine else s
        return remote(
            GS.at[pl.ds(pl.multiple_of(s * p.rows, p.rows), p.rows), cols], grad_ref.at[src_of, :, cols],
            gz_send.at[part, s], gz_recv.at[part, src_of], (dp, s),
        )

    def start_bands(part):
        if p.inline:
            each_peer(n_dp, dp, lambda d: band_send(part, d, True).start())

    def start_pieces(part):
        if not p.inline:
            return
        cols = group_cols(part)
        each_peer(n_dp, dp, lambda d: band_send(part, d, False).wait_recv())

        def one(i):
            rows = pl.ds(pl.multiple_of(i * p.rows, p.rows), p.rows)
            total = G[pl.ds(pl.multiple_of(dp * p.band + i * p.rows, p.rows), p.rows), cols].astype(F32)
            mine = total

            def add(d, acc):
                use = jnp.where(d == dp, 0.0, 1.0)
                return acc + use * jnp.where(d == dp, mine, GR[d, rows, cols].astype(F32))

            for step in range(1, n_dp):
                total = total + GR[lax.rem(dp + step, n_dp), rows, cols].astype(F32)
            GS[rows, cols] = total.astype(BF16)

        loop(n_seq, one)
        each_peer(n_seq, seq, lambda s: piece_send(part, s, True).start())
        grad_ref[seq, :, cols] = GS[pl.ds(pl.multiple_of(seq * p.rows, p.rows), p.rows), cols]

    def second_sum(k):
        sum_step(1, PARTA, k)
        share = D // LANES // n_z
        loop(share, lambda i: back_of_weights(k * share + i))

    loop(n_z, second_sum)
    sum_result(1, PARTA, BSTREAM)
    back_normed = BSTREAM[...]
    stream = STREAM[...]
    factor = factor_of(stream)
    n = stream * factor
    e = back_normed * gain_mlp
    BSTREAM[...] = cot_ref[...].astype(F32) + factor * (e - n * jnp.mean(e * n, -1, keepdims=True))
    BM = BSTREAM[...].astype(BF16)
    BAT[...] = product(BM, WO[...].reshape(D, p.joined)).astype(BF16)
    each_peer(n_seq, seq, lambda s: back_copy(s, True).start())
    BATT[seq] = BAT[:, lanes_of(seq)]
    GO[...] = product_tn(BM, AO[...]).astype(BF16).reshape(GO.shape)

    start_bands(1)
    if p.inline:
        slab_sum_half().start()
    else:
        done = pltpu.make_async_copy(GO.at[0, 0, 0], go_ref, local_sem.at[0])
        done.start()
        done.wait()

    def back_heads(j):
        back = BATT[j].astype(F32)
        den = DEN[j]
        BNUM[j] = (back / den).astype(BF16)
        prod = back * ATTF[j]
        out = jnp.zeros((B, p.vp), F32)
        for h in range(p.heads):
            total = jnp.sum(prod * value_masks[h].astype(F32), -1, keepdims=True)
            out = jnp.where(value_masks[h] > 0, -total, out)
        ATTF[j] = out / den
        DKF[j] = jnp.zeros((B, p.qk), F32)
        DVF[j] = jnp.zeros((B, p.vp), F32)

    loop(n_z, lambda k: sum_step(2, PARTB, k))
    each_peer(n_seq, seq, lambda s: back_copy(s, False).wait_recv())
    loop(n_seq, back_heads)

    def attend_back(i):
        queries, numer, denom = chip_rows(Q, i), chip_rows(BNUM, i), chip_rows(ATTF, i)
        high = denom.astype(BF16)
        low = (denom - high.astype(F32)).astype(BF16)

        def inner(j, dq, diagonal):
            keys, values = chip_rows(K, j), chip_rows(V, j)
            dk, dv = chip_rows(DKF, j), chip_rows(DVF, j)
            one = (vlane < 2).astype(BF16)
            wide_values = jnp.concatenate([values, jnp.broadcast_to(one, (C, p.vp))], -1)
            for h in range(p.heads):
                qh, bh = query_of(queries, h), numer * value_masks[h]
                first = h * HEAD_V
                extra = jnp.where(
                    vlane == 0, high[:, first : first + 1].astype(F32),
                    jnp.where(vlane == 1, low[:, first : first + 1].astype(F32), 0.0),
                ).astype(BF16)
                u = product_nt(qh, keys)
                ds = product_nt(jnp.concatenate([bh, extra], -1), wide_values)
                s, dt = 0.5 * u * u + 0.5, ds * u
                if diagonal:
                    s, dt = jnp.where(below_diag, s, 0.0), jnp.where(below_diag, dt, 0.0)
                dt = dt.astype(BF16)
                dq = dq + product(dt, keys * feat_masks[h])
                dk = dk + product_tn(dt, queries * feat_masks[h])
                dv = dv + product_tn(s.astype(BF16), bh)
            store_rows(DKF, j, dk)
            store_rows(DVF, j, dv)
            return dq

        dq = lax.fori_loop(0, i, lambda j, dq: inner(j, dq, False), jnp.zeros((C, p.qk), F32))
        dq = inner(i, dq, True)
        store_rows(DQK, i, dq * scale)

    loop(n_z // 2, attend_back)
    if p.inline:
        slab_sum_half().wait_recv()
        GO[:, :, core] = (GO[:, :, core].astype(F32) + SO[...].astype(F32)).astype(BF16)
        each_peer(n_dp, dp, lambda d: slab_sum_band(d, True).start())
    loop(n_z - 1 - n_z // 2, lambda k: attend_back(k + n_z // 2))
    start_pieces(1)
    loop(1, lambda k: attend_back(k + n_z - 1))
    sum_drain(1, PARTA)

    def back_input(j):
        dk = DKF[j].astype(BF16)
        qk = (DQK[j].astype(F32) + product_nt(dk, shift)).astype(BF16)
        DQK[j] = qk
        DV[j] = DVF[j].astype(BF16)
        PARTA[j] = (
            product_nt(qk, W[:, : p.qk]) + product_nt(DV[j], W[:, p.at_v : p.at_gate])
        ).astype(BF16)

    def fourth_sum(k):
        loop(2, lambda side: back_input(2 * far(k) + side))
        sibling_copy(3, PARTA, far(k)).start()

    loop(n_z, fourth_sum)
    loop(1, lambda k: sum_step(3, PARTA, k))

    def attention_weights(i):
        d0 = pl.multiple_of(i * LANES, LANES)
        rows = pl.ds(d0, LANES)
        normed = all_rows(NA, d0, LANES)
        tile_qk = product_tn(normed, DQK[...].reshape(n_seq * B, p.qk))
        tile_v = product_tn(normed, DV[...].reshape(n_seq * B, p.vp))
        G[rows, p.at_v : p.at_gate] = tile_v.astype(BF16)
        own_qk = W[rows, : p.qk].astype(F32)
        gain_grad = (
            jnp.sum(jnp.where(lane < at_gain, tile_qk * own_qk, 0.0), -1, keepdims=True)
            + jnp.sum(tile_v * W[rows, p.at_v : p.at_gate].astype(F32), -1, keepdims=True)
        ) / own_qk[:, at_gain : at_gain + 1]
        rest = jnp.where(lane == at_gain, gain_grad, G[rows, : p.qk].astype(F32))
        G[rows, : p.qk] = jnp.where(lane < at_gain, tile_qk, rest).astype(BF16)

    half = D // LANES // 2
    loop(half, attention_weights)
    loop(1, lambda k: sum_step(3, PARTA, k + 1))
    loop(half, lambda i: attention_weights(i + half))
    start_bands(0)
    if p.inline:
        each_peer(n_dp, dp, lambda d: slab_sum_band(d, False).wait_recv())
        band_total = GO[dp, :, core].astype(F32)
        for step in range(1, n_dp):
            band_total = band_total + DO[lax.rem(dp + step, n_dp)].astype(F32)
        ZS[...] = band_total.astype(BF16)
        each_peer(n_z, z, lambda zk: slab_sum(zk, True).start())
    loop(n_z - 2, lambda k: sum_step(3, PARTA, k + 2))
    start_pieces(0)

    sum_result(2, PARTB, gtok_ref)
    out_ref[...] = (STREAM[...] + gtok_ref[...]).astype(BF16)
    sum_result(3, PARTA, gtok_ref)
    x = tok_ref[...].astype(F32)
    factor = factor_of(x)
    m = x * factor
    f = gtok_ref[...] * gain_attn
    gtok_ref[...] = BSTREAM[...] + factor * (f - m * jnp.mean(f * m, -1, keepdims=True))

    if p.inline:
        each_peer(n_z, z, lambda zk: slab_sum(zk, False).wait_recv())
        slab_total = ZS[z].astype(F32)
        for step in range(1, n_z):
            slab_total = slab_total + ZO[lax.rem(z + step, n_z)].astype(F32)
        go_ref[...] = slab_total
        for part in (1, 0):
            each_peer(n_seq, seq, lambda s: piece_send(part, s, False).wait_recv())
    else:
        done = pltpu.make_async_copy(G, grad_ref, local_sem.at[0])
        done.start()
        done.wait()

    gather_drain(0, TOK)
    gather_drain(1, COT)
    gather_drain(2, NM)
    sum_drain(2, PARTB)
    sum_drain(3, PARTA)
    each_peer(n_seq, seq, lambda s: attended_copy(s, True).wait_send())
    each_peer(n_seq, seq, lambda s: back_copy(s, True).wait_send())
    if p.inline:
        each_peer(n_z, z, lambda zk: slab_copy(zk, True).wait_send())
        each_peer(n_dp, dp, lambda d: slab_band(d, True).wait_send())
        slab_half(core).wait_send()
        slab_sum_half().wait_send()
        each_peer(n_dp, dp, lambda d: slab_sum_band(d, True).wait_send())
        each_peer(n_z, z, lambda zk: slab_sum(zk, True).wait_send())
        for part in (0, 1):
            each_peer(n_seq, seq, lambda s: piece_copy(part, s, True).wait_send())
            each_peer(n_dp, dp, lambda d: band_copy(part, d, True).wait_send())
            each_peer(n_dp, dp, lambda d: band_send(part, d, True).wait_send())
            each_peer(n_seq, seq, lambda s: piece_send(part, s, True).wait_send())


def run_layer(plan, tokens, cotangent, weights, output_rows):
    p = plan
    n_seq, n_z, n_dp, B, D = p.n_seq, p.n_z, p.n_dp, p.block, p.width
    vmem = pl.BlockSpec(memory_space=pltpu.VMEM)
    grads = (n_seq, p.rows, p.cols) if p.inline else (D, p.cols)
    dma = pltpu.SemaphoreType.DMA

    def rows(width, kind=BF16):
        return pltpu.VMEM((n_seq, B, width), kind)

    band = p.band if p.inline else 16
    n_gr = n_dp if p.inline else 1
    anywhere = pl.BlockSpec(memory_space=pl.ANY)
    whole = (n_dp, n_z, 2, p.rows, p.joined) if p.inline else (1, 1, 1, D, p.joined)
    slabs = (n_z, p.rows, p.joined) if p.inline else (1, 16, LANES)
    bands = (n_dp,) + slabs if p.inline else (1, 1, 16, LANES)
    return pl.pallas_call(
        functools.partial(layer_kernel, plan),
        out_shape=(
            jax.ShapeDtypeStruct((B, D), BF16),
            jax.ShapeDtypeStruct((B, D), F32),
            jax.ShapeDtypeStruct(grads, BF16),
            jax.ShapeDtypeStruct((p.rows, p.joined), F32) if p.inline else jax.ShapeDtypeStruct((D, p.joined), BF16),
        ),
        in_specs=[vmem, vmem] + [vmem if p.inline else anywhere] * 2,
        out_specs=(vmem, vmem) + (vmem if p.inline else anywhere,) * 2,
        scratch_shapes=[
            rows(D), rows(D), rows(D), rows(D),
            pltpu.VMEM(whole, BF16), pltpu.VMEM(whole if p.inline else (1, 1, 1, 16, LANES), BF16), pltpu.VMEM(bands, BF16), pltpu.VMEM(bands, BF16),
            pltpu.VMEM(slabs, BF16), pltpu.VMEM(slabs, BF16),
            pltpu.VMEM((B, p.joined), BF16), pltpu.VMEM((B, p.joined), BF16), rows(p.vp),
            pltpu.VMEM((D, p.cols), BF16), pltpu.VMEM((D, p.cols), BF16),
            pltpu.VMEM((n_gr, band, p.cols), BF16), pltpu.VMEM((band, p.cols), BF16),
            rows(p.qk), rows(p.qk), rows(p.vp), rows(p.vp), rows(p.vp, F32), rows(p.vp, F32),
            rows(p.vp), rows(p.qk), rows(p.vp), rows(p.qk, F32), rows(p.vp, F32),
            rows(p.fp), rows(p.fp), rows(p.fp),
            rows(D), rows(D),
            pltpu.VMEM((3, n_z, B, D), BF16), pltpu.VMEM((3, n_z + 1, B, D), BF16),
            pltpu.VMEM((B, D), F32), pltpu.VMEM((B, D), F32),
            dma((4, 3, n_seq)), dma((4, n_seq)), dma((4, n_z)), dma((4, n_z)),
            dma((4, n_z)), dma((4, n_z + 1)),
            dma((2, n_seq)), dma((2, n_seq)), dma((2, n_dp)), dma((2, n_dp)),
            dma((2, n_dp)), dma((2, n_dp)), dma((2, n_seq)), dma((2, n_seq)), dma((1,)),
            dma((n_z,)), dma((n_z,)), dma((n_dp,)), dma((n_dp,)), dma((2,)), dma((2,)),
            dma((n_z,)), dma((n_z,)), dma((n_dp,)), dma((n_dp,)),
            dma((n_seq,)), dma((n_seq,)), dma((n_seq,)), dma((n_seq,)),
        ],
        compiler_params=pltpu.CompilerParams(
            collective_id=0, has_side_effects=True, vmem_limit_bytes=66_000_000
        ),
    )(tokens, cotangent, weights, output_rows)


def on_device(tokens, w_query, w_key, w_value, w_output, w_gate, w_up, w_down, norm_attn, norm_mlp, cotangent):
    plan = Plan(
        lax.axis_size("dp"), lax.axis_size("seq"), tokens.shape[0], tokens.shape[1], w_gate.shape[1]
    )
    weights = pack_weights(
        plan, w_query, w_key, w_value, w_gate, w_up, w_down, norm_attn, norm_mlp
    )
    output_rows = pack_output(plan, w_output)
    if not plan.inline:
        weights = lax.all_to_all(weights, "seq", split_axis=0, concat_axis=0, tiled=True)
        weights = lax.all_gather(weights, "dp").reshape(plan.width, plan.cols)
        output_rows = lax.all_gather(output_rows, ("dp", "seq"), axis=0, tiled=True)
    layer_out, grad_tokens, grads, grad_output = run_layer(plan, tokens, cotangent, weights, output_rows)
    if not plan.inline:
        grads = lax.psum_scatter(grads, "dp", scatter_dimension=0, tiled=True)
        grads = grads.reshape(plan.n_seq, plan.rows, plan.cols)
        grads = lax.all_to_all(grads, "seq", split_axis=0, concat_axis=0, tiled=True)
        grad_output = lax.psum_scatter(grad_output, ("dp", "seq"), scatter_dimension=0, tiled=True).astype(F32)
    return (layer_out, grad_tokens) + unpack_grads(plan, grads, grad_output)


def solution(mesh):
    rows, cols, vec = P(("dp", "seq"), None), P(None, ("dp", "seq")), P(("dp", "seq"))
    return jax.shard_map(
        on_device,
        mesh=mesh,
        in_specs=(rows, rows, rows, rows, cols, rows, rows, cols, vec, vec, rows),
        out_specs=(rows, rows, rows, rows, rows, cols, rows, rows, cols, vec, vec),
        check_vma=False,
    )
```

```python
import functools

import jax
import jax.numpy as jnp
from jax import lax
from jax.experimental import pallas as pl
from jax.experimental.pallas import tpu as pltpu
from jax.sharding import PartitionSpec as P

HEADS = 16
FEAT_DIM = 16
HEAD_V = 64
EPSILON = 1e-06
LANES = 128
GROUP = 8
MESH = pl.DeviceIdType.MESH
BF16 = jnp.bfloat16
F32 = jnp.float32


def round_up(size, unit):
    return -(-size // unit) * unit


def product(a, b):
    return jnp.dot(a, b, preferred_element_type=F32)


def product_nt(a, b):
    return lax.dot_general(a, b, (((1,), (1,)), ((), ())), preferred_element_type=F32)


def product_tn(a, b):
    return lax.dot_general(a, b, (((0,), (0,)), ((), ())), preferred_element_type=F32)


class Plan:
    def __init__(self, n_dp, n_seq, block, width, hidden):
        self.n_dp, self.n_seq, self.n_z = n_dp, n_seq, n_seq // 2
        self.block, self.width = block, width
        self.heads = HEADS // n_seq
        self.feat = self.heads * FEAT_DIM
        self.value = self.heads * HEAD_V
        self.unit = hidden // GROUP
        self.qk = round_up(2 * self.feat + 2, LANES)
        self.vp = round_up(self.value, LANES)
        self.fp = round_up(self.unit + 1, LANES)
        self.rows = width // (n_dp * n_seq)
        self.band = width // n_dp
        self.cols = self.qk + self.vp
        self.wide = 3 * self.fp
        self.joined = n_seq * self.vp
        self.n_y, self.n_zz = n_dp // 2, self.n_z // 2
        self.inline = 4 * self.rows == LANES


def cut(w, parts):
    return w.reshape(w.shape[0], parts, -1).transpose(1, 0, 2)


def pad(parts, to):
    joined = jnp.concatenate(parts, -1) if len(parts) > 1 else parts[0]
    return jnp.pad(joined, ((0, 0), (0, 0), (0, to - joined.shape[-1])))


def pack_attention(plan, w_query, w_key, w_value, norm_attn, norm_mlp):
    s = plan.n_seq
    gains = jnp.broadcast_to(jnp.stack([norm_attn, norm_mlp], -1), (s, plan.rows, 2))
    return jnp.concatenate(
        [pad([cut(w_query, s), cut(w_key, s), gains], plan.qk), pad([cut(w_value, s)], plan.vp)], -1
    )


def pack_feed(plan, w_gate, w_up, w_down):
    return jnp.concatenate([pad([cut(w, GROUP)], plan.fp) for w in (w_gate, w_up, w_down.T)], -1)


def pack_output(plan, w_output):
    heads = w_output.T.reshape(plan.rows, plan.n_seq, plan.value)
    return jnp.pad(heads, ((0, 0), (0, 0), (0, plan.vp - plan.value))).reshape(plan.rows, plan.joined)


def unpack_grads(plan, owned, owned_feed, owned_output):
    r = plan.rows

    def join(pieces, start, unit):
        return pieces[:, :, start : start + unit].transpose(1, 0, 2).reshape(r, -1).astype(F32)

    at_gain = 2 * plan.feat
    return (
        join(owned, 0, plan.feat),
        join(owned, plan.feat, plan.feat),
        join(owned, plan.qk, plan.value),
        owned_output.reshape(r, plan.n_seq, plan.vp)[:, :, : plan.value].reshape(r, -1).T,
        join(owned_feed, 0, plan.unit),
        join(owned_feed, plan.fp, plan.unit),
        join(owned_feed, 2 * plan.fp, plan.unit).T,
        jnp.sum(owned[:, :, at_gain].astype(F32), 0),
        jnp.sum(owned_feed[:, :, plan.fp + plan.unit].astype(F32), 0),
    )


def layer_kernel(plan, *refs):
    p = plan
    (
        tok_ref, cot_ref, w_ref, wm_ref, wo_ref,
        out_ref, gtok_ref, grad_ref, gm_ref, go_ref,
        TOK, NA, COT, NM, WO, GO, SO, DO, ZS, ZO, AO, BAT, BATT,
        W, WM, G, GM, GY, GZ, GR, GS,
        Q, K, V, ATT, ATTF, DEN, BNUM, DQK, DV, DKF, DVF,
        H, BG, BU,
        PART, PARTA, PARTB, SIB, CH, HALF, XR, ZR, STREAM, BSTREAM,
        ag_send, ag_recv, sib_send, sib_recv, ch_send, ch_recv,
        w_send, w_recv, wd_send, wd_recv,
        g_send, g_recv, gz_send, gz_recv, local_sem,
        wo_send, wo_recv, wod_send, wod_recv, sl_send, sl_recv,
        go_send, go_recv, gd_send, gd_recv, at_send, at_recv, bt_send, bt_recv,
        sh_send, sh_recv, ha_send, ha_recv, xr_send, xr_recv, zr_send, zr_recv,
        wp_send, wp_recv, wz_send, wz_recv, wy_send, wy_recv,
        gp_send, gp_recv, gw_send, gw_recv, gy_send, gy_recv,
    ) = refs
    if not p.inline:
        GO = WO
    dp, seq = lax.axis_index("dp"), lax.axis_index("seq")
    n_seq, n_z, n_dp, B, D = p.n_seq, p.n_z, p.n_dp, p.block, p.width
    z, core = seq // 2, seq % 2
    sibling = (dp, seq + 1 - 2 * core)
    above, below = (dp, seq + 2), (dp, seq - 2)
    is_top, is_bottom = z == n_z - 1, z == 0
    n_y, n_zz = p.n_y, p.n_zz
    x, y, zl, zz = dp % 2, dp // 2, z % 2, z // 2
    rank = 4 * x + 2 * zl + core

    def at(r):
        return (2 * y + r // 4, 4 * zz + r % 4)

    x_peer, z_peer = (dp + 1 - 2 * x, seq), (dp, seq + 2 - 4 * zl)

    def remote(src, dst, send, recv, device):
        return pltpu.make_async_remote_copy(
            src_ref=src, dst_ref=dst, send_sem=send, recv_sem=recv,
            device_id=device, device_id_type=MESH,
        )

    def each_peer(count, mine, body):
        def one(i, carry):
            @pl.when(i != mine)
            def _():
                body(i)

            return carry

        lax.fori_loop(0, count, one, 0)

    def loop(count, body):
        def one(i, carry):
            body(i)
            return carry

        lax.fori_loop(0, count, one, 0)

    barrier = pltpu.get_barrier_semaphore()
    each_peer(n_seq, seq, lambda i: pl.semaphore_signal(barrier, inc=1, device_id=(dp, i), device_id_type=MESH))
    each_peer(n_dp, dp, lambda i: pl.semaphore_signal(barrier, inc=1, device_id=(i, seq), device_id_type=MESH))
    for other in (4 - 4 * x + 2 * zl + 1 - core, 4 - 4 * x + 2 - 2 * zl + core, 4 - 4 * x + 2 - 2 * zl + 1 - core):
        pl.semaphore_signal(barrier, inc=1, device_id=at(other), device_id_type=MESH)
    pl.semaphore_wait(barrier, n_seq - 1 + n_dp - 1 + 3)

    near = jnp.minimum(z, n_z - 1 - z)
    far_side = jnp.where(z < n_z - 1 - z, 1, -1)

    def order(k):
        step = (k + 1) // 2
        alternate = jnp.where(k % 2 == 1, -step, step)
        return z + jnp.where(k <= 2 * near, alternate, far_side * (k - near))

    def piece_rows(d, s):
        return pl.ds(pl.multiple_of((d * n_seq + s) * p.rows, p.rows), p.rows)

    def band_rows(d):
        return pl.ds(pl.multiple_of(d * p.band, p.band), p.band)

    def piece_copy(s, mine):
        src_of = seq if mine else s
        return remote(w_ref.at[s], W.at[piece_rows(dp, src_of)], w_send.at[s], w_recv.at[src_of], (dp, s))

    def band_copy(d, mine):
        src_of = dp if mine else d
        return remote(
            W.at[band_rows(src_of)], W.at[band_rows(src_of)], wd_send.at[d], wd_recv.at[src_of], (d, seq)
        )

    def third(q):
        return pl.ds(q * p.fp, p.fp)

    def feed_piece(q, r, mine):
        src_of = rank if mine else r
        rows = pl.ds(pl.multiple_of((src_of % 4) * p.rows, p.rows), p.rows)
        return remote(
            wm_ref.at[r, :, third(q)], WM.at[y, src_of // 4, zz, rows, third(q)],
            wp_send.at[q, r], wp_recv.at[q, src_of], at(r),
        )

    def feed_along_z(q, g, mine):
        src_of = zz if mine else g
        section = WM.at[y, :, src_of, :, third(q)]
        return remote(section, section, wz_send.at[q, g], wz_recv.at[q, src_of], (dp, 4 * g + 2 * zl + core))

    def feed_along_y(q, h, g, mine):
        src_of = y if mine else h
        section = WM.at[src_of, :, g, :, third(q)]
        return remote(section, section, wy_send.at[q, h, g], wy_recv.at[q, src_of, g], (2 * h + x, seq))

    def feed_own_section(q):
        if p.inline:
            each_peer(GROUP, rank, lambda r: feed_piece(q, r, False).wait_recv())
            each_peer(n_zz, zz, lambda g: feed_along_z(q, g, True).start())
            each_peer(n_y, y, lambda h: feed_along_y(q, h, zz, True).start())

    def feed_pass_on(q):
        def one(g):
            feed_along_z(q, g, False).wait_recv()
            each_peer(n_y, y, lambda h: feed_along_y(q, h, g, True).start())

        if p.inline:
            each_peer(n_zz, zz, one)

    def feed_arrived(q):
        if p.inline:
            each_peer(n_y, y, lambda h: loop(n_zz, lambda g: feed_along_y(q, h, g, False).wait_recv()))

    def grad_along_y(q, h, g, mine):
        src_of = y if mine else h
        return remote(
            GM.at[h, :, g, :, third(q)], GY.at[src_of, g, :, :, third(q)],
            gy_send.at[q, h, g], gy_recv.at[q, src_of, g], (2 * h + x, seq),
        )

    def grad_along_z(q, g, mine):
        src_of = zz if mine else g
        return remote(
            GM.at[y, :, g, :, third(q)], GZ.at[src_of, :, :, third(q)],
            gw_send.at[q, g], gw_recv.at[q, src_of], (dp, 4 * g + 2 * zl + core),
        )

    def grad_piece(q, r, mine):
        src_of = rank if mine else r
        rows = pl.ds(pl.multiple_of((r % 4) * p.rows, p.rows), p.rows)
        return remote(
            GM.at[y, r // 4, zz, rows, third(q)], gm_ref.at[src_of, :, third(q)],
            gp_send.at[q, r], gp_recv.at[q, src_of], at(r),
        )

    def grad_to_y(q):
        if p.inline:
            for step in range(n_zz):
                g = lax.rem(zz + 1 + step, n_zz)
                each_peer(n_y, y, lambda h: grad_along_y(q, h, g, True).start())

    def grad_to_z(q):
        if not p.inline:
            return
        for step in range(n_zz):
            g = lax.rem(zz + 1 + step, n_zz)
            total = GM[y, :, g, :, third(q)].astype(F32)
            for other in range(1, n_y):
                h = lax.rem(y + other, n_y)
                grad_along_y(q, h, g, False).wait_recv()
                total = total + GY[h, g, :, :, third(q)].astype(F32)
            GM[y, :, g, :, third(q)] = total.astype(BF16)
            if step < n_zz - 1:
                grad_along_z(q, g, True).start()

    def grad_to_group(q):
        if not p.inline:
            return
        total = GM[y, :, zz, :, third(q)].astype(F32)
        for step in range(1, n_zz):
            g = lax.rem(zz + step, n_zz)
            grad_along_z(q, g, False).wait_recv()
            total = total + GZ[g, :, :, third(q)].astype(F32)
        GM[y, :, zz, :, third(q)] = total.astype(BF16)
        each_peer(GROUP, rank, lambda r: grad_piece(q, r, True).start())
        rows = pl.ds(pl.multiple_of((rank % 4) * p.rows, p.rows), p.rows)
        gm_ref[rank, :, third(q)] = GM[y, x, zz, rows, third(q)]

    def spot(w):
        return 4 * jnp.where(w >= 2, 1 - x, x) + 2 * jnp.where(w % 2 == 1, 1 - zl, zl)

    def share_copy(a, buf, b, way, device):
        return remote(buf.at[b], buf.at[b], sh_send.at[a, way, b], sh_recv.at[a, b], device)

    def share_step(a, buf, w, on_block):
        def one(side):
            take = jnp.where(side == 0, w < 4, w >= 1)

            @pl.when(take)
            def _():
                b = spot(w - side) + jnp.where(side == 0, core, 1 - core)

                @pl.when(b != rank)
                def _():
                    share_copy(a, buf, b, 2, sibling).wait_recv()

                @pl.when(side == 0)
                def _():
                    @pl.when(w == 0)
                    def _():
                        share_copy(a, buf, b, 0, z_peer).start()

                    @pl.when(w <= 1)
                    def _():
                        share_copy(a, buf, b, 1, x_peer).start()

                    share_copy(a, buf, b, 2, sibling).start()

                if on_block is not None:
                    on_block(b)

        loop(2, one)

    def share_drain(a, buf):
        def one(w):
            b = spot(w) + core

            @pl.when(w == 0)
            def _():
                share_copy(a, buf, b, 0, z_peer).wait_send()

            @pl.when(w <= 1)
            def _():
                share_copy(a, buf, b, 1, x_peer).wait_send()

            share_copy(a, buf, b, 2, sibling).wait_send()

        loop(4, one)

    def half_copy(i, part, w):
        return remote(part.at[spot(w) + 1 - core], HALF.at[i, w], ha_send.at[i, w], ha_recv.at[i, w], sibling)

    def x_copy(i, part, w):
        return remote(part.at[spot(w) + core], XR.at[i, w - 2], xr_send.at[i, w - 2], xr_recv.at[i, w - 2], x_peer)

    def z_copy(i, part):
        return remote(part.at[spot(1) + core], ZR.at[i], zr_send.at[i], zr_recv.at[i], z_peer)

    def group_sum_step(i, part, w):
        b = spot(w) + core
        half_copy(i, part, w).wait_recv()
        total = part[b].astype(F32) + HALF[i, w].astype(F32)
        if w == 1:
            x_copy(i, part, 3).wait_recv()
            total = total + XR[i, 1].astype(F32)
        part[b] = total.astype(BF16)
        (z_copy(i, part) if w == 1 else x_copy(i, part, w)).start()

    def group_sum_result(i, part, total):
        half_copy(i, part, 0).wait_recv()
        x_copy(i, part, 2).wait_recv()
        z_copy(i, part).wait_recv()
        total[...] = (
            part[rank].astype(F32) + HALF[i, 0].astype(F32) + XR[i, 0].astype(F32) + ZR[i].astype(F32)
        )

    def group_sum_drain(i, part):
        loop(4, lambda w: half_copy(i, part, w).wait_send())
        x_copy(i, part, 2).wait_send()
        x_copy(i, part, 3).wait_send()
        z_copy(i, part).wait_send()

    def gather_copy(buf, j, way, device):
        return remote(buf.at[j], buf.at[j], ag_send.at[way, j], ag_recv.at[j], device)

    def gather_step(buf, k, on_block):
        def one(side):
            take = jnp.where(side == 0, k < n_z, k >= 1)

            @pl.when(take)
            def _():
                zk = order(k - side)
                j = 2 * zk + jnp.where(side == 0, core, 1 - core)

                @pl.when(j != seq)
                def _():
                    gather_copy(buf, j, 0, sibling).wait_recv()

                @pl.when(side == 0)
                def _():
                    @pl.when(jnp.logical_and(zk <= z, jnp.logical_not(is_top)))
                    def _():
                        gather_copy(buf, j, 0, above).start()

                    @pl.when(jnp.logical_and(zk >= z, jnp.logical_not(is_bottom)))
                    def _():
                        gather_copy(buf, j, 1, below).start()

                    gather_copy(buf, j, 2, sibling).start()

                if on_block is not None:
                    on_block(j)

        loop(2, one)

    def gather_drain(buf):
        def one(zk):
            j = 2 * zk + core

            @pl.when(jnp.logical_and(zk <= z, jnp.logical_not(is_top)))
            def _():
                gather_copy(buf, j, 0, above).wait_send()

            @pl.when(jnp.logical_and(zk >= z, jnp.logical_not(is_bottom)))
            def _():
                gather_copy(buf, j, 1, below).wait_send()

            gather_copy(buf, j, 2, sibling).wait_send()

        loop(n_z, one)

    def sibling_copy(part, zk):
        return remote(
            part.at[2 * zk + 1 - core], SIB.at[zk], sib_send.at[zk], sib_recv.at[zk], sibling
        )

    def chain_copy(part, zk, up):
        slot = zk if up else jnp.where(zk == z - 1, n_z, zk)
        return remote(
            part.at[2 * zk + core], CH.at[slot], ch_send.at[zk], ch_recv.at[slot],
            above if up else below,
        )

    def chain_wait(part, slot):
        remote(part.at[0], CH.at[slot], ch_send.at[0], ch_recv.at[slot], sibling).wait_recv()

    def far(k):
        return order(n_z - 1 - k)

    def sum_step(part, k):
        zk = far(k)
        j = 2 * zk + core
        remote(part.at[0], SIB.at[zk], sib_send.at[zk], sib_recv.at[zk], sibling).wait_recv()

        @pl.when(zk != z)
        def _():
            first = jnp.where(zk > z, is_bottom, is_top)

            @pl.when(first)
            def _():
                part[j] = (part[j].astype(F32) + SIB[zk].astype(F32)).astype(BF16)

            @pl.when(jnp.logical_not(first))
            def _():
                chain_wait(part, zk)
                part[j] = (
                    part[j].astype(F32) + SIB[zk].astype(F32) + CH[zk].astype(F32)
                ).astype(BF16)

            @pl.when(zk > z)
            def _():
                chain_copy(part, zk, True).start()

            @pl.when(zk < z)
            def _():
                chain_copy(part, zk, False).start()

    def sum_result(part, total):
        total[...] = part[seq].astype(F32) + SIB[z].astype(F32)

        @pl.when(jnp.logical_not(is_bottom))
        def _():
            chain_wait(part, z)
            total[...] += CH[z].astype(F32)

        @pl.when(jnp.logical_not(is_top))
        def _():
            chain_wait(part, n_z)
            total[...] += CH[n_z].astype(F32)

    def sum_drain(part):
        def one(zk):
            sibling_copy(part, zk).wait_send()

            @pl.when(zk > z)
            def _():
                chain_copy(part, zk, True).wait_send()

            @pl.when(zk < z)
            def _():
                chain_copy(part, zk, False).wait_send()

        loop(n_z, one)

    def slab_copy(zk, mine):
        src_of = z if mine else zk
        return remote(
            wo_ref, WO.at[dp, src_of, core], wo_send.at[zk], wo_recv.at[src_of], (dp, 2 * zk + core)
        )

    def slab_band(d, mine):
        src_of = dp if mine else d
        return remote(
            WO.at[src_of, :, core], WO.at[src_of, :, core], wod_send.at[d], wod_recv.at[src_of], (d, seq)
        )

    def slab_half(which):
        return remote(WO.at[:, :, which], WO.at[:, :, which], sl_send.at[0], sl_recv.at[0], sibling)

    def slab_sum_half():
        return remote(GO.at[:, :, 1 - core], SO, sl_send.at[1], sl_recv.at[1], sibling)

    def slab_sum_band(d, mine):
        src_of = dp if mine else d
        return remote(GO.at[d, :, core], DO.at[src_of], gd_send.at[d], gd_recv.at[src_of], (d, seq))

    def slab_sum(zk, mine):
        src_of = z if mine else zk
        return remote(ZS.at[zk], ZO.at[src_of], go_send.at[zk], go_recv.at[src_of], (dp, 2 * zk + core))

    def lanes_of(s):
        return pl.ds(pl.multiple_of(s * p.vp, p.vp), p.vp)

    def attended_copy(s, mine):
        src_of = seq if mine else s
        return remote(ATT.at[s], AO.at[:, lanes_of(src_of)], at_send.at[s], at_recv.at[src_of], (dp, s))

    def back_copy(s, mine):
        src_of = seq if mine else s
        return remote(BAT.at[:, lanes_of(s)], BATT.at[src_of], bt_send.at[s], bt_recv.at[src_of], (dp, s))

    def stay(src, dst):
        own = pltpu.make_async_copy(src, dst, local_sem.at[0])
        own.start()
        own.wait()

    if p.inline:
        each_peer(n_seq, seq, lambda s: piece_copy(s, True).start())
        TOK[seq] = tok_ref[...]
        gather_step(TOK, 0, None)
        for q in range(3):
            each_peer(GROUP, rank, lambda r: feed_piece(q, r, True).start())
        stay(w_ref.at[seq], W.at[piece_rows(dp, seq)])
        own_rows = pl.ds(pl.multiple_of((rank % 4) * p.rows, p.rows), p.rows)
        stay(wm_ref.at[rank], WM.at[y, x, zz, own_rows])
        stay(wo_ref, WO.at[dp, z, core])
        COT[rank] = cot_ref[...]
        each_peer(n_seq, seq, lambda s: piece_copy(s, False).wait_recv())
        each_peer(n_dp, dp, lambda d: band_copy(d, True).start())
    else:
        TOK[seq] = tok_ref[...]
        gather_step(TOK, 0, None)
        stay(w_ref, W)
        stay(wm_ref, WM.at[0, 0, 0])
        stay(wo_ref, WO.at[0, 0, 0])
        COT[rank] = cot_ref[...]
    gather_step(TOK, 1, None)
    if p.inline:
        each_peer(n_z, z, lambda zk: slab_copy(zk, True).start())
    for q in range(3):
        feed_own_section(q)
    loop(n_z - 3, lambda k: gather_step(TOK, k + 2, None))
    if p.inline:
        each_peer(n_dp, dp, lambda d: band_copy(d, False).wait_recv())

    lane = lax.broadcasted_iota(jnp.int32, (1, p.qk), 1)
    vlane = lax.broadcasted_iota(jnp.int32, (1, p.vp), 1)
    feat_masks = [
        jnp.logical_and(lane >= h * FEAT_DIM, lane < (h + 1) * FEAT_DIM).astype(BF16) for h in range(p.heads)
    ]
    value_masks = [
        jnp.logical_and(vlane >= h * HEAD_V, vlane < (h + 1) * HEAD_V).astype(BF16) for h in range(p.heads)
    ]
    spare = (vlane >= p.value).astype(F32)
    row = lax.broadcasted_iota(jnp.int32, (p.qk, p.qk), 0)
    col = lax.broadcasted_iota(jnp.int32, (p.qk, p.qk), 1)
    shift = jnp.logical_and(row == col + p.feat, col < p.feat).astype(F32).astype(BF16)
    at_gain = 2 * p.feat
    pick = lax.broadcasted_iota(jnp.int32, (16, p.qk), 0) + at_gain == lax.broadcasted_iota(
        jnp.int32, (16, p.qk), 1
    )
    gain_rows = product_nt(pick.astype(F32).astype(BF16), W[:, : p.qk])
    gain_attn, gain_mlp = gain_rows[0:1], gain_rows[1:2]
    scale = FEAT_DIM ** -0.5
    one_lane = (lane == p.qk - 1).astype(F32)
    C = 2 * B
    below_diag = lax.broadcasted_iota(jnp.int32, (C, C), 0) >= lax.broadcasted_iota(jnp.int32, (C, C), 1)

    def factor_of(x):
        return lax.rsqrt(jnp.mean(x * x, -1, keepdims=True) + EPSILON)

    def project(j):
        x = TOK[j].astype(F32)
        normed = (x * factor_of(x) * gain_attn).astype(BF16)
        NA[j] = normed
        qk = product(normed, W[:, : p.qk]).astype(BF16)
        Q[j] = (qk.astype(F32) * scale).astype(BF16)
        K[j] = (product(qk, shift) + one_lane).astype(BF16)
        V[j] = product(normed, W[:, p.qk : p.cols]).astype(BF16)

    loop(n_z - 1, lambda k: project(2 * order(k) + core))
    loop(n_z - 2, lambda k: project(2 * order(k) + 1 - core))
    loop(1, lambda k: gather_step(TOK, k + n_z - 1, project))
    if p.inline:
        each_peer(n_z, z, lambda zk: slab_copy(zk, False).wait_recv())
        each_peer(n_dp, dp, lambda d: slab_band(d, True).start())
    share_step(1, COT, 0, None)
    loop(1, lambda k: gather_step(TOK, k + n_z, project))

    def chip_rows(buf, i):
        return buf[pl.ds(2 * i, 2)].reshape(C, buf.shape[-1])

    def store_rows(buf, i, value):
        buf[pl.ds(2 * i, 2)] = value.reshape(2, B, value.shape[-1]).astype(buf.dtype)

    def one_plus_t(query, key):
        return product_nt(query, key)

    def query_of(queries, h):
        return queries * feat_masks[h] + one_lane.astype(BF16)

    def attend(i):
        queries = chip_rows(Q, i)

        def inner(j, acc, diagonal):
            keys, values = chip_rows(K, j), chip_rows(V, j)
            for h in range(p.heads):
                u = product_nt(query_of(queries, h), keys)
                s = 0.5 * u * u + 0.5
                if diagonal:
                    s = jnp.where(below_diag, s, 0.0)
                ones = jnp.broadcast_to(value_masks[h], (C, p.vp))
                acc = acc + product(s.astype(BF16), jnp.concatenate([values * value_masks[h], ones], -1))
            return acc

        acc = lax.fori_loop(0, i, lambda j, acc: inner(j, acc, False), jnp.zeros((C, 2 * p.vp), F32))
        acc = inner(i, acc, True)
        den = acc[:, p.vp :] + spare
        att = acc[:, : p.vp] / den
        store_rows(DEN, i, den)
        store_rows(ATTF, i, att)
        store_rows(ATT, i, att)

        def give(side):
            @pl.when(2 * i + side != seq)
            def _():
                attended_copy(2 * i + side, True).start()

        loop(2, give)

    loop(n_z, lambda k: attend(far(k)))
    AO[:, lanes_of(seq)] = ATT[seq]
    share_step(1, COT, 1, None)
    feed_pass_on(0)
    feed_pass_on(1)
    if p.inline:
        each_peer(n_dp, dp, lambda d: slab_band(d, False).wait_recv())
        slab_half(core).start()
    each_peer(n_seq, seq, lambda s: attended_copy(s, False).wait_recv())
    if p.inline:
        slab_half(1 - core).wait_recv()
    STREAM[...] = tok_ref[...].astype(F32) + product_nt(AO[...], WO[...].reshape(D, p.joined))

    stream = STREAM[...]
    NM[rank] = (stream * factor_of(stream) * gain_mlp).astype(BF16)
    share_step(0, NM, 0, None)
    feed_pass_on(2)
    loop(3, lambda w: share_step(1, COT, w + 2, None))
    for q in range(3):
        feed_arrived(q)

    def weight(q):
        return WM[:, :, :, :, third(q)].reshape(D, p.fp)

    def feed(j):
        normed = NM[j]
        gate = product(normed, weight(0))
        up = product(normed, weight(1))
        back = product(COT[j], weight(2))
        sig = jax.nn.sigmoid(gate)
        act = gate * sig
        H[j] = (act * up).astype(BF16)
        BG[j] = (back * up * sig * (1.0 + gate * (1.0 - sig))).astype(BF16)
        BU[j] = (back * act).astype(BF16)
        PARTA[j] = (product_nt(BG[j], weight(0)) + product_nt(BU[j], weight(1))).astype(BF16)
        PARTB[j] = product_nt(H[j], weight(2)).astype(BF16)

        @pl.when(j % 2 != core)
        def _():
            w = 2 * jnp.where(j // 4 != x, 1, 0) + jnp.where((j // 2) % 2 != zl, 1, 0)
            half_copy(0, PARTA, w).start()
            half_copy(1, PARTB, w).start()

    feed(rank)
    loop(4, lambda w: share_step(0, NM, w + 1, feed))

    def all_rows(buf, d0, size):
        return buf[:, :, pl.ds(d0, size)].reshape(buf.shape[0] * B, size)

    def chunk_of(buf, i):
        if p.inline:
            return buf.at[i // (2 * n_zz), (i // n_zz) % 2, i % n_zz]
        return buf.at[0, 0, 0, pl.ds(pl.multiple_of(i * LANES, LANES), LANES)]

    feed_lane = lax.broadcasted_iota(jnp.int32, (1, p.fp), 1)

    def back_of_weights(q, left, right):
        def one(i):
            d0 = pl.multiple_of(i * LANES, LANES)
            tile = product_tn(all_rows(left, d0, LANES), right[...].reshape(GROUP * B, p.fp))
            grads, own = chunk_of(GM, i), chunk_of(WM, i)
            if q == 1:
                both = tile * own[:, third(1)].astype(F32) + grads[:, third(0)].astype(F32) * own[
                    :, third(0)
                ].astype(F32)
                gain = W[pl.ds(d0, LANES), : p.qk].astype(F32)[:, at_gain + 1 : at_gain + 2]
                tile = jnp.where(feed_lane == p.unit, jnp.sum(both, -1, keepdims=True) / gain, tile)
            grads[:, third(q)] = tile.astype(BF16)

        loop(D // LANES, one)
        grad_to_y(q)

    group_sum_step(0, PARTA, 3)
    group_sum_step(0, PARTA, 2)
    back_of_weights(2, COT, H)
    group_sum_step(0, PARTA, 1)
    back_of_weights(0, NM, BG)
    grad_to_z(2)
    back_of_weights(1, NM, BU)
    group_sum_result(0, PARTA, BSTREAM)
    back_normed = BSTREAM[...]
    stream = STREAM[...]
    factor = factor_of(stream)
    n = stream * factor
    e = back_normed * gain_mlp
    BSTREAM[...] = cot_ref[...].astype(F32) + factor * (e - n * jnp.mean(e * n, -1, keepdims=True))
    BM = BSTREAM[...].astype(BF16)
    BAT[...] = product(BM, WO[...].reshape(D, p.joined)).astype(BF16)
    each_peer(n_seq, seq, lambda s: back_copy(s, True).start())
    BATT[seq] = BAT[:, lanes_of(seq)]
    GO[...] = product_tn(BM, AO[...]).astype(BF16).reshape(GO.shape)

    if p.inline:
        slab_sum_half().start()
    else:
        stay(GO.at[0, 0, 0], go_ref)

    def band_send(d, mine):
        src_of = dp if mine else d
        return remote(G.at[band_rows(d)], GR.at[src_of], g_send.at[d], g_recv.at[src_of], (d, seq))

    def piece_send(s, mine):
        src_of = seq if mine else s
        rows = pl.ds(pl.multiple_of(s * p.rows, p.rows), p.rows)
        return remote(GS.at[rows], grad_ref.at[src_of], gz_send.at[s], gz_recv.at[src_of], (dp, s))

    def back_heads(j):
        back = BATT[j].astype(F32)
        den = DEN[j]
        BNUM[j] = (back / den).astype(BF16)
        prod = back * ATTF[j]
        out = jnp.zeros((B, p.vp), F32)
        for h in range(p.heads):
            total = jnp.sum(prod * value_masks[h].astype(F32), -1, keepdims=True)
            out = jnp.where(value_masks[h] > 0, -total, out)
        ATTF[j] = out / den
        DKF[j] = jnp.zeros((B, p.qk), F32)
        DVF[j] = jnp.zeros((B, p.vp), F32)

    group_sum_step(1, PARTB, 3)
    group_sum_step(1, PARTB, 2)
    grad_to_z(0)
    each_peer(n_seq, seq, lambda s: back_copy(s, False).wait_recv())
    loop(n_seq, back_heads)

    def attend_back(i):
        queries, numer, denom = chip_rows(Q, i), chip_rows(BNUM, i), chip_rows(ATTF, i)
        high = denom.astype(BF16)
        low = (denom - high.astype(F32)).astype(BF16)

        def inner(j, dq, diagonal):
            keys, values = chip_rows(K, j), chip_rows(V, j)
            dk, dv = chip_rows(DKF, j), chip_rows(DVF, j)
            one = (vlane < 2).astype(BF16)
            wide_values = jnp.concatenate([values, jnp.broadcast_to(one, (C, p.vp))], -1)
            for h in range(p.heads):
                qh, bh = query_of(queries, h), numer * value_masks[h]
                first = h * HEAD_V
                extra = jnp.where(
                    vlane == 0, high[:, first : first + 1].astype(F32),
                    jnp.where(vlane == 1, low[:, first : first + 1].astype(F32), 0.0),
                ).astype(BF16)
                u = product_nt(qh, keys)
                ds = product_nt(jnp.concatenate([bh, extra], -1), wide_values)
                s, dt = 0.5 * u * u + 0.5, ds * u
                if diagonal:
                    s, dt = jnp.where(below_diag, s, 0.0), jnp.where(below_diag, dt, 0.0)
                dt = dt.astype(BF16)
                dq = dq + product(dt, keys * feat_masks[h])
                dk = dk + product_tn(dt, queries * feat_masks[h])
                dv = dv + product_tn(s.astype(BF16), bh)
            store_rows(DKF, j, dk)
            store_rows(DVF, j, dv)
            return dq

        dq = lax.fori_loop(0, i, lambda j, dq: inner(j, dq, False), jnp.zeros((C, p.qk), F32))
        dq = inner(i, dq, True)
        store_rows(DQK, i, dq * scale)

    loop(n_z // 2, attend_back)
    if p.inline:
        slab_sum_half().wait_recv()
        GO[:, :, core] = (GO[:, :, core].astype(F32) + SO[...].astype(F32)).astype(BF16)
        each_peer(n_dp, dp, lambda d: slab_sum_band(d, True).start())
    group_sum_step(1, PARTB, 1)
    grad_to_z(1)
    loop(n_z - n_z // 2, lambda k: attend_back(k + n_z // 2))

    def back_input(j):
        dk = DKF[j].astype(BF16)
        qk = (DQK[j].astype(F32) + product_nt(dk, shift)).astype(BF16)
        DQK[j] = qk
        DV[j] = DVF[j].astype(BF16)
        PART[j] = (
            product_nt(qk, W[:, : p.qk]) + product_nt(DV[j], W[:, p.qk : p.cols])
        ).astype(BF16)

    def fourth_sum(k):
        loop(2, lambda side: back_input(2 * far(k) + side))
        sibling_copy(PART, far(k)).start()

    loop(n_z, fourth_sum)
    loop(1, lambda k: sum_step(PART, k))
    grad_to_group(2)

    def attention_weights(i):
        d0 = pl.multiple_of(i * LANES, LANES)
        rows = pl.ds(d0, LANES)
        normed = all_rows(NA, d0, LANES)
        tile_qk = product_tn(normed, DQK[...].reshape(n_seq * B, p.qk))
        tile_v = product_tn(normed, DV[...].reshape(n_seq * B, p.vp))
        G[rows, p.qk : p.cols] = tile_v.astype(BF16)
        own_qk = W[rows, : p.qk].astype(F32)
        gain_grad = (
            jnp.sum(jnp.where(lane < at_gain, tile_qk * own_qk, 0.0), -1, keepdims=True)
            + jnp.sum(tile_v * W[rows, p.qk : p.cols].astype(F32), -1, keepdims=True)
        ) / own_qk[:, at_gain : at_gain + 1]
        rest = jnp.where(lane == at_gain, gain_grad, 0.0)
        G[rows, : p.qk] = jnp.where(lane < at_gain, tile_qk, rest).astype(BF16)

    half = D // LANES // 2
    loop(half, attention_weights)
    loop(1, lambda k: sum_step(PART, k + 1))
    loop(half, lambda i: attention_weights(i + half))
    if p.inline:
        each_peer(n_dp, dp, lambda d: band_send(d, True).start())
        each_peer(n_dp, dp, lambda d: slab_sum_band(d, False).wait_recv())
        band_total = GO[dp, :, core].astype(F32)
        for step in range(1, n_dp):
            band_total = band_total + DO[lax.rem(dp + step, n_dp)].astype(F32)
        ZS[...] = band_total.astype(BF16)
        each_peer(n_z, z, lambda zk: slab_sum(zk, True).start())
    grad_to_group(0)
    loop(n_z - 2, lambda k: sum_step(PART, k + 2))
    if p.inline:
        each_peer(n_dp, dp, lambda d: band_send(d, False).wait_recv())
        total = G[band_rows(dp)].astype(F32)
        for step in range(1, n_dp):
            total = total + GR[lax.rem(dp + step, n_dp)].astype(F32)
        GS[...] = total.astype(BF16)
        each_peer(n_seq, seq, lambda s: piece_send(s, True).start())
        grad_ref[seq] = GS[pl.ds(pl.multiple_of(seq * p.rows, p.rows), p.rows)]
    grad_to_group(1)

    group_sum_result(1, PARTB, gtok_ref)
    out_ref[...] = (STREAM[...] + gtok_ref[...]).astype(BF16)
    sum_result(PART, gtok_ref)
    inputs = tok_ref[...].astype(F32)
    factor = factor_of(inputs)
    m = inputs * factor
    f = gtok_ref[...] * gain_attn
    gtok_ref[...] = BSTREAM[...] + factor * (f - m * jnp.mean(f * m, -1, keepdims=True))

    if p.inline:
        each_peer(n_z, z, lambda zk: slab_sum(zk, False).wait_recv())
        slab_total = ZS[z].astype(F32)
        for step in range(1, n_z):
            slab_total = slab_total + ZO[lax.rem(z + step, n_z)].astype(F32)
        go_ref[...] = slab_total
        each_peer(n_seq, seq, lambda s: piece_send(s, False).wait_recv())
        for q in range(3):
            each_peer(GROUP, rank, lambda r: grad_piece(q, r, False).wait_recv())
    else:
        stay(G, grad_ref)
        stay(GM.at[0, 0, 0], gm_ref)

    gather_drain(TOK)
    share_drain(0, NM)
    share_drain(1, COT)
    group_sum_drain(0, PARTA)
    group_sum_drain(1, PARTB)
    sum_drain(PART)
    each_peer(n_seq, seq, lambda s: attended_copy(s, True).wait_send())
    each_peer(n_seq, seq, lambda s: back_copy(s, True).wait_send())
    if p.inline:
        each_peer(n_z, z, lambda zk: slab_copy(zk, True).wait_send())
        each_peer(n_dp, dp, lambda d: slab_band(d, True).wait_send())
        slab_half(core).wait_send()
        slab_sum_half().wait_send()
        each_peer(n_dp, dp, lambda d: slab_sum_band(d, True).wait_send())
        each_peer(n_z, z, lambda zk: slab_sum(zk, True).wait_send())
        each_peer(n_seq, seq, lambda s: piece_copy(s, True).wait_send())
        each_peer(n_dp, dp, lambda d: band_copy(d, True).wait_send())
        each_peer(n_dp, dp, lambda d: band_send(d, True).wait_send())
        each_peer(n_seq, seq, lambda s: piece_send(s, True).wait_send())
        for q in range(3):
            each_peer(GROUP, rank, lambda r: feed_piece(q, r, True).wait_send())
            each_peer(GROUP, rank, lambda r: grad_piece(q, r, True).wait_send())
            each_peer(n_zz, zz, lambda g: feed_along_z(q, g, True).wait_send())
            each_peer(n_zz, zz, lambda g: grad_along_z(q, g, True).wait_send())

            def left_along_y(h):
                loop(n_zz, lambda g: feed_along_y(q, h, g, True).wait_send())
                loop(n_zz, lambda g: grad_along_y(q, h, g, True).wait_send())

            each_peer(n_y, y, left_along_y)


def run_layer(plan, tokens, cotangent, weights, feed, output_rows):
    p = plan
    n_seq, n_z, n_dp, B, D = p.n_seq, p.n_z, p.n_dp, p.block, p.width
    vmem = pl.BlockSpec(memory_space=pltpu.VMEM)
    grads = (n_seq, p.rows, p.cols) if p.inline else (D, p.cols)
    dma = pltpu.SemaphoreType.DMA

    def rows(width, kind=BF16):
        return pltpu.VMEM((n_seq, B, width), kind)

    def group(width):
        return pltpu.VMEM((GROUP, B, width), BF16)

    n_y, n_zz = p.n_y, p.n_zz
    feed_grads = (GROUP, p.rows, p.wide) if p.inline else (D, p.wide)
    feed_whole = (n_y, 2, n_zz, LANES, p.wide) if p.inline else (1, 1, 1, D, p.wide)
    section = (2, LANES, p.wide) if p.inline else (1, 16, LANES)
    feed_y = (n_y, n_zz) if p.inline else (1, 1)
    band = p.band if p.inline else 16
    n_gr = n_dp if p.inline else 1
    anywhere = pl.BlockSpec(memory_space=pl.ANY)
    whole = (n_dp, n_z, 2, p.rows, p.joined) if p.inline else (1, 1, 1, D, p.joined)
    slabs = (n_z, p.rows, p.joined) if p.inline else (1, 16, LANES)
    bands = (n_dp,) + slabs if p.inline else (1, 1, 16, LANES)
    return pl.pallas_call(
        functools.partial(layer_kernel, plan),
        out_shape=(
            jax.ShapeDtypeStruct((B, D), BF16),
            jax.ShapeDtypeStruct((B, D), F32),
            jax.ShapeDtypeStruct(grads, BF16),
            jax.ShapeDtypeStruct(feed_grads, BF16),
            jax.ShapeDtypeStruct((p.rows, p.joined), F32) if p.inline else jax.ShapeDtypeStruct((D, p.joined), BF16),
        ),
        in_specs=[vmem, vmem] + [vmem if p.inline else anywhere] * 3,
        out_specs=(vmem, vmem) + (vmem if p.inline else anywhere,) * 3,
        scratch_shapes=[
            rows(D), rows(D), group(D), group(D),
            pltpu.VMEM(whole, BF16), pltpu.VMEM(whole if p.inline else (1, 1, 1, 16, LANES), BF16), pltpu.VMEM(bands, BF16), pltpu.VMEM(bands, BF16),
            pltpu.VMEM(slabs, BF16), pltpu.VMEM(slabs, BF16),
            pltpu.VMEM((B, p.joined), BF16), pltpu.VMEM((B, p.joined), BF16), rows(p.vp),
            pltpu.VMEM((D, p.cols), BF16), pltpu.VMEM(feed_whole, BF16),
            pltpu.VMEM((D, p.cols), BF16), pltpu.VMEM(feed_whole, BF16),
            pltpu.VMEM(feed_y + section, BF16), pltpu.VMEM(feed_y[1:] + section, BF16),
            pltpu.VMEM((n_gr, band, p.cols), BF16), pltpu.VMEM((band, p.cols), BF16),
            rows(p.qk), rows(p.qk), rows(p.vp), rows(p.vp), rows(p.vp, F32), rows(p.vp, F32),
            rows(p.vp), rows(p.qk), rows(p.vp), rows(p.qk, F32), rows(p.vp, F32),
            group(p.fp), group(p.fp), group(p.fp),
            rows(D), group(D), group(D),
            pltpu.VMEM((n_z, B, D), BF16), pltpu.VMEM((n_z + 1, B, D), BF16),
            pltpu.VMEM((2, 4, B, D), BF16), pltpu.VMEM((2, 2, B, D), BF16), pltpu.VMEM((2, B, D), BF16),
            pltpu.VMEM((B, D), F32), pltpu.VMEM((B, D), F32),
            dma((3, n_seq)), dma((n_seq,)), dma((n_z,)), dma((n_z,)), dma((n_z,)), dma((n_z + 1,)),
            dma((n_seq,)), dma((n_seq,)), dma((n_dp,)), dma((n_dp,)),
            dma((n_dp,)), dma((n_dp,)), dma((n_seq,)), dma((n_seq,)), dma((1,)),
            dma((n_z,)), dma((n_z,)), dma((n_dp,)), dma((n_dp,)), dma((2,)), dma((2,)),
            dma((n_z,)), dma((n_z,)), dma((n_dp,)), dma((n_dp,)),
            dma((n_seq,)), dma((n_seq,)), dma((n_seq,)), dma((n_seq,)),
            dma((2, 3, GROUP)), dma((2, GROUP)), dma((2, 4)), dma((2, 4)), dma((2, 2)), dma((2, 2)), dma((2,)), dma((2,)),
            dma((3, GROUP)), dma((3, GROUP)), dma((3, n_zz)), dma((3, n_zz)), dma((3, n_y, n_zz)), dma((3, n_y, n_zz)),
            dma((3, GROUP)), dma((3, GROUP)), dma((3, n_zz)), dma((3, n_zz)), dma((3, n_y, n_zz)), dma((3, n_y, n_zz)),
        ],
        compiler_params=pltpu.CompilerParams(
            collective_id=0, has_side_effects=True, vmem_limit_bytes=66_000_000
        ),
    )(tokens, cotangent, weights, feed, output_rows)


def on_device(tokens, w_query, w_key, w_value, w_output, w_gate, w_up, w_down, norm_attn, norm_mlp, cotangent):
    plan = Plan(
        lax.axis_size("dp"), lax.axis_size("seq"), tokens.shape[0], tokens.shape[1], w_gate.shape[1]
    )
    weights = pack_attention(plan, w_query, w_key, w_value, norm_attn, norm_mlp)
    feed = pack_feed(plan, w_gate, w_up, w_down)
    output_rows = pack_output(plan, w_output)
    axes = ("dp", "seq")
    if not plan.inline:
        dp, seq = lax.axis_index("dp"), lax.axis_index("seq")
        rank = 4 * (dp % 2) + seq % 4
        weights = lax.all_to_all(weights, "seq", split_axis=0, concat_axis=0, tiled=True)
        weights = lax.all_gather(weights, "dp").reshape(plan.width, plan.cols)
        feed = lax.all_gather(feed, axes, axis=1, tiled=True)
        feed = lax.dynamic_index_in_dim(feed, rank, 0, False)
        output_rows = lax.all_gather(output_rows, axes, axis=0, tiled=True)
    layer_out, grad_tokens, grads, grads_feed, grad_output = run_layer(
        plan, tokens, cotangent, weights, feed, output_rows
    )
    if not plan.inline:
        grads = lax.psum_scatter(grads, "dp", scatter_dimension=0, tiled=True)
        grads = grads.reshape(plan.n_seq, plan.rows, plan.cols)
        grads = lax.all_to_all(grads, "seq", split_axis=0, concat_axis=0, tiled=True)
        spread = jnp.zeros((GROUP, plan.width, plan.wide), BF16)
        spread = lax.dynamic_update_index_in_dim(spread, grads_feed, rank, 0)
        grads_feed = lax.psum_scatter(spread, axes, scatter_dimension=1, tiled=True)
        grad_output = lax.psum_scatter(grad_output, axes, scatter_dimension=0, tiled=True).astype(F32)
    return (layer_out, grad_tokens) + unpack_grads(plan, grads, grads_feed, grad_output)


def solution(mesh):
    rows, cols, vec = P(("dp", "seq"), None), P(None, ("dp", "seq")), P(("dp", "seq"))
    return jax.shard_map(
        on_device,
        mesh=mesh,
        in_specs=(rows, rows, rows, rows, cols, rows, rows, cols, vec, vec, rows),
        out_specs=(rows, rows, rows, rows, rows, cols, rows, rows, cols, vec, vec),
        check_vma=False,
    )
```

```python
import functools

import jax
import jax.numpy as jnp
from jax import lax
from jax.experimental import pallas as pl
from jax.experimental.pallas import tpu as pltpu
from jax.sharding import PartitionSpec as P

HEADS = 16
FEAT_DIM = 16
HEAD_V = 64
EPSILON = 1e-06
LANES = 128
GROUP = 8
MESH = pl.DeviceIdType.MESH
BF16 = jnp.bfloat16
F32 = jnp.float32


def round_up(size, unit):
    return -(-size // unit) * unit


def product(a, b):
    return jnp.dot(a, b, preferred_element_type=F32)


def product_nt(a, b):
    return lax.dot_general(a, b, (((1,), (1,)), ((), ())), preferred_element_type=F32)


def product_tn(a, b):
    return lax.dot_general(a, b, (((0,), (0,)), ((), ())), preferred_element_type=F32)


class Plan:
    def __init__(self, n_dp, n_seq, block, width, hidden):
        self.n_dp, self.n_seq, self.n_z = n_dp, n_seq, n_seq // 2
        self.block, self.width = block, width
        self.heads = HEADS // n_seq
        self.feat = self.heads * FEAT_DIM
        self.value = self.heads * HEAD_V
        self.unit = hidden // GROUP
        self.qk = round_up(2 * self.feat + 2, LANES)
        self.vp = round_up(self.value, LANES)
        self.fp = round_up(self.unit + 1, LANES)
        self.rows = width // (n_dp * n_seq)
        self.band = width // n_dp
        self.cols = self.qk + self.vp
        self.wide = 3 * self.fp
        self.joined = n_seq * self.vp
        self.n_y, self.n_zz = n_dp // 2, self.n_z // 2
        self.inline = 4 * self.rows == LANES and self.vp == self.value


def cut(w, parts):
    return w.reshape(w.shape[0], parts, -1).transpose(1, 0, 2)


def pad(parts, to):
    joined = jnp.concatenate(parts, -1) if len(parts) > 1 else parts[0]
    return jnp.pad(joined, ((0, 0), (0, 0), (0, to - joined.shape[-1])))


def pack_attention(plan, w_query, w_key, w_value, norm_attn, norm_mlp):
    s = plan.n_seq
    gains = jnp.broadcast_to(jnp.stack([norm_attn, norm_mlp], -1), (s, plan.rows, 2))
    return jnp.concatenate(
        [pad([cut(w_query, s), cut(w_key, s), gains], plan.qk), pad([cut(w_value, s)], plan.vp)], -1
    )


def pack_feed(plan, w_gate, w_up, w_down):
    return jnp.concatenate([pad([cut(w, GROUP)], plan.fp) for w in (w_gate, w_up, w_down.T)], -1)


def pack_output(plan, w_output):
    heads = w_output.T.reshape(plan.rows, plan.n_seq, plan.value)
    return jnp.pad(heads, ((0, 0), (0, 0), (0, plan.vp - plan.value))).reshape(plan.rows, plan.joined)


def unpack_grads(plan, owned, owned_feed, owned_output):
    r = plan.rows

    def join(pieces, start, unit):
        return pieces[:, :, start : start + unit].transpose(1, 0, 2).reshape(r, -1).astype(F32)

    at_gain = 2 * plan.feat
    return (
        join(owned, 0, plan.feat),
        join(owned, plan.feat, plan.feat),
        join(owned, plan.qk, plan.value),
        owned_output.reshape(r, plan.n_seq, plan.vp)[:, :, : plan.value].reshape(r, -1).T,
        join(owned_feed, 0, plan.unit),
        join(owned_feed, plan.fp, plan.unit),
        join(owned_feed, 2 * plan.fp, plan.unit).T,
        jnp.sum(owned[:, :, at_gain].astype(F32), 0),
        jnp.sum(owned_feed[:, :, plan.fp + plan.unit].astype(F32), 0),
    )


def pack_in_kernel(p, raw, w_ref, wm_ref, wo_ref):
    wq, wk, wv, wo, wg, wu, wd, gain_attn, gain_mlp = raw
    columns = [gain_attn[...].astype(F32).T.astype(BF16), gain_mlp[...].astype(F32).T.astype(BF16)]
    spare = jnp.zeros((p.rows, p.qk - 2 * p.feat - 2), BF16)
    for c in range(p.n_seq):
        here = slice(c * p.feat, (c + 1) * p.feat)
        w_ref[c, :, : p.qk] = jnp.concatenate([wq[:, here], wk[:, here]] + columns + [spare], -1)
        w_ref[c, :, p.qk : p.qk + p.value] = wv[:, c * p.value : (c + 1) * p.value]
    wo_ref[...] = wo[...]
    blank = jnp.zeros((p.rows, p.fp - p.unit), BF16)
    for q, whole in enumerate((wg, wu, wd)):
        for r in range(GROUP):
            piece = whole[:, r * p.unit : (r + 1) * p.unit]
            wm_ref[r, :, q * p.fp : (q + 1) * p.fp] = jnp.concatenate([piece, blank], -1)


def layer_kernel(plan, *refs):
    p = plan
    (
        tok_ref, cot_ref, *rest
    ) = refs
    if p.inline:
        sources, rest = refs[:11], refs[11:]
        out_ref, gtok_ref, grad_ref, gm_ref, go_ref, *rest = rest
        w_ref, wm_ref, wo_ref, WZ, *rest = rest
        held, in_sem, rest = rest[:11], rest[11], rest[12:]
        tok_ref, cot_ref = held[:2]
    else:
        w_ref, wm_ref, wo_ref, out_ref, gtok_ref, grad_ref, gm_ref, go_ref, *rest = rest
        WZ = None
    (
        TOK, NA, COT, NM, WO, GO, SO, DO, ZS, ZO, AO, BAT, BATT,
        W, WM, G, GM, GY, GZ, GR, GS,
        Q, K, V, ATT, ATTF, DEN, BNUM, DQK, DV, DKF, DVF,
        H, BG, BU,
        PART, PARTA, PARTB, SIB, CH, HALF, XR, ZR, STREAM, BSTREAM,
        ag_send, ag_recv, sib_send, sib_recv, ch_send, ch_recv,
        w_send, w_recv, wd_send, wd_recv,
        g_send, g_recv, gz_send, gz_recv, local_sem,
        wo_send, wo_recv, wod_send, wod_recv, sl_send, sl_recv,
        go_send, go_recv, gd_send, gd_recv, at_send, at_recv, bt_send, bt_recv,
        sh_send, sh_recv, ha_send, ha_recv, xr_send, xr_recv, zr_send, zr_recv,
        wp_send, wp_recv, wz_send, wz_recv, wy_send, wy_recv,
        gp_send, gp_recv, gw_send, gw_recv, gy_send, gy_recv,
    ) = rest
    if not p.inline:
        GO = WO
    dp, seq = lax.axis_index("dp"), lax.axis_index("seq")
    n_seq, n_z, n_dp, B, D = p.n_seq, p.n_z, p.n_dp, p.block, p.width
    z, core = seq // 2, seq % 2
    sibling = (dp, seq + 1 - 2 * core)
    above, below = (dp, seq + 2), (dp, seq - 2)
    is_top, is_bottom = z == n_z - 1, z == 0
    n_y, n_zz = p.n_y, p.n_zz
    x, y, zl, zz = dp % 2, dp // 2, z % 2, z // 2
    rank = 4 * x + 2 * zl + core

    def at(r):
        return (2 * y + r // 4, 4 * zz + r % 4)

    x_peer, z_peer = (dp + 1 - 2 * x, seq), (dp, seq + 2 - 4 * zl)

    def remote(src, dst, send, recv, device):
        return pltpu.make_async_remote_copy(
            src_ref=src, dst_ref=dst, send_sem=send, recv_sem=recv,
            device_id=device, device_id_type=MESH,
        )

    def each_peer(count, mine, body):
        def one(i, carry):
            @pl.when(i != mine)
            def _():
                body(i)

            return carry

        lax.fori_loop(0, count, one, 0)

    def loop(count, body):
        def one(i, carry):
            body(i)
            return carry

        lax.fori_loop(0, count, one, 0)

    if p.inline:
        reading = [
            pltpu.make_async_copy(src, dst, in_sem.at[i]) for i, (src, dst) in enumerate(zip(sources, held))
        ]
        for copy in reading:
            copy.start()

    barrier = pltpu.get_barrier_semaphore()
    each_peer(n_seq, seq, lambda i: pl.semaphore_signal(barrier, inc=1, device_id=(dp, i), device_id_type=MESH))
    each_peer(n_dp, dp, lambda i: pl.semaphore_signal(barrier, inc=1, device_id=(i, seq), device_id_type=MESH))
    for other in (4 - 4 * x + 2 * zl + 1 - core, 4 - 4 * x + 2 - 2 * zl + core, 4 - 4 * x + 2 - 2 * zl + 1 - core):
        pl.semaphore_signal(barrier, inc=1, device_id=at(other), device_id_type=MESH)
    if p.inline:
        for copy in reading:
            copy.wait()
        pack_in_kernel(p, held[2:], w_ref, wm_ref, wo_ref)
    pl.semaphore_wait(barrier, n_seq - 1 + n_dp - 1 + 3)

    near = jnp.minimum(z, n_z - 1 - z)
    far_side = jnp.where(z < n_z - 1 - z, 1, -1)

    def order(k):
        step = (k + 1) // 2
        alternate = jnp.where(k % 2 == 1, -step, step)
        return z + jnp.where(k <= 2 * near, alternate, far_side * (k - near))

    def piece_rows(d, s):
        return pl.ds(pl.multiple_of((d * n_seq + s) * p.rows, p.rows), p.rows)

    def band_rows(d):
        return pl.ds(pl.multiple_of(d * p.band, p.band), p.band)

    def piece_copy(s, mine):
        src_of = seq if mine else s
        return remote(w_ref.at[s], W.at[piece_rows(dp, src_of)], w_send.at[s], w_recv.at[src_of], (dp, s))

    def band_copy(d, mine):
        src_of = dp if mine else d
        return remote(
            W.at[band_rows(src_of)], W.at[band_rows(src_of)], wd_send.at[d], wd_recv.at[src_of], (d, seq)
        )

    def third(q):
        return pl.ds(q * p.fp, p.fp)

    def feed_along_z(q, g, mine):
        src_of = zz if mine else g
        return remote(
            wm_ref.at[:, :, third(q)], WZ.at[src_of, :, :, third(q)],
            wz_send.at[q, g], wz_recv.at[q, src_of], (dp, 4 * g + 2 * zl + core),
        )

    def feed_source(q, g, r):
        return wm_ref.at[r, :, third(q)] if g is None else WZ.at[g, r, :, third(q)]

    def feed_piece(q, g, r, mine):
        src_of = rank if mine else r
        section = zz if g is None else g
        rows = pl.ds(pl.multiple_of((src_of % 4) * p.rows, p.rows), p.rows)
        return remote(
            feed_source(q, g, r), WM.at[y, src_of // 4, section, rows, third(q)],
            wp_send.at[q, section, r], wp_recv.at[q, section, src_of], at(r),
        )

    def feed_along_y(q, h, g, mine):
        src_of = y if mine else h
        section = WM.at[src_of, :, g, :, third(q)]
        return remote(section, section, wy_send.at[q, h, g], wy_recv.at[q, src_of, g], (2 * h + x, seq))

    def feed_to_z(q):
        if p.inline:
            each_peer(n_zz, zz, lambda g: feed_along_z(q, g, True).start())

    def feed_to_group(q, g):
        each_peer(GROUP, rank, lambda r: feed_piece(q, g, r, True).start())
        rows = pl.ds(pl.multiple_of((rank % 4) * p.rows, p.rows), p.rows)
        WM[y, x, zz if g is None else g, rows, third(q)] = feed_source(q, g, rank)[...]

    def feed_on_to_group(q):
        def one(g):
            feed_along_z(q, g, False).wait_recv()
            feed_to_group(q, g)

        if p.inline:
            each_peer(n_zz, zz, one)

    def feed_section_to_y(q, g):
        each_peer(GROUP, rank, lambda r: feed_piece(q, g, r, False).wait_recv())
        each_peer(n_y, y, lambda h: feed_along_y(q, h, zz if g is None else g, True).start())

    def feed_on_to_y(q):
        if p.inline:
            each_peer(n_zz, zz, lambda g: feed_section_to_y(q, g))

    def feed_arrived(q):
        if p.inline:
            each_peer(n_y, y, lambda h: loop(n_zz, lambda g: feed_along_y(q, h, g, False).wait_recv()))

    def grad_along_y(q, h, g, mine):
        src_of = y if mine else h
        return remote(
            GM.at[h, :, g, :, third(q)], GY.at[src_of, g, :, :, third(q)],
            gy_send.at[q, h, g], gy_recv.at[q, src_of, g], (2 * h + x, seq),
        )

    def grad_along_z(q, g, mine):
        src_of = zz if mine else g
        return remote(
            GM.at[y, :, g, :, third(q)], GZ.at[src_of, :, :, third(q)],
            gw_send.at[q, g], gw_recv.at[q, src_of], (dp, 4 * g + 2 * zl + core),
        )

    def grad_piece(q, r, mine):
        src_of = rank if mine else r
        rows = pl.ds(pl.multiple_of((r % 4) * p.rows, p.rows), p.rows)
        return remote(
            GM.at[y, r // 4, zz, rows, third(q)], gm_ref.at[src_of, :, third(q)],
            gp_send.at[q, r], gp_recv.at[q, src_of], at(r),
        )

    def grad_to_y(q):
        if p.inline:
            for step in range(n_zz):
                g = lax.rem(zz + 1 + step, n_zz)
                each_peer(n_y, y, lambda h: grad_along_y(q, h, g, True).start())

    def grad_to_z(q):
        if not p.inline:
            return
        for step in range(n_zz):
            g = lax.rem(zz + 1 + step, n_zz)
            total = GM[y, :, g, :, third(q)].astype(F32)
            for other in range(1, n_y):
                h = lax.rem(y + other, n_y)
                grad_along_y(q, h, g, False).wait_recv()
                total = total + GY[h, g, :, :, third(q)].astype(F32)
            GM[y, :, g, :, third(q)] = total.astype(BF16)
            if step < n_zz - 1:
                grad_along_z(q, g, True).start()

    def grad_to_group(q):
        if not p.inline:
            return
        total = GM[y, :, zz, :, third(q)].astype(F32)
        for step in range(1, n_zz):
            g = lax.rem(zz + step, n_zz)
            grad_along_z(q, g, False).wait_recv()
            total = total + GZ[g, :, :, third(q)].astype(F32)
        GM[y, :, zz, :, third(q)] = total.astype(BF16)
        each_peer(GROUP, rank, lambda r: grad_piece(q, r, True).start())
        rows = pl.ds(pl.multiple_of((rank % 4) * p.rows, p.rows), p.rows)
        gm_ref[rank, :, third(q)] = GM[y, x, zz, rows, third(q)]

    def spot(w):
        return 4 * jnp.where(w >= 2, 1 - x, x) + 2 * jnp.where(w % 2 == 1, 1 - zl, zl)

    def share_copy(a, buf, b, way, device):
        return remote(buf.at[b], buf.at[b], sh_send.at[a, way, b], sh_recv.at[a, b], device)

    def share_step(a, buf, w, on_block):
        def one(side):
            take = jnp.where(side == 0, w < 4, w >= 1)

            @pl.when(take)
            def _():
                b = spot(w - side) + jnp.where(side == 0, core, 1 - core)

                @pl.when(b != rank)
                def _():
                    share_copy(a, buf, b, 2, sibling).wait_recv()

                @pl.when(side == 0)
                def _():
                    @pl.when(w == 0)
                    def _():
                        share_copy(a, buf, b, 0, z_peer).start()

                    @pl.when(w <= 1)
                    def _():
                        share_copy(a, buf, b, 1, x_peer).start()

                    share_copy(a, buf, b, 2, sibling).start()

                if on_block is not None:
                    on_block(b)

        loop(2, one)

    def share_drain(a, buf):
        def one(w):
            b = spot(w) + core

            @pl.when(w == 0)
            def _():
                share_copy(a, buf, b, 0, z_peer).wait_send()

            @pl.when(w <= 1)
            def _():
                share_copy(a, buf, b, 1, x_peer).wait_send()

            share_copy(a, buf, b, 2, sibling).wait_send()

        loop(4, one)

    def half_copy(i, part, w):
        return remote(part.at[spot(w) + 1 - core], HALF.at[i, w], ha_send.at[i, w], ha_recv.at[i, w], sibling)

    def x_copy(i, part, w):
        return remote(part.at[spot(w) + core], XR.at[i, w - 2], xr_send.at[i, w - 2], xr_recv.at[i, w - 2], x_peer)

    def z_copy(i, part):
        return remote(part.at[spot(1) + core], ZR.at[i], zr_send.at[i], zr_recv.at[i], z_peer)

    def group_sum_step(i, part, w):
        b = spot(w) + core
        half_copy(i, part, w).wait_recv()
        total = part[b].astype(F32) + HALF[i, w].astype(F32)
        if w == 1:
            x_copy(i, part, 3).wait_recv()
            total = total + XR[i, 1].astype(F32)
        part[b] = total.astype(BF16)
        (z_copy(i, part) if w == 1 else x_copy(i, part, w)).start()

    def group_sum_result(i, part, total):
        half_copy(i, part, 0).wait_recv()
        x_copy(i, part, 2).wait_recv()
        z_copy(i, part).wait_recv()
        total[...] = (
            part[rank].astype(F32) + HALF[i, 0].astype(F32) + XR[i, 0].astype(F32) + ZR[i].astype(F32)
        )

    def group_sum_drain(i, part):
        loop(4, lambda w: half_copy(i, part, w).wait_send())
        x_copy(i, part, 2).wait_send()
        x_copy(i, part, 3).wait_send()
        z_copy(i, part).wait_send()

    def gather_copy(buf, j, way, device):
        return remote(buf.at[j], buf.at[j], ag_send.at[way, j], ag_recv.at[j], device)

    def gather_step(buf, k, on_block):
        def one(side):
            take = jnp.where(side == 0, k < n_z, k >= 1)

            @pl.when(take)
            def _():
                zk = order(k - side)
                j = 2 * zk + jnp.where(side == 0, core, 1 - core)

                @pl.when(j != seq)
                def _():
                    gather_copy(buf, j, 0, sibling).wait_recv()

                @pl.when(side == 0)
                def _():
                    @pl.when(jnp.logical_and(zk <= z, jnp.logical_not(is_top)))
                    def _():
                        gather_copy(buf, j, 0, above).start()

                    @pl.when(jnp.logical_and(zk >= z, jnp.logical_not(is_bottom)))
                    def _():
                        gather_copy(buf, j, 1, below).start()

                    gather_copy(buf, j, 2, sibling).start()

                if on_block is not None:
                    on_block(j)

        loop(2, one)

    def gather_drain(buf):
        def one(zk):
            j = 2 * zk + core

            @pl.when(jnp.logical_and(zk <= z, jnp.logical_not(is_top)))
            def _():
                gather_copy(buf, j, 0, above).wait_send()

            @pl.when(jnp.logical_and(zk >= z, jnp.logical_not(is_bottom)))
            def _():
                gather_copy(buf, j, 1, below).wait_send()

            gather_copy(buf, j, 2, sibling).wait_send()

        loop(n_z, one)

    def sibling_copy(part, zk):
        return remote(
            part.at[2 * zk + 1 - core], SIB.at[zk], sib_send.at[zk], sib_recv.at[zk], sibling
        )

    def chain_copy(part, zk, up):
        slot = zk if up else jnp.where(zk == z - 1, n_z, zk)
        return remote(
            part.at[2 * zk + core], CH.at[slot], ch_send.at[zk], ch_recv.at[slot],
            above if up else below,
        )

    def chain_wait(part, slot):
        remote(part.at[0], CH.at[slot], ch_send.at[0], ch_recv.at[slot], sibling).wait_recv()

    def far(k):
        return order(n_z - 1 - k)

    def sum_step(part, k):
        zk = far(k)
        j = 2 * zk + core
        remote(part.at[0], SIB.at[zk], sib_send.at[zk], sib_recv.at[zk], sibling).wait_recv()

        @pl.when(zk != z)
        def _():
            first = jnp.where(zk > z, is_bottom, is_top)

            @pl.when(first)
            def _():
                part[j] = (part[j].astype(F32) + SIB[zk].astype(F32)).astype(BF16)

            @pl.when(jnp.logical_not(first))
            def _():
                chain_wait(part, zk)
                part[j] = (
                    part[j].astype(F32) + SIB[zk].astype(F32) + CH[zk].astype(F32)
                ).astype(BF16)

            @pl.when(zk > z)
            def _():
                chain_copy(part, zk, True).start()

            @pl.when(zk < z)
            def _():
                chain_copy(part, zk, False).start()

    def sum_result(part, total):
        total[...] = part[seq].astype(F32) + SIB[z].astype(F32)

        @pl.when(jnp.logical_not(is_bottom))
        def _():
            chain_wait(part, z)
            total[...] += CH[z].astype(F32)

        @pl.when(jnp.logical_not(is_top))
        def _():
            chain_wait(part, n_z)
            total[...] += CH[n_z].astype(F32)

    def sum_drain(part):
        def one(zk):
            sibling_copy(part, zk).wait_send()

            @pl.when(zk > z)
            def _():
                chain_copy(part, zk, True).wait_send()

            @pl.when(zk < z)
            def _():
                chain_copy(part, zk, False).wait_send()

        loop(n_z, one)

    def slab_copy(zk, mine):
        src_of = z if mine else zk
        return remote(
            wo_ref, WO.at[dp, src_of, core], wo_send.at[zk], wo_recv.at[src_of], (dp, 2 * zk + core)
        )

    def slab_band(d, mine):
        src_of = dp if mine else d
        return remote(
            WO.at[src_of, :, core], WO.at[src_of, :, core], wod_send.at[d], wod_recv.at[src_of], (d, seq)
        )

    def slab_half(which):
        return remote(WO.at[:, :, which], WO.at[:, :, which], sl_send.at[0], sl_recv.at[0], sibling)

    def slab_sum_half():
        return remote(GO.at[:, :, 1 - core], SO, sl_send.at[1], sl_recv.at[1], sibling)

    def slab_sum_band(d, mine):
        src_of = dp if mine else d
        return remote(GO.at[d, :, core], DO.at[src_of], gd_send.at[d], gd_recv.at[src_of], (d, seq))

    def slab_sum(zk, mine):
        src_of = z if mine else zk
        return remote(ZS.at[zk], ZO.at[src_of], go_send.at[zk], go_recv.at[src_of], (dp, 2 * zk + core))

    def lanes_of(s):
        return pl.ds(pl.multiple_of(s * p.vp, p.vp), p.vp)

    def attended_copy(s, mine):
        src_of = seq if mine else s
        return remote(ATT.at[s], AO.at[:, lanes_of(src_of)], at_send.at[s], at_recv.at[src_of], (dp, s))

    def back_copy(s, mine):
        src_of = seq if mine else s
        return remote(BAT.at[:, lanes_of(s)], BATT.at[src_of], bt_send.at[s], bt_recv.at[src_of], (dp, s))

    def stay(src, dst):
        own = pltpu.make_async_copy(src, dst, local_sem.at[0])
        own.start()
        own.wait()

    if p.inline:
        each_peer(n_seq, seq, lambda s: piece_copy(s, True).start())
        each_peer(n_z, z, lambda zk: slab_copy(zk, True).start())
        TOK[seq] = tok_ref[...]
        gather_step(TOK, 0, None)
        for q in range(3):
            feed_to_group(q, None)
        feed_to_z(0)
        W[piece_rows(dp, seq)] = w_ref[seq]
        WO[dp, z, core] = wo_ref[...]
        COT[rank] = cot_ref[...]
        each_peer(n_seq, seq, lambda s: piece_copy(s, False).wait_recv())
        each_peer(n_dp, dp, lambda d: band_copy(d, True).start())
        each_peer(n_z, z, lambda zk: slab_copy(zk, False).wait_recv())
        each_peer(n_dp, dp, lambda d: slab_band(d, True).start())
        gather_step(TOK, 1, None)
        feed_to_z(1)
        for q in range(3):
            feed_section_to_y(q, None)
        gather_step(TOK, 2, None)
        feed_to_z(2)
        each_peer(n_dp, dp, lambda d: band_copy(d, False).wait_recv())
    else:
        TOK[seq] = tok_ref[...]
        gather_step(TOK, 0, None)
        stay(w_ref, W)
        stay(wm_ref, WM.at[0, 0, 0])
        stay(wo_ref, WO.at[0, 0, 0])
        COT[rank] = cot_ref[...]
        gather_step(TOK, 1, None)
        gather_step(TOK, 2, None)
    loop(n_z - 4, lambda k: gather_step(TOK, k + 3, None))

    lane = lax.broadcasted_iota(jnp.int32, (1, p.qk), 1)
    vlane = lax.broadcasted_iota(jnp.int32, (1, p.vp), 1)
    feat_masks = [
        jnp.logical_and(lane >= h * FEAT_DIM, lane < (h + 1) * FEAT_DIM).astype(BF16) for h in range(p.heads)
    ]
    value_masks = [
        jnp.logical_and(vlane >= h * HEAD_V, vlane < (h + 1) * HEAD_V).astype(BF16) for h in range(p.heads)
    ]
    spare = (vlane >= p.value).astype(F32)
    row = lax.broadcasted_iota(jnp.int32, (p.qk, p.qk), 0)
    col = lax.broadcasted_iota(jnp.int32, (p.qk, p.qk), 1)
    shift = jnp.logical_and(row == col + p.feat, col < p.feat).astype(F32).astype(BF16)
    at_gain = 2 * p.feat
    pick = lax.broadcasted_iota(jnp.int32, (16, p.qk), 0) + at_gain == lax.broadcasted_iota(
        jnp.int32, (16, p.qk), 1
    )
    gain_rows = product_nt(pick.astype(F32).astype(BF16), W[:, : p.qk])
    gain_attn, gain_mlp = gain_rows[0:1], gain_rows[1:2]
    scale = FEAT_DIM ** -0.5
    one_lane = (lane == p.qk - 1).astype(F32)
    C = 2 * B
    below_diag = lax.broadcasted_iota(jnp.int32, (C, C), 0) >= lax.broadcasted_iota(jnp.int32, (C, C), 1)

    def factor_of(x):
        return lax.rsqrt(jnp.mean(x * x, -1, keepdims=True) + EPSILON)

    def project(j):
        x = TOK[j].astype(F32)
        normed = (x * factor_of(x) * gain_attn).astype(BF16)
        NA[j] = normed
        qk = product(normed, W[:, : p.qk]).astype(BF16)
        Q[j] = (qk.astype(F32) * scale).astype(BF16)
        K[j] = (product(qk, shift) + one_lane).astype(BF16)
        V[j] = product(normed, W[:, p.qk : p.cols]).astype(BF16)

    loop(n_z - 1, lambda k: project(2 * order(k) + core))
    loop(n_z - 2, lambda k: project(2 * order(k) + 1 - core))
    feed_on_to_group(0)
    gather_step(TOK, n_z - 1, project)
    share_step(1, COT, 0, None)
    feed_on_to_y(0)
    feed_on_to_group(1)
    gather_step(TOK, n_z, project)

    def chip_rows(buf, i):
        return buf[pl.ds(2 * i, 2)].reshape(C, buf.shape[-1])

    def store_rows(buf, i, value):
        buf[pl.ds(2 * i, 2)] = value.reshape(2, B, value.shape[-1]).astype(buf.dtype)

    def one_plus_t(query, key):
        return product_nt(query, key)

    def query_of(queries, h):
        return queries * feat_masks[h] + one_lane.astype(BF16)

    def attend(i):
        queries = chip_rows(Q, i)

        def inner(j, acc, diagonal):
            keys, values = chip_rows(K, j), chip_rows(V, j)
            for h in range(p.heads):
                u = product_nt(query_of(queries, h), keys)
                s = 0.5 * u * u + 0.5
                if diagonal:
                    s = jnp.where(below_diag, s, 0.0)
                ones = jnp.broadcast_to(value_masks[h], (C, p.vp))
                acc = acc + product(s.astype(BF16), jnp.concatenate([values * value_masks[h], ones], -1))
            return acc

        acc = lax.fori_loop(0, i, lambda j, acc: inner(j, acc, False), jnp.zeros((C, 2 * p.vp), F32))
        acc = inner(i, acc, True)
        den = acc[:, p.vp :] + spare
        att = acc[:, : p.vp] / den
        store_rows(DEN, i, den)
        store_rows(ATTF, i, att)
        store_rows(ATT, i, att)

        def give(side):
            @pl.when(2 * i + side != seq)
            def _():
                attended_copy(2 * i + side, True).start()

        loop(2, give)

    loop(n_z, lambda k: attend(far(k)))
    AO[:, lanes_of(seq)] = ATT[seq]
    share_step(1, COT, 1, None)
    feed_on_to_y(1)
    feed_on_to_group(2)
    if p.inline:
        each_peer(n_dp, dp, lambda d: slab_band(d, False).wait_recv())
        slab_half(core).start()
    each_peer(n_seq, seq, lambda s: attended_copy(s, False).wait_recv())
    if p.inline:
        slab_half(1 - core).wait_recv()
    STREAM[...] = tok_ref[...].astype(F32) + product_nt(AO[...], WO[...].reshape(D, p.joined))

    stream = STREAM[...]
    NM[rank] = (stream * factor_of(stream) * gain_mlp).astype(BF16)
    share_step(0, NM, 0, None)
    feed_on_to_y(2)
    loop(3, lambda w: share_step(1, COT, w + 2, None))
    for q in range(3):
        feed_arrived(q)

    def weight(q):
        return WM[:, :, :, :, third(q)].reshape(D, p.fp)

    def feed(j):
        normed = NM[j]
        gate = product(normed, weight(0))
        up = product(normed, weight(1))
        back = product(COT[j], weight(2))
        sig = jax.nn.sigmoid(gate)
        act = gate * sig
        H[j] = (act * up).astype(BF16)
        BG[j] = (back * up * sig * (1.0 + gate * (1.0 - sig))).astype(BF16)
        BU[j] = (back * act).astype(BF16)
        PARTA[j] = (product_nt(BG[j], weight(0)) + product_nt(BU[j], weight(1))).astype(BF16)
        PARTB[j] = product_nt(H[j], weight(2)).astype(BF16)

        @pl.when(j % 2 != core)
        def _():
            w = 2 * jnp.where(j // 4 != x, 1, 0) + jnp.where((j // 2) % 2 != zl, 1, 0)
            half_copy(0, PARTA, w).start()
            half_copy(1, PARTB, w).start()

    feed(rank)
    loop(4, lambda w: share_step(0, NM, w + 1, feed))

    def all_rows(buf, d0, size):
        return buf[:, :, pl.ds(d0, size)].reshape(buf.shape[0] * B, size)

    def chunk_of(buf, i):
        if p.inline:
            return buf.at[i // (2 * n_zz), (i // n_zz) % 2, i % n_zz]
        return buf.at[0, 0, 0, pl.ds(pl.multiple_of(i * LANES, LANES), LANES)]

    feed_lane = lax.broadcasted_iota(jnp.int32, (1, p.fp), 1)

    def back_of_weights(q, left, right):
        def one(i):
            d0 = pl.multiple_of(i * LANES, LANES)
            tile = product_tn(all_rows(left, d0, LANES), right[...].reshape(GROUP * B, p.fp))
            grads, own = chunk_of(GM, i), chunk_of(WM, i)
            if q == 1:
                both = tile * own[:, third(1)].astype(F32) + grads[:, third(0)].astype(F32) * own[
                    :, third(0)
                ].astype(F32)
                gain = W[pl.ds(d0, LANES), : p.qk].astype(F32)[:, at_gain + 1 : at_gain + 2]
                tile = jnp.where(feed_lane == p.unit, jnp.sum(both, -1, keepdims=True) / gain, tile)
            grads[:, third(q)] = tile.astype(BF16)

        loop(D // LANES, one)
        grad_to_y(q)

    group_sum_step(0, PARTA, 3)
    group_sum_step(0, PARTA, 2)
    back_of_weights(2, COT, H)
    group_sum_step(0, PARTA, 1)
    back_of_weights(0, NM, BG)
    grad_to_z(2)
    back_of_weights(1, NM, BU)
    group_sum_result(0, PARTA, BSTREAM)
    back_normed = BSTREAM[...]
    stream = STREAM[...]
    factor = factor_of(stream)
    n = stream * factor
    e = back_normed * gain_mlp
    BSTREAM[...] = cot_ref[...].astype(F32) + factor * (e - n * jnp.mean(e * n, -1, keepdims=True))
    BM = BSTREAM[...].astype(BF16)
    BAT[...] = product(BM, WO[...].reshape(D, p.joined)).astype(BF16)
    each_peer(n_seq, seq, lambda s: back_copy(s, True).start())
    BATT[seq] = BAT[:, lanes_of(seq)]
    GO[...] = product_tn(BM, AO[...]).astype(BF16).reshape(GO.shape)

    if p.inline:
        slab_sum_half().start()
    else:
        stay(GO.at[0, 0, 0], go_ref)

    def band_send(d, mine):
        src_of = dp if mine else d
        return remote(G.at[band_rows(d)], GR.at[src_of], g_send.at[d], g_recv.at[src_of], (d, seq))

    def piece_send(s, mine):
        src_of = seq if mine else s
        rows = pl.ds(pl.multiple_of(s * p.rows, p.rows), p.rows)
        return remote(GS.at[rows], grad_ref.at[src_of], gz_send.at[s], gz_recv.at[src_of], (dp, s))

    def back_heads(j):
        back = BATT[j].astype(F32)
        den = DEN[j]
        BNUM[j] = (back / den).astype(BF16)
        prod = back * ATTF[j]
        out = jnp.zeros((B, p.vp), F32)
        for h in range(p.heads):
            total = jnp.sum(prod * value_masks[h].astype(F32), -1, keepdims=True)
            out = jnp.where(value_masks[h] > 0, -total, out)
        ATTF[j] = out / den
        DKF[j] = jnp.zeros((B, p.qk), F32)
        DVF[j] = jnp.zeros((B, p.vp), F32)

    group_sum_step(1, PARTB, 3)
    group_sum_step(1, PARTB, 2)
    grad_to_z(0)
    each_peer(n_seq, seq, lambda s: back_copy(s, False).wait_recv())
    loop(n_seq, back_heads)

    def attend_back(i):
        queries, numer, denom = chip_rows(Q, i), chip_rows(BNUM, i), chip_rows(ATTF, i)
        high = denom.astype(BF16)
        low = (denom - high.astype(F32)).astype(BF16)

        def inner(j, dq, diagonal):
            keys, values = chip_rows(K, j), chip_rows(V, j)
            dk, dv = chip_rows(DKF, j), chip_rows(DVF, j)
            one = (vlane < 2).astype(BF16)
            wide_values = jnp.concatenate([values, jnp.broadcast_to(one, (C, p.vp))], -1)
            for h in range(p.heads):
                qh, bh = query_of(queries, h), numer * value_masks[h]
                first = h * HEAD_V
                extra = jnp.where(
                    vlane == 0, high[:, first : first + 1].astype(F32),
                    jnp.where(vlane == 1, low[:, first : first + 1].astype(F32), 0.0),
                ).astype(BF16)
                u = product_nt(qh, keys)
                ds = product_nt(jnp.concatenate([bh, extra], -1), wide_values)
                s, dt = 0.5 * u * u + 0.5, ds * u
                if diagonal:
                    s, dt = jnp.where(below_diag, s, 0.0), jnp.where(below_diag, dt, 0.0)
                dt = dt.astype(BF16)
                dq = dq + product(dt, keys * feat_masks[h])
                dk = dk + product_tn(dt, queries * feat_masks[h])
                dv = dv + product_tn(s.astype(BF16), bh)
            store_rows(DKF, j, dk)
            store_rows(DVF, j, dv)
            return dq

        dq = lax.fori_loop(0, i, lambda j, dq: inner(j, dq, False), jnp.zeros((C, p.qk), F32))
        dq = inner(i, dq, True)
        store_rows(DQK, i, dq * scale)

    loop(n_z // 2, attend_back)
    if p.inline:
        slab_sum_half().wait_recv()
        GO[:, :, core] = (GO[:, :, core].astype(F32) + SO[...].astype(F32)).astype(BF16)
        each_peer(n_dp, dp, lambda d: slab_sum_band(d, True).start())
    group_sum_step(1, PARTB, 1)
    grad_to_z(1)
    loop(n_z - n_z // 2, lambda k: attend_back(k + n_z // 2))

    def back_input(j):
        dk = DKF[j].astype(BF16)
        qk = (DQK[j].astype(F32) + product_nt(dk, shift)).astype(BF16)
        DQK[j] = qk
        DV[j] = DVF[j].astype(BF16)
        PART[j] = (
            product_nt(qk, W[:, : p.qk]) + product_nt(DV[j], W[:, p.qk : p.cols])
        ).astype(BF16)

    def fourth_sum(k):
        loop(2, lambda side: back_input(2 * far(k) + side))
        sibling_copy(PART, far(k)).start()

    loop(n_z, fourth_sum)
    loop(1, lambda k: sum_step(PART, k))
    grad_to_group(2)

    def attention_weights(i):
        d0 = pl.multiple_of(i * LANES, LANES)
        rows = pl.ds(d0, LANES)
        normed = all_rows(NA, d0, LANES)
        tile_qk = product_tn(normed, DQK[...].reshape(n_seq * B, p.qk))
        tile_v = product_tn(normed, DV[...].reshape(n_seq * B, p.vp))
        G[rows, p.qk : p.cols] = tile_v.astype(BF16)
        own_qk = W[rows, : p.qk].astype(F32)
        gain_grad = (
            jnp.sum(jnp.where(lane < at_gain, tile_qk * own_qk, 0.0), -1, keepdims=True)
            + jnp.sum(tile_v * W[rows, p.qk : p.cols].astype(F32), -1, keepdims=True)
        ) / own_qk[:, at_gain : at_gain + 1]
        rest = jnp.where(lane == at_gain, gain_grad, 0.0)
        G[rows, : p.qk] = jnp.where(lane < at_gain, tile_qk, rest).astype(BF16)

    half = D // LANES // 2
    loop(half, attention_weights)
    loop(1, lambda k: sum_step(PART, k + 1))
    loop(half, lambda i: attention_weights(i + half))
    if p.inline:
        each_peer(n_dp, dp, lambda d: band_send(d, True).start())
        each_peer(n_dp, dp, lambda d: slab_sum_band(d, False).wait_recv())
        band_total = GO[dp, :, core].astype(F32)
        for step in range(1, n_dp):
            band_total = band_total + DO[lax.rem(dp + step, n_dp)].astype(F32)
        ZS[...] = band_total.astype(BF16)
        each_peer(n_z, z, lambda zk: slab_sum(zk, True).start())
    grad_to_group(0)
    loop(n_z - 2, lambda k: sum_step(PART, k + 2))
    if p.inline:
        each_peer(n_dp, dp, lambda d: band_send(d, False).wait_recv())
        total = G[band_rows(dp)].astype(F32)
        for step in range(1, n_dp):
            total = total + GR[lax.rem(dp + step, n_dp)].astype(F32)
        GS[...] = total.astype(BF16)
        each_peer(n_seq, seq, lambda s: piece_send(s, True).start())
        grad_ref[seq] = GS[pl.ds(pl.multiple_of(seq * p.rows, p.rows), p.rows)]
    grad_to_group(1)

    group_sum_result(1, PARTB, gtok_ref)
    out_ref[...] = (STREAM[...] + gtok_ref[...]).astype(BF16)
    sum_result(PART, gtok_ref)
    inputs = tok_ref[...].astype(F32)
    factor = factor_of(inputs)
    m = inputs * factor
    f = gtok_ref[...] * gain_attn
    gtok_ref[...] = BSTREAM[...] + factor * (f - m * jnp.mean(f * m, -1, keepdims=True))

    if p.inline:
        each_peer(n_z, z, lambda zk: slab_sum(zk, False).wait_recv())
        slab_total = ZS[z].astype(F32)
        for step in range(1, n_z):
            slab_total = slab_total + ZO[lax.rem(z + step, n_z)].astype(F32)
        go_ref[...] = slab_total
        each_peer(n_seq, seq, lambda s: piece_send(s, False).wait_recv())
        for q in range(3):
            each_peer(GROUP, rank, lambda r: grad_piece(q, r, False).wait_recv())
    else:
        stay(G, grad_ref)
        stay(GM.at[0, 0, 0], gm_ref)

    gather_drain(TOK)
    share_drain(0, NM)
    share_drain(1, COT)
    group_sum_drain(0, PARTA)
    group_sum_drain(1, PARTB)
    sum_drain(PART)
    each_peer(n_seq, seq, lambda s: attended_copy(s, True).wait_send())
    each_peer(n_seq, seq, lambda s: back_copy(s, True).wait_send())
    if p.inline:
        each_peer(n_z, z, lambda zk: slab_copy(zk, True).wait_send())
        each_peer(n_dp, dp, lambda d: slab_band(d, True).wait_send())
        slab_half(core).wait_send()
        slab_sum_half().wait_send()
        each_peer(n_dp, dp, lambda d: slab_sum_band(d, True).wait_send())
        each_peer(n_z, z, lambda zk: slab_sum(zk, True).wait_send())
        each_peer(n_seq, seq, lambda s: piece_copy(s, True).wait_send())
        each_peer(n_dp, dp, lambda d: band_copy(d, True).wait_send())
        each_peer(n_dp, dp, lambda d: band_send(d, True).wait_send())
        each_peer(n_seq, seq, lambda s: piece_send(s, True).wait_send())
        for q in range(3):
            each_peer(GROUP, rank, lambda r: feed_piece(q, None, r, True).wait_send())
            each_peer(n_zz, zz, lambda g: each_peer(GROUP, rank, lambda r: feed_piece(q, g, r, True).wait_send()))
            each_peer(GROUP, rank, lambda r: grad_piece(q, r, True).wait_send())
            each_peer(n_zz, zz, lambda g: feed_along_z(q, g, True).wait_send())
            each_peer(n_zz, zz, lambda g: grad_along_z(q, g, True).wait_send())

            def left_along_y(h):
                loop(n_zz, lambda g: feed_along_y(q, h, g, True).wait_send())
                loop(n_zz, lambda g: grad_along_y(q, h, g, True).wait_send())

            each_peer(n_y, y, left_along_y)


def run_layer(plan, hidden, tokens, cotangent, *weights):
    p = plan
    n_seq, n_z, n_dp, B, D = p.n_seq, p.n_z, p.n_dp, p.block, p.width
    vmem = pl.BlockSpec(memory_space=pltpu.VMEM)
    grads = (n_seq, p.rows, p.cols) if p.inline else (D, p.cols)
    dma = pltpu.SemaphoreType.DMA

    def rows(width, kind=BF16):
        return pltpu.VMEM((n_seq, B, width), kind)

    def group(width):
        return pltpu.VMEM((GROUP, B, width), BF16)

    n_y, n_zz = p.n_y, p.n_zz
    feed_grads = (GROUP, p.rows, p.wide) if p.inline else (D, p.wide)
    feed_whole = (n_y, 2, n_zz, LANES, p.wide) if p.inline else (1, 1, 1, D, p.wide)
    section = (2, LANES, p.wide) if p.inline else (1, 16, LANES)
    feed_y = (n_y, n_zz) if p.inline else (1, 1)
    band = p.band if p.inline else 16
    n_gr = n_dp if p.inline else 1
    anywhere = pl.BlockSpec(memory_space=pl.ANY)
    whole = (n_dp, n_z, 2, p.rows, p.joined) if p.inline else (1, 1, 1, D, p.joined)
    slabs = (n_z, p.rows, p.joined) if p.inline else (1, 16, LANES)
    bands = (n_dp,) + slabs if p.inline else (1, 1, 16, LANES)
    outs = [((B, D), BF16), ((B, D), F32)]
    packed = []
    if p.inline:
        r = p.rows
        outs += [(grads, BF16), (feed_grads, BF16), ((r, p.joined), F32)]
        packed = [pltpu.VMEM(shape, BF16) for shape in (grads, feed_grads, (r, p.joined))]
        packed += [pltpu.VMEM((n_zz,) + feed_grads, BF16)]
        packed += [pltpu.VMEM(a.shape, a.dtype) for a in (tokens, cotangent) + weights]
        packed += [dma((11,))]
    else:
        outs += [(grads, BF16), (feed_grads, BF16), ((D, p.joined), BF16)]
    return pl.pallas_call(
        functools.partial(layer_kernel, plan),
        out_shape=[jax.ShapeDtypeStruct(shape, kind) for shape, kind in outs],
        in_specs=[anywhere if p.inline else vmem] * 2 + [anywhere] * len(weights),
        out_specs=[vmem, vmem] + [vmem if p.inline else anywhere] * (len(outs) - 2),
        scratch_shapes=packed + [
            rows(D), rows(D), group(D), group(D),
            pltpu.VMEM(whole, BF16), pltpu.VMEM(whole if p.inline else (1, 1, 1, 16, LANES), BF16), pltpu.VMEM(bands, BF16), pltpu.VMEM(bands, BF16),
            pltpu.VMEM(slabs, BF16), pltpu.VMEM(slabs, BF16),
            pltpu.VMEM((B, p.joined), BF16), pltpu.VMEM((B, p.joined), BF16), rows(p.vp),
            pltpu.VMEM((D, p.cols), BF16), pltpu.VMEM(feed_whole, BF16),
            pltpu.VMEM((D, p.cols), BF16), pltpu.VMEM(feed_whole, BF16),
            pltpu.VMEM(feed_y + section, BF16), pltpu.VMEM(feed_y[1:] + section, BF16),
            pltpu.VMEM((n_gr, band, p.cols), BF16), pltpu.VMEM((band, p.cols), BF16),
            rows(p.qk), rows(p.qk), rows(p.vp), rows(p.vp), rows(p.vp, F32), rows(p.vp, F32),
            rows(p.vp), rows(p.qk), rows(p.vp), rows(p.qk, F32), rows(p.vp, F32),
            group(p.fp), group(p.fp), group(p.fp),
            rows(D), group(D), group(D),
            pltpu.VMEM((n_z, B, D), BF16), pltpu.VMEM((n_z + 1, B, D), BF16),
            pltpu.VMEM((2, 4, B, D), BF16), pltpu.VMEM((2, 2, B, D), BF16), pltpu.VMEM((2, B, D), BF16),
            pltpu.VMEM((B, D), F32), pltpu.VMEM((B, D), F32),
            dma((3, n_seq)), dma((n_seq,)), dma((n_z,)), dma((n_z,)), dma((n_z,)), dma((n_z + 1,)),
            dma((n_seq,)), dma((n_seq,)), dma((n_dp,)), dma((n_dp,)),
            dma((n_dp,)), dma((n_dp,)), dma((n_seq,)), dma((n_seq,)), dma((1,)),
            dma((n_z,)), dma((n_z,)), dma((n_dp,)), dma((n_dp,)), dma((2,)), dma((2,)),
            dma((n_z,)), dma((n_z,)), dma((n_dp,)), dma((n_dp,)),
            dma((n_seq,)), dma((n_seq,)), dma((n_seq,)), dma((n_seq,)),
            dma((2, 3, GROUP)), dma((2, GROUP)), dma((2, 4)), dma((2, 4)), dma((2, 2)), dma((2, 2)), dma((2,)), dma((2,)),
            dma((3, n_zz, GROUP)), dma((3, n_zz, GROUP)), dma((3, n_zz)), dma((3, n_zz)), dma((3, n_y, n_zz)), dma((3, n_y, n_zz)),
            dma((3, GROUP)), dma((3, GROUP)), dma((3, n_zz)), dma((3, n_zz)), dma((3, n_y, n_zz)), dma((3, n_y, n_zz)),
        ],
        compiler_params=pltpu.CompilerParams(
            collective_id=0, has_side_effects=True, vmem_limit_bytes=66_000_000
        ),
    )(tokens, cotangent, *weights)


def finish_kernel(plan, *refs):
    p = plan
    ins, outs, held, made = refs[:5], refs[5:16], refs[16:21], refs[21:30]
    in_sem, out_sem = refs[30:]
    reading = [pltpu.make_async_copy(a, b, in_sem.at[i]) for i, (a, b) in enumerate(zip(ins, held))]
    for copy in reading:
        copy.start()
    sources = [held[0], held[1]] + list(made[:3]) + [held[4]] + list(made[3:])
    sources = sources[:11]
    writing = [pltpu.make_async_copy(a, b, out_sem.at[i]) for i, (a, b) in enumerate(zip(sources, outs))]
    g_query, g_key, g_value, g_gate, g_up, g_down, g_attn, g_mlp = made[:8]
    pieces, feed = held[2], held[3]
    for i in (0, 1, 4):
        reading[i].wait()
    for i in (0, 1, 5):
        writing[i].start()
    reading[3].wait()
    for q, to in enumerate((g_gate, g_up, g_down)):
        for r in range(GROUP):
            to[:, r * p.unit : (r + 1) * p.unit] = feed[r, :, q * p.fp : q * p.fp + p.unit].astype(F32)
        writing[6 + q].start()
    g_mlp[...] = jnp.sum(feed[:, :, p.fp + p.unit : p.fp + p.unit + 1].astype(F32), 0).T
    reading[2].wait()
    gain = jnp.zeros((p.rows, 1), F32)
    for c in range(p.n_seq):
        piece = pieces[c].astype(F32)
        g_query[:, c * p.feat : (c + 1) * p.feat] = piece[:, : p.feat]
        g_key[:, c * p.feat : (c + 1) * p.feat] = piece[:, p.feat : 2 * p.feat]
        g_value[:, c * p.value : (c + 1) * p.value] = piece[:, p.qk : p.qk + p.value]
        gain = gain + piece[:, 2 * p.feat : 2 * p.feat + 1]
    g_attn[...] = gain.T
    for i in (2, 3, 4, 9, 10):
        writing[i].start()
    for copy in writing:
        copy.wait()


def finish(plan, hidden, *owned):
    r = plan.rows
    shapes = [(r, HEADS * FEAT_DIM), (r, HEADS * FEAT_DIM), (r, HEADS * HEAD_V)]
    feeds = [(r, hidden)] * 3 + [(1, r)] * 2
    kinds = [(owned[0].shape, BF16), (owned[1].shape, F32)]
    kinds += [(shape, F32) for shape in shapes + [owned[4].shape] + feeds]
    anywhere = pl.BlockSpec(memory_space=pl.ANY)
    return pl.pallas_call(
        functools.partial(finish_kernel, plan),
        out_shape=[jax.ShapeDtypeStruct(shape, kind) for shape, kind in kinds],
        in_specs=[anywhere] * 5,
        out_specs=[anywhere] * 11,
        scratch_shapes=[pltpu.VMEM(a.shape, a.dtype) for a in owned]
        + [pltpu.VMEM(shape, F32) for shape in shapes + feeds + [(8, LANES)]]
        + [pltpu.SemaphoreType.DMA((5,)), pltpu.SemaphoreType.DMA((11,))],
    )(*owned)


def on_device(tokens, w_query, w_key, w_value, w_output, w_gate, w_up, w_down, norm_attn, norm_mlp, cotangent):
    plan = Plan(
        lax.axis_size("dp"), lax.axis_size("seq"), tokens.shape[0], tokens.shape[1], w_gate.shape[1]
    )
    hidden = w_gate.shape[1]
    if plan.inline:
        results = run_layer(
            plan, hidden, tokens, cotangent, w_query, w_key, w_value, w_output.T, w_gate, w_up, w_down.T,
            norm_attn[None], norm_mlp[None],
        )
        results = finish(plan, hidden, *results)
        layer_out, grad_tokens, g_query, g_key, g_value, g_output, g_gate, g_up, g_down, g_attn, g_mlp = results
        return (
            layer_out, grad_tokens, g_query, g_key, g_value, g_output.T, g_gate, g_up, g_down.T, g_attn[0], g_mlp[0]
        )
    axes = ("dp", "seq")
    dp, seq = lax.axis_index("dp"), lax.axis_index("seq")
    rank = 4 * (dp % 2) + seq % 4
    weights = pack_attention(plan, w_query, w_key, w_value, norm_attn, norm_mlp)
    weights = lax.all_to_all(weights, "seq", split_axis=0, concat_axis=0, tiled=True)
    weights = lax.all_gather(weights, "dp").reshape(plan.width, plan.cols)
    feed = lax.all_gather(pack_feed(plan, w_gate, w_up, w_down), axes, axis=1, tiled=True)
    feed = lax.dynamic_index_in_dim(feed, rank, 0, False)
    output_rows = lax.all_gather(pack_output(plan, w_output), axes, axis=0, tiled=True)
    layer_out, grad_tokens, grads, grads_feed, grad_output = run_layer(
        plan, hidden, tokens, cotangent, weights, feed, output_rows
    )
    grads = lax.psum_scatter(grads, "dp", scatter_dimension=0, tiled=True)
    grads = grads.reshape(plan.n_seq, plan.rows, plan.cols)
    grads = lax.all_to_all(grads, "seq", split_axis=0, concat_axis=0, tiled=True)
    spread = jnp.zeros((GROUP, plan.width, plan.wide), BF16)
    spread = lax.dynamic_update_index_in_dim(spread, grads_feed, rank, 0)
    grads_feed = lax.psum_scatter(spread, axes, scatter_dimension=1, tiled=True)
    grad_output = lax.psum_scatter(grad_output, axes, scatter_dimension=0, tiled=True).astype(F32)
    return (layer_out, grad_tokens) + unpack_grads(plan, grads, grads_feed, grad_output)


def solution(mesh):
    rows, cols, vec = P(("dp", "seq"), None), P(None, ("dp", "seq")), P(("dp", "seq"))
    return jax.shard_map(
        on_device,
        mesh=mesh,
        in_specs=(rows, rows, rows, rows, cols, rows, rows, cols, vec, vec, rows),
        out_specs=(rows, rows, rows, rows, rows, cols, rows, rows, cols, vec, vec),
        check_vma=False,
    )
```

```python
import functools

import jax
import jax.numpy as jnp
from jax import lax
from jax.experimental import pallas as pl
from jax.experimental.pallas import tpu as pltpu
from jax.sharding import PartitionSpec as P

HEADS = 16
FEAT_DIM = 16
HEAD_V = 64
EPSILON = 1e-06
LANES = 128
GROUP = 8
MESH = pl.DeviceIdType.MESH
BF16 = jnp.bfloat16
F32 = jnp.float32


def round_up(size, unit):
    return -(-size // unit) * unit


def product(a, b):
    return jnp.dot(a, b, preferred_element_type=F32)


def product_nt(a, b):
    return lax.dot_general(a, b, (((1,), (1,)), ((), ())), preferred_element_type=F32)


def product_tn(a, b):
    return lax.dot_general(a, b, (((0,), (0,)), ((), ())), preferred_element_type=F32)


class Plan:
    def __init__(self, n_dp, n_seq, block, width, hidden):
        self.n_dp, self.n_seq, self.n_z = n_dp, n_seq, n_seq // 2
        self.block, self.width = block, width
        self.heads = HEADS // n_seq
        self.feat = self.heads * FEAT_DIM
        self.value = self.heads * HEAD_V
        self.unit = hidden // GROUP
        self.qk = round_up(2 * self.feat + 2, LANES)
        self.vp = round_up(self.value, LANES)
        self.fp = round_up(self.unit + 1, LANES)
        self.rows = width // (n_dp * n_seq)
        self.band = width // n_dp
        self.cols = self.qk + self.vp
        self.wide = 3 * self.fp
        self.joined = n_seq * self.vp
        self.n_y, self.n_zz = n_dp // 2, self.n_z // 2
        self.inline = 4 * self.rows == LANES and self.vp == self.value


def cut(w, parts):
    return w.reshape(w.shape[0], parts, -1).transpose(1, 0, 2)


def pad(parts, to):
    joined = jnp.concatenate(parts, -1) if len(parts) > 1 else parts[0]
    return jnp.pad(joined, ((0, 0), (0, 0), (0, to - joined.shape[-1])))


def pack_attention(plan, w_query, w_key, w_value, norm_attn, norm_mlp):
    s = plan.n_seq
    gains = jnp.broadcast_to(jnp.stack([norm_attn, norm_mlp], -1), (s, plan.rows, 2))
    return jnp.concatenate(
        [pad([cut(w_query, s), cut(w_key, s), gains], plan.qk), pad([cut(w_value, s)], plan.vp)], -1
    )


def pack_feed(plan, w_gate, w_up, w_down):
    return jnp.concatenate([pad([cut(w, GROUP)], plan.fp) for w in (w_gate, w_up, w_down.T)], -1)


def pack_output(plan, w_output):
    heads = w_output.T.reshape(plan.rows, plan.n_seq, plan.value)
    return jnp.pad(heads, ((0, 0), (0, 0), (0, plan.vp - plan.value))).reshape(plan.rows, plan.joined)


def unpack_grads(plan, owned, owned_feed, owned_output):
    r = plan.rows

    def join(pieces, start, unit):
        return pieces[:, :, start : start + unit].transpose(1, 0, 2).reshape(r, -1).astype(F32)

    at_gain = 2 * plan.feat
    return (
        join(owned, 0, plan.feat),
        join(owned, plan.feat, plan.feat),
        join(owned, plan.qk, plan.value),
        owned_output.reshape(r, plan.n_seq, plan.vp)[:, :, : plan.value].reshape(r, -1).T,
        join(owned_feed, 0, plan.unit),
        join(owned_feed, plan.fp, plan.unit),
        join(owned_feed, 2 * plan.fp, plan.unit).T,
        jnp.sum(owned[:, :, at_gain].astype(F32), 0),
        jnp.sum(owned_feed[:, :, plan.fp + plan.unit].astype(F32), 0),
    )


def pack_in_kernel(p, raw, w_ref, wm_ref, wo_ref):
    wq, wk, wv, wo, wg, wu, wd, gain_attn, gain_mlp = raw
    columns = [gain_attn[...].astype(F32).T.astype(BF16), gain_mlp[...].astype(F32).T.astype(BF16)]
    spare = jnp.zeros((p.rows, p.qk - 2 * p.feat - 2), BF16)
    for c in range(p.n_seq):
        here = slice(c * p.feat, (c + 1) * p.feat)
        w_ref[c, :, : p.qk] = jnp.concatenate([wq[:, here], wk[:, here]] + columns + [spare], -1)
        w_ref[c, :, p.qk : p.qk + p.value] = wv[:, c * p.value : (c + 1) * p.value]
    wo_ref[...] = wo[...]
    blank = jnp.zeros((p.rows, p.fp - p.unit), BF16)
    for q, whole in enumerate((wg, wu, wd)):
        for r in range(GROUP):
            piece = whole[:, r * p.unit : (r + 1) * p.unit]
            wm_ref[r, :, q * p.fp : (q + 1) * p.fp] = jnp.concatenate([piece, blank], -1)


def layer_kernel(plan, *refs):
    p = plan
    (
        tok_ref, cot_ref, *rest
    ) = refs
    if p.inline:
        sources, rest = refs[:11], refs[11:]
        out_ref, gtok_ref, grad_ref, gm_ref, go_ref, *rest = rest
        w_ref, wm_ref, wo_ref, WZ, *rest = rest
        held, in_sem, rest = rest[:11], rest[11], rest[12:]
        tok_ref, cot_ref = held[:2]
    else:
        w_ref, wm_ref, wo_ref, out_ref, gtok_ref, grad_ref, gm_ref, go_ref, *rest = rest
        WZ = None
    (
        TOK, NA, COT, NM, WO, GO, SO, DO, ZS, ZO, AO, BAT, BATT,
        W, WM, G, GM, GY, GZ, GR, GS,
        Q, K, V, ATT, ATTF, DEN, BNUM, DQK, DV, DKF, DVF,
        H, BG, BU,
        PART, PARTA, PARTB, SIB, CH, HALF, XR, ZR, STREAM, BSTREAM,
        ag_send, ag_recv, sib_send, sib_recv, ch_send, ch_recv,
        w_send, w_recv, wd_send, wd_recv,
        g_send, g_recv, gz_send, gz_recv, local_sem,
        wo_send, wo_recv, wod_send, wod_recv, sl_send, sl_recv,
        go_send, go_recv, gd_send, gd_recv, at_send, at_recv, bt_send, bt_recv,
        sh_send, sh_recv, ha_send, ha_recv, xr_send, xr_recv, zr_send, zr_recv,
        wp_send, wp_recv, wz_send, wz_recv, wy_send, wy_recv,
        gp_send, gp_recv, gw_send, gw_recv, gy_send, gy_recv,
    ) = rest
    if not p.inline:
        GO = WO
    dp, seq = lax.axis_index("dp"), lax.axis_index("seq")
    n_seq, n_z, n_dp, B, D = p.n_seq, p.n_z, p.n_dp, p.block, p.width
    z, core = seq // 2, seq % 2
    sibling = (dp, seq + 1 - 2 * core)
    above, below = (dp, seq + 2), (dp, seq - 2)
    is_top, is_bottom = z == n_z - 1, z == 0
    n_y, n_zz = p.n_y, p.n_zz
    x, y, zl, zz = dp % 2, dp // 2, z % 2, z // 2
    rank = 4 * x + 2 * zl + core

    def at(r):
        return (2 * y + r // 4, 4 * zz + r % 4)

    x_peer, z_peer = (dp + 1 - 2 * x, seq), (dp, seq + 2 - 4 * zl)

    def remote(src, dst, send, recv, device):
        return pltpu.make_async_remote_copy(
            src_ref=src, dst_ref=dst, send_sem=send, recv_sem=recv,
            device_id=device, device_id_type=MESH,
        )

    def each_peer(count, mine, body):
        def one(i, carry):
            @pl.when(i != mine)
            def _():
                body(i)

            return carry

        lax.fori_loop(0, count, one, 0)

    def loop(count, body):
        def one(i, carry):
            body(i)
            return carry

        lax.fori_loop(0, count, one, 0)

    if p.inline:
        reading = [
            pltpu.make_async_copy(src, dst, in_sem.at[i]) for i, (src, dst) in enumerate(zip(sources, held))
        ]
        for copy in reading:
            copy.start()

    barrier = pltpu.get_barrier_semaphore()
    each_peer(n_seq, seq, lambda i: pl.semaphore_signal(barrier, inc=1, device_id=(dp, i), device_id_type=MESH))
    each_peer(n_dp, dp, lambda i: pl.semaphore_signal(barrier, inc=1, device_id=(i, seq), device_id_type=MESH))
    for other in (4 - 4 * x + 2 * zl + 1 - core, 4 - 4 * x + 2 - 2 * zl + core, 4 - 4 * x + 2 - 2 * zl + 1 - core):
        pl.semaphore_signal(barrier, inc=1, device_id=at(other), device_id_type=MESH)
    if p.inline:
        for copy in reading:
            copy.wait()
        pack_in_kernel(p, held[2:], w_ref, wm_ref, wo_ref)
    pl.semaphore_wait(barrier, n_seq - 1 + n_dp - 1 + 3)

    near = jnp.minimum(z, n_z - 1 - z)
    far_side = jnp.where(z < n_z - 1 - z, 1, -1)

    def order(k):
        step = (k + 1) // 2
        alternate = jnp.where(k % 2 == 1, -step, step)
        return z + jnp.where(k <= 2 * near, alternate, far_side * (k - near))

    def piece_rows(d, s):
        return pl.ds(pl.multiple_of((d * n_seq + s) * p.rows, p.rows), p.rows)

    def band_rows(d):
        return pl.ds(pl.multiple_of(d * p.band, p.band), p.band)

    def piece_copy(s, mine):
        src_of = seq if mine else s
        return remote(w_ref.at[s], W.at[piece_rows(dp, src_of)], w_send.at[s], w_recv.at[src_of], (dp, s))

    def band_copy(d, mine):
        src_of = dp if mine else d
        return remote(
            W.at[band_rows(src_of)], W.at[band_rows(src_of)], wd_send.at[d], wd_recv.at[src_of], (d, seq)
        )

    def third(q):
        return pl.ds(q * p.fp, p.fp)

    def feed_along_z(q, g, mine):
        src_of = zz if mine else g
        return remote(
            wm_ref.at[:, :, third(q)], WZ.at[src_of, :, :, third(q)],
            wz_send.at[q, g], wz_recv.at[q, src_of], (dp, 4 * g + 2 * zl + core),
        )

    def feed_source(q, g, r):
        return wm_ref.at[r, :, third(q)] if g is None else WZ.at[g, r, :, third(q)]

    def feed_piece(q, g, r, mine):
        src_of = rank if mine else r
        section = zz if g is None else g
        rows = pl.ds(pl.multiple_of((src_of % 4) * p.rows, p.rows), p.rows)
        return remote(
            feed_source(q, g, r), WM.at[y, src_of // 4, section, rows, third(q)],
            wp_send.at[q, section, r], wp_recv.at[q, section, src_of], at(r),
        )

    def feed_along_y(q, h, g, mine):
        src_of = y if mine else h
        section = WM.at[src_of, :, g, :, third(q)]
        return remote(section, section, wy_send.at[q, h, g], wy_recv.at[q, src_of, g], (2 * h + x, seq))

    def feed_to_z(q):
        if p.inline:
            each_peer(n_zz, zz, lambda g: feed_along_z(q, g, True).start())

    def feed_to_group(q, g):
        each_peer(GROUP, rank, lambda r: feed_piece(q, g, r, True).start())
        rows = pl.ds(pl.multiple_of((rank % 4) * p.rows, p.rows), p.rows)
        WM[y, x, zz if g is None else g, rows, third(q)] = feed_source(q, g, rank)[...]

    def feed_on_to_group(q):
        def one(g):
            feed_along_z(q, g, False).wait_recv()
            feed_to_group(q, g)

        if p.inline:
            each_peer(n_zz, zz, one)

    def feed_section_to_y(q, g):
        each_peer(GROUP, rank, lambda r: feed_piece(q, g, r, False).wait_recv())
        each_peer(n_y, y, lambda h: feed_along_y(q, h, zz if g is None else g, True).start())

    def feed_on_to_y(q):
        if p.inline:
            each_peer(n_zz, zz, lambda g: feed_section_to_y(q, g))

    def feed_arrived(q):
        if p.inline:
            each_peer(n_y, y, lambda h: loop(n_zz, lambda g: feed_along_y(q, h, g, False).wait_recv()))

    def grad_along_y(q, h, g, mine):
        src_of = y if mine else h
        return remote(
            GM.at[h, :, g, :, third(q)], GY.at[src_of, g, :, :, third(q)],
            gy_send.at[q, h, g], gy_recv.at[q, src_of, g], (2 * h + x, seq),
        )

    def grad_along_z(q, g, mine):
        src_of = zz if mine else g
        return remote(
            GM.at[y, :, g, :, third(q)], GZ.at[src_of, :, :, third(q)],
            gw_send.at[q, g], gw_recv.at[q, src_of], (dp, 4 * g + 2 * zl + core),
        )

    def grad_piece(q, r, mine):
        src_of = rank if mine else r
        rows = pl.ds(pl.multiple_of((r % 4) * p.rows, p.rows), p.rows)
        return remote(
            GM.at[y, r // 4, zz, rows, third(q)], gm_ref.at[src_of, :, third(q)],
            gp_send.at[q, r], gp_recv.at[q, src_of], at(r),
        )

    def grad_to_y(q):
        if p.inline:
            for step in range(n_zz):
                g = lax.rem(zz + 1 + step, n_zz)
                each_peer(n_y, y, lambda h: grad_along_y(q, h, g, True).start())

    def grad_to_z(q):
        if not p.inline:
            return
        for step in range(n_zz):
            g = lax.rem(zz + 1 + step, n_zz)
            total = GM[y, :, g, :, third(q)].astype(F32)
            for other in range(1, n_y):
                h = lax.rem(y + other, n_y)
                grad_along_y(q, h, g, False).wait_recv()
                total = total + GY[h, g, :, :, third(q)].astype(F32)
            GM[y, :, g, :, third(q)] = total.astype(BF16)
            if step < n_zz - 1:
                grad_along_z(q, g, True).start()

    def grad_to_group(q):
        if not p.inline:
            return
        total = GM[y, :, zz, :, third(q)].astype(F32)
        for step in range(1, n_zz):
            g = lax.rem(zz + step, n_zz)
            grad_along_z(q, g, False).wait_recv()
            total = total + GZ[g, :, :, third(q)].astype(F32)
        GM[y, :, zz, :, third(q)] = total.astype(BF16)
        each_peer(GROUP, rank, lambda r: grad_piece(q, r, True).start())
        rows = pl.ds(pl.multiple_of((rank % 4) * p.rows, p.rows), p.rows)
        gm_ref[rank, :, third(q)] = GM[y, x, zz, rows, third(q)]

    def spot(w):
        return 4 * jnp.where(w >= 2, 1 - x, x) + 2 * jnp.where(w % 2 == 1, 1 - zl, zl)

    def share_copy(a, buf, b, way, device):
        return remote(buf.at[b], buf.at[b], sh_send.at[a, way, b], sh_recv.at[a, b], device)

    def share_step(a, buf, w, on_block):
        def one(side):
            take = jnp.where(side == 0, w < 4, w >= 1)

            @pl.when(take)
            def _():
                b = spot(w - side) + jnp.where(side == 0, core, 1 - core)

                @pl.when(b != rank)
                def _():
                    share_copy(a, buf, b, 2, sibling).wait_recv()

                @pl.when(side == 0)
                def _():
                    @pl.when(w == 0)
                    def _():
                        share_copy(a, buf, b, 0, z_peer).start()

                    @pl.when(w <= 1)
                    def _():
                        share_copy(a, buf, b, 1, x_peer).start()

                    share_copy(a, buf, b, 2, sibling).start()

                if on_block is not None:
                    on_block(b)

        loop(2, one)

    def share_drain(a, buf):
        def one(w):
            b = spot(w) + core

            @pl.when(w == 0)
            def _():
                share_copy(a, buf, b, 0, z_peer).wait_send()

            @pl.when(w <= 1)
            def _():
                share_copy(a, buf, b, 1, x_peer).wait_send()

            share_copy(a, buf, b, 2, sibling).wait_send()

        loop(4, one)

    def half_copy(i, part, w):
        return remote(part.at[spot(w) + 1 - core], HALF.at[i, w], ha_send.at[i, w], ha_recv.at[i, w], sibling)

    def x_copy(i, part, w):
        return remote(part.at[spot(w) + core], XR.at[i, w - 2], xr_send.at[i, w - 2], xr_recv.at[i, w - 2], x_peer)

    def z_copy(i, part):
        return remote(part.at[spot(1) + core], ZR.at[i], zr_send.at[i], zr_recv.at[i], z_peer)

    def group_sum_step(i, part, w):
        b = spot(w) + core
        half_copy(i, part, w).wait_recv()
        total = part[b].astype(F32) + HALF[i, w].astype(F32)
        if w == 1:
            x_copy(i, part, 3).wait_recv()
            total = total + XR[i, 1].astype(F32)
        part[b] = total.astype(BF16)
        (z_copy(i, part) if w == 1 else x_copy(i, part, w)).start()

    def group_sum_result(i, part, total):
        half_copy(i, part, 0).wait_recv()
        x_copy(i, part, 2).wait_recv()
        z_copy(i, part).wait_recv()
        total[...] = (
            part[rank].astype(F32) + HALF[i, 0].astype(F32) + XR[i, 0].astype(F32) + ZR[i].astype(F32)
        )

    def group_sum_drain(i, part):
        loop(4, lambda w: half_copy(i, part, w).wait_send())
        x_copy(i, part, 2).wait_send()
        x_copy(i, part, 3).wait_send()
        z_copy(i, part).wait_send()

    def gather_copy(buf, j, way, device):
        return remote(buf.at[j], buf.at[j], ag_send.at[way, j], ag_recv.at[j], device)

    def gather_step(buf, k, on_block):
        def one(side):
            take = jnp.where(side == 0, k < n_z, k >= 1)

            @pl.when(take)
            def _():
                zk = order(k - side)
                j = 2 * zk + jnp.where(side == 0, core, 1 - core)

                @pl.when(j != seq)
                def _():
                    gather_copy(buf, j, 0, sibling).wait_recv()

                @pl.when(side == 0)
                def _():
                    @pl.when(jnp.logical_and(zk <= z, jnp.logical_not(is_top)))
                    def _():
                        gather_copy(buf, j, 0, above).start()

                    @pl.when(jnp.logical_and(zk >= z, jnp.logical_not(is_bottom)))
                    def _():
                        gather_copy(buf, j, 1, below).start()

                    gather_copy(buf, j, 2, sibling).start()

                if on_block is not None:
                    on_block(j)

        loop(2, one)

    def gather_drain(buf):
        def one(zk):
            j = 2 * zk + core

            @pl.when(jnp.logical_and(zk <= z, jnp.logical_not(is_top)))
            def _():
                gather_copy(buf, j, 0, above).wait_send()

            @pl.when(jnp.logical_and(zk >= z, jnp.logical_not(is_bottom)))
            def _():
                gather_copy(buf, j, 1, below).wait_send()

            gather_copy(buf, j, 2, sibling).wait_send()

        loop(n_z, one)

    def sibling_copy(part, zk):
        return remote(
            part.at[2 * zk + 1 - core], SIB.at[zk], sib_send.at[zk], sib_recv.at[zk], sibling
        )

    def chain_copy(part, zk, up):
        slot = zk if up else jnp.where(zk == z - 1, n_z, zk)
        return remote(
            part.at[2 * zk + core], CH.at[slot], ch_send.at[zk], ch_recv.at[slot],
            above if up else below,
        )

    def chain_wait(part, slot):
        remote(part.at[0], CH.at[slot], ch_send.at[0], ch_recv.at[slot], sibling).wait_recv()

    def far(k):
        return order(n_z - 1 - k)

    def sum_step(part, k):
        zk = far(k)
        j = 2 * zk + core
        remote(part.at[0], SIB.at[zk], sib_send.at[zk], sib_recv.at[zk], sibling).wait_recv()

        @pl.when(zk != z)
        def _():
            first = jnp.where(zk > z, is_bottom, is_top)

            @pl.when(first)
            def _():
                part[j] = (part[j].astype(F32) + SIB[zk].astype(F32)).astype(BF16)

            @pl.when(jnp.logical_not(first))
            def _():
                chain_wait(part, zk)
                part[j] = (
                    part[j].astype(F32) + SIB[zk].astype(F32) + CH[zk].astype(F32)
                ).astype(BF16)

            @pl.when(zk > z)
            def _():
                chain_copy(part, zk, True).start()

            @pl.when(zk < z)
            def _():
                chain_copy(part, zk, False).start()

    def sum_result(part, total):
        total[...] = part[seq].astype(F32) + SIB[z].astype(F32)

        @pl.when(jnp.logical_not(is_bottom))
        def _():
            chain_wait(part, z)
            total[...] += CH[z].astype(F32)

        @pl.when(jnp.logical_not(is_top))
        def _():
            chain_wait(part, n_z)
            total[...] += CH[n_z].astype(F32)

    def sum_drain(part):
        def one(zk):
            sibling_copy(part, zk).wait_send()

            @pl.when(zk > z)
            def _():
                chain_copy(part, zk, True).wait_send()

            @pl.when(zk < z)
            def _():
                chain_copy(part, zk, False).wait_send()

        loop(n_z, one)

    def slab_copy(zk, mine):
        src_of = z if mine else zk
        return remote(
            wo_ref, WO.at[dp, src_of, core], wo_send.at[zk], wo_recv.at[src_of], (dp, 2 * zk + core)
        )

    def slab_band(d, mine):
        src_of = dp if mine else d
        return remote(
            WO.at[src_of, :, core], WO.at[src_of, :, core], wod_send.at[d], wod_recv.at[src_of], (d, seq)
        )

    def slab_half(which):
        return remote(WO.at[:, :, which], WO.at[:, :, which], sl_send.at[0], sl_recv.at[0], sibling)

    def slab_sum_half():
        return remote(GO.at[:, :, 1 - core], SO, sl_send.at[1], sl_recv.at[1], sibling)

    def slab_sum_band(d, mine):
        src_of = dp if mine else d
        return remote(GO.at[d, :, core], DO.at[src_of], gd_send.at[d], gd_recv.at[src_of], (d, seq))

    def slab_sum(zk, mine):
        src_of = z if mine else zk
        return remote(ZS.at[zk], ZO.at[src_of], go_send.at[zk], go_recv.at[src_of], (dp, 2 * zk + core))

    def lanes_of(s):
        return pl.ds(pl.multiple_of(s * p.vp, p.vp), p.vp)

    def attended_copy(s, mine):
        src_of = seq if mine else s
        return remote(ATT.at[s], AO.at[:, lanes_of(src_of)], at_send.at[s], at_recv.at[src_of], (dp, s))

    def back_copy(s, mine):
        src_of = seq if mine else s
        return remote(BAT.at[:, lanes_of(s)], BATT.at[src_of], bt_send.at[s], bt_recv.at[src_of], (dp, s))

    def stay(src, dst):
        own = pltpu.make_async_copy(src, dst, local_sem.at[0])
        own.start()
        own.wait()

    if p.inline:
        each_peer(n_seq, seq, lambda s: piece_copy(s, True).start())
        TOK[seq] = tok_ref[...]
        gather_step(TOK, 0, None)
        feed_to_group(0, None)
        feed_to_group(1, None)
        feed_to_group(2, None)
        feed_to_z(0)
        W[piece_rows(dp, seq)] = w_ref[seq]
        WO[dp, z, core] = wo_ref[...]
        COT[rank] = cot_ref[...]
        each_peer(n_seq, seq, lambda s: piece_copy(s, False).wait_recv())
        each_peer(n_dp, dp, lambda d: band_copy(d, True).start())
        gather_step(TOK, 1, None)
        feed_to_z(1)
        each_peer(n_z, z, lambda zk: slab_copy(zk, True).start())
        feed_section_to_y(0, None)
        feed_section_to_y(1, None)
        feed_section_to_y(2, None)
        gather_step(TOK, 2, None)
        feed_to_z(2)
        each_peer(n_dp, dp, lambda d: band_copy(d, False).wait_recv())
    else:
        TOK[seq] = tok_ref[...]
        gather_step(TOK, 0, None)
        stay(w_ref, W)
        stay(wm_ref, WM.at[0, 0, 0])
        stay(wo_ref, WO.at[0, 0, 0])
        COT[rank] = cot_ref[...]
        gather_step(TOK, 1, None)
        gather_step(TOK, 2, None)
    loop(n_z - 4, lambda k: gather_step(TOK, k + 3, None))

    lane = lax.broadcasted_iota(jnp.int32, (1, p.qk), 1)
    vlane = lax.broadcasted_iota(jnp.int32, (1, p.vp), 1)
    feat_masks = [
        jnp.logical_and(lane >= h * FEAT_DIM, lane < (h + 1) * FEAT_DIM).astype(BF16) for h in range(p.heads)
    ]
    value_masks = [
        jnp.logical_and(vlane >= h * HEAD_V, vlane < (h + 1) * HEAD_V).astype(BF16) for h in range(p.heads)
    ]
    spare = (vlane >= p.value).astype(F32)
    row = lax.broadcasted_iota(jnp.int32, (p.qk, p.qk), 0)
    col = lax.broadcasted_iota(jnp.int32, (p.qk, p.qk), 1)
    shift = jnp.logical_and(row == col + p.feat, col < p.feat).astype(F32).astype(BF16)
    at_gain = 2 * p.feat
    pick = lax.broadcasted_iota(jnp.int32, (16, p.qk), 0) + at_gain == lax.broadcasted_iota(
        jnp.int32, (16, p.qk), 1
    )
    gain_rows = product_nt(pick.astype(F32).astype(BF16), W[:, : p.qk])
    gain_attn, gain_mlp = gain_rows[0:1], gain_rows[1:2]
    scale = FEAT_DIM ** -0.5
    one_lane = (lane == p.qk - 1).astype(F32)
    C = 2 * B
    below_diag = lax.broadcasted_iota(jnp.int32, (C, C), 0) >= lax.broadcasted_iota(jnp.int32, (C, C), 1)

    def factor_of(x):
        return lax.rsqrt(jnp.mean(x * x, -1, keepdims=True) + EPSILON)

    def project(j):
        x = TOK[j].astype(F32)
        normed = (x * factor_of(x) * gain_attn).astype(BF16)
        NA[j] = normed
        qk = product(normed, W[:, : p.qk]).astype(BF16)
        Q[j] = (qk.astype(F32) * scale).astype(BF16)
        K[j] = (product(qk, shift) + one_lane).astype(BF16)
        V[j] = product(normed, W[:, p.qk : p.cols]).astype(BF16)

    loop(n_z - 1, lambda k: project(2 * order(k) + core))
    loop(n_z - 2, lambda k: project(2 * order(k) + 1 - core))
    if p.inline:
        each_peer(n_z, z, lambda zk: slab_copy(zk, False).wait_recv())
        each_peer(n_dp, dp, lambda d: slab_band(d, True).start())
    feed_on_to_group(0)
    gather_step(TOK, n_z - 1, project)
    share_step(1, COT, 0, None)
    feed_on_to_y(0)
    feed_on_to_group(1)
    gather_step(TOK, n_z, project)

    def chip_rows(buf, i):
        return buf[pl.ds(2 * i, 2)].reshape(C, buf.shape[-1])

    def store_rows(buf, i, value):
        buf[pl.ds(2 * i, 2)] = value.reshape(2, B, value.shape[-1]).astype(buf.dtype)

    def one_plus_t(query, key):
        return product_nt(query, key)

    def query_of(queries, h):
        return queries * feat_masks[h] + one_lane.astype(BF16)

    def attend(i):
        queries = chip_rows(Q, i)

        def inner(j, acc, diagonal):
            keys, values = chip_rows(K, j), chip_rows(V, j)
            for h in range(p.heads):
                u = product_nt(query_of(queries, h), keys)
                s = 0.5 * u * u + 0.5
                if diagonal:
                    s = jnp.where(below_diag, s, 0.0)
                ones = jnp.broadcast_to(value_masks[h], (C, p.vp))
                acc = acc + product(s.astype(BF16), jnp.concatenate([values * value_masks[h], ones], -1))
            return acc

        acc = lax.fori_loop(0, i, lambda j, acc: inner(j, acc, False), jnp.zeros((C, 2 * p.vp), F32))
        acc = inner(i, acc, True)
        den = acc[:, p.vp :] + spare
        att = acc[:, : p.vp] / den
        store_rows(DEN, i, den)
        store_rows(ATTF, i, att)
        store_rows(ATT, i, att)

        def give(side):
            @pl.when(2 * i + side != seq)
            def _():
                attended_copy(2 * i + side, True).start()

        loop(2, give)

    loop(n_z, lambda k: attend(far(k)))
    AO[:, lanes_of(seq)] = ATT[seq]
    share_step(1, COT, 1, None)
    feed_on_to_y(1)
    feed_on_to_group(2)
    if p.inline:
        each_peer(n_dp, dp, lambda d: slab_band(d, False).wait_recv())
        slab_half(core).start()
    each_peer(n_seq, seq, lambda s: attended_copy(s, False).wait_recv())
    if p.inline:
        slab_half(1 - core).wait_recv()
    STREAM[...] = tok_ref[...].astype(F32) + product_nt(AO[...], WO[...].reshape(D, p.joined))

    stream = STREAM[...]
    NM[rank] = (stream * factor_of(stream) * gain_mlp).astype(BF16)
    share_step(0, NM, 0, None)
    feed_on_to_y(2)
    loop(3, lambda w: share_step(1, COT, w + 2, None))
    for q in range(3):
        feed_arrived(q)

    def weight(q):
        return WM[:, :, :, :, third(q)].reshape(D, p.fp)

    def feed(j):
        normed = NM[j]
        gate = product(normed, weight(0))
        up = product(normed, weight(1))
        back = product(COT[j], weight(2))
        sig = jax.nn.sigmoid(gate)
        act = gate * sig
        H[j] = (act * up).astype(BF16)
        BG[j] = (back * up * sig * (1.0 + gate * (1.0 - sig))).astype(BF16)
        BU[j] = (back * act).astype(BF16)
        PARTA[j] = (product_nt(BG[j], weight(0)) + product_nt(BU[j], weight(1))).astype(BF16)
        PARTB[j] = product_nt(H[j], weight(2)).astype(BF16)

        @pl.when(j % 2 != core)
        def _():
            w = 2 * jnp.where(j // 4 != x, 1, 0) + jnp.where((j // 2) % 2 != zl, 1, 0)
            half_copy(0, PARTA, w).start()
            half_copy(1, PARTB, w).start()

    feed(rank)
    loop(4, lambda w: share_step(0, NM, w + 1, feed))

    def all_rows(buf, d0, size):
        return buf[:, :, pl.ds(d0, size)].reshape(buf.shape[0] * B, size)

    def chunk_of(buf, i):
        if p.inline:
            return buf.at[i // (2 * n_zz), (i // n_zz) % 2, i % n_zz]
        return buf.at[0, 0, 0, pl.ds(pl.multiple_of(i * LANES, LANES), LANES)]

    feed_lane = lax.broadcasted_iota(jnp.int32, (1, p.fp), 1)

    def back_of_weights(q, left, right):
        def one(i):
            d0 = pl.multiple_of(i * LANES, LANES)
            tile = product_tn(all_rows(left, d0, LANES), right[...].reshape(GROUP * B, p.fp))
            grads, own = chunk_of(GM, i), chunk_of(WM, i)
            if q == 1:
                both = tile * own[:, third(1)].astype(F32) + grads[:, third(0)].astype(F32) * own[
                    :, third(0)
                ].astype(F32)
                gain = W[pl.ds(d0, LANES), : p.qk].astype(F32)[:, at_gain + 1 : at_gain + 2]
                tile = jnp.where(feed_lane == p.unit, jnp.sum(both, -1, keepdims=True) / gain, tile)
            grads[:, third(q)] = tile.astype(BF16)

        loop(D // LANES, one)
        grad_to_y(q)

    group_sum_step(0, PARTA, 3)
    group_sum_step(0, PARTA, 2)
    back_of_weights(2, COT, H)
    group_sum_step(0, PARTA, 1)
    back_of_weights(0, NM, BG)
    grad_to_z(2)
    back_of_weights(1, NM, BU)
    group_sum_result(0, PARTA, BSTREAM)
    back_normed = BSTREAM[...]
    stream = STREAM[...]
    factor = factor_of(stream)
    n = stream * factor
    e = back_normed * gain_mlp
    BSTREAM[...] = cot_ref[...].astype(F32) + factor * (e - n * jnp.mean(e * n, -1, keepdims=True))
    BM = BSTREAM[...].astype(BF16)
    BAT[...] = product(BM, WO[...].reshape(D, p.joined)).astype(BF16)
    each_peer(n_seq, seq, lambda s: back_copy(s, True).start())
    BATT[seq] = BAT[:, lanes_of(seq)]
    GO[...] = product_tn(BM, AO[...]).astype(BF16).reshape(GO.shape)

    if p.inline:
        slab_sum_half().start()
    else:
        stay(GO.at[0, 0, 0], go_ref)

    def band_send(d, mine):
        src_of = dp if mine else d
        return remote(G.at[band_rows(d)], GR.at[src_of], g_send.at[d], g_recv.at[src_of], (d, seq))

    def piece_send(s, mine):
        src_of = seq if mine else s
        rows = pl.ds(pl.multiple_of(s * p.rows, p.rows), p.rows)
        return remote(GS.at[rows], grad_ref.at[src_of], gz_send.at[s], gz_recv.at[src_of], (dp, s))

    def back_heads(j):
        back = BATT[j].astype(F32)
        den = DEN[j]
        BNUM[j] = (back / den).astype(BF16)
        prod = back * ATTF[j]
        out = jnp.zeros((B, p.vp), F32)
        for h in range(p.heads):
            total = jnp.sum(prod * value_masks[h].astype(F32), -1, keepdims=True)
            out = jnp.where(value_masks[h] > 0, -total, out)
        ATTF[j] = out / den
        DKF[j] = jnp.zeros((B, p.qk), F32)
        DVF[j] = jnp.zeros((B, p.vp), F32)

    group_sum_step(1, PARTB, 3)
    group_sum_step(1, PARTB, 2)
    grad_to_z(0)
    each_peer(n_seq, seq, lambda s: back_copy(s, False).wait_recv())
    loop(n_seq, back_heads)

    def attend_back(i):
        queries, numer, denom = chip_rows(Q, i), chip_rows(BNUM, i), chip_rows(ATTF, i)
        high = denom.astype(BF16)
        low = (denom - high.astype(F32)).astype(BF16)

        def inner(j, dq, diagonal):
            keys, values = chip_rows(K, j), chip_rows(V, j)
            dk, dv = chip_rows(DKF, j), chip_rows(DVF, j)
            one = (vlane < 2).astype(BF16)
            wide_values = jnp.concatenate([values, jnp.broadcast_to(one, (C, p.vp))], -1)
            for h in range(p.heads):
                qh, bh = query_of(queries, h), numer * value_masks[h]
                first = h * HEAD_V
                extra = jnp.where(
                    vlane == 0, high[:, first : first + 1].astype(F32),
                    jnp.where(vlane == 1, low[:, first : first + 1].astype(F32), 0.0),
                ).astype(BF16)
                u = product_nt(qh, keys)
                ds = product_nt(jnp.concatenate([bh, extra], -1), wide_values)
                s, dt = 0.5 * u * u + 0.5, ds * u
                if diagonal:
                    s, dt = jnp.where(below_diag, s, 0.0), jnp.where(below_diag, dt, 0.0)
                dt = dt.astype(BF16)
                dq = dq + product(dt, keys * feat_masks[h])
                dk = dk + product_tn(dt, queries * feat_masks[h])
                dv = dv + product_tn(s.astype(BF16), bh)
            store_rows(DKF, j, dk)
            store_rows(DVF, j, dv)
            return dq

        dq = lax.fori_loop(0, i, lambda j, dq: inner(j, dq, False), jnp.zeros((C, p.qk), F32))
        dq = inner(i, dq, True)
        store_rows(DQK, i, dq * scale)

    loop(n_z // 2, attend_back)
    if p.inline:
        slab_sum_half().wait_recv()
        GO[:, :, core] = (GO[:, :, core].astype(F32) + SO[...].astype(F32)).astype(BF16)
        each_peer(n_dp, dp, lambda d: slab_sum_band(d, True).start())
    group_sum_step(1, PARTB, 1)
    grad_to_z(1)
    loop(n_z - n_z // 2, lambda k: attend_back(k + n_z // 2))

    def back_input(j):
        dk = DKF[j].astype(BF16)
        qk = (DQK[j].astype(F32) + product_nt(dk, shift)).astype(BF16)
        DQK[j] = qk
        DV[j] = DVF[j].astype(BF16)
        PART[j] = (
            product_nt(qk, W[:, : p.qk]) + product_nt(DV[j], W[:, p.qk : p.cols])
        ).astype(BF16)

    def fourth_sum(k):
        loop(2, lambda side: back_input(2 * far(k) + side))
        sibling_copy(PART, far(k)).start()

    loop(n_z, fourth_sum)
    loop(1, lambda k: sum_step(PART, k))
    grad_to_group(2)

    def attention_weights(i):
        d0 = pl.multiple_of(i * LANES, LANES)
        rows = pl.ds(d0, LANES)
        normed = all_rows(NA, d0, LANES)
        tile_qk = product_tn(normed, DQK[...].reshape(n_seq * B, p.qk))
        tile_v = product_tn(normed, DV[...].reshape(n_seq * B, p.vp))
        G[rows, p.qk : p.cols] = tile_v.astype(BF16)
        own_qk = W[rows, : p.qk].astype(F32)
        gain_grad = (
            jnp.sum(jnp.where(lane < at_gain, tile_qk * own_qk, 0.0), -1, keepdims=True)
            + jnp.sum(tile_v * W[rows, p.qk : p.cols].astype(F32), -1, keepdims=True)
        ) / own_qk[:, at_gain : at_gain + 1]
        rest = jnp.where(lane == at_gain, gain_grad, 0.0)
        G[rows, : p.qk] = jnp.where(lane < at_gain, tile_qk, rest).astype(BF16)

    half = D // LANES // 2
    loop(half, attention_weights)
    loop(1, lambda k: sum_step(PART, k + 1))
    loop(half, lambda i: attention_weights(i + half))
    if p.inline:
        each_peer(n_dp, dp, lambda d: band_send(d, True).start())
        each_peer(n_dp, dp, lambda d: slab_sum_band(d, False).wait_recv())
        band_total = GO[dp, :, core].astype(F32)
        for step in range(1, n_dp):
            band_total = band_total + DO[lax.rem(dp + step, n_dp)].astype(F32)
        ZS[...] = band_total.astype(BF16)
        each_peer(n_z, z, lambda zk: slab_sum(zk, True).start())
    grad_to_group(0)
    loop(n_z - 2, lambda k: sum_step(PART, k + 2))
    if p.inline:
        each_peer(n_dp, dp, lambda d: band_send(d, False).wait_recv())
        total = G[band_rows(dp)].astype(F32)
        for step in range(1, n_dp):
            total = total + GR[lax.rem(dp + step, n_dp)].astype(F32)
        GS[...] = total.astype(BF16)
        each_peer(n_seq, seq, lambda s: piece_send(s, True).start())
        grad_ref[seq] = GS[pl.ds(pl.multiple_of(seq * p.rows, p.rows), p.rows)]
    grad_to_group(1)

    group_sum_result(1, PARTB, gtok_ref)
    out_ref[...] = (STREAM[...] + gtok_ref[...]).astype(BF16)
    sum_result(PART, gtok_ref)
    inputs = tok_ref[...].astype(F32)
    factor = factor_of(inputs)
    m = inputs * factor
    f = gtok_ref[...] * gain_attn
    gtok_ref[...] = BSTREAM[...] + factor * (f - m * jnp.mean(f * m, -1, keepdims=True))

    if p.inline:
        each_peer(n_z, z, lambda zk: slab_sum(zk, False).wait_recv())
        slab_total = ZS[z].astype(F32)
        for step in range(1, n_z):
            slab_total = slab_total + ZO[lax.rem(z + step, n_z)].astype(F32)
        go_ref[...] = slab_total
        each_peer(n_seq, seq, lambda s: piece_send(s, False).wait_recv())
        for q in range(3):
            each_peer(GROUP, rank, lambda r: grad_piece(q, r, False).wait_recv())
    else:
        stay(G, grad_ref)
        stay(GM.at[0, 0, 0], gm_ref)

    gather_drain(TOK)
    share_drain(0, NM)
    share_drain(1, COT)
    group_sum_drain(0, PARTA)
    group_sum_drain(1, PARTB)
    sum_drain(PART)
    each_peer(n_seq, seq, lambda s: attended_copy(s, True).wait_send())
    each_peer(n_seq, seq, lambda s: back_copy(s, True).wait_send())
    if p.inline:
        each_peer(n_z, z, lambda zk: slab_copy(zk, True).wait_send())
        each_peer(n_dp, dp, lambda d: slab_band(d, True).wait_send())
        slab_half(core).wait_send()
        slab_sum_half().wait_send()
        each_peer(n_dp, dp, lambda d: slab_sum_band(d, True).wait_send())
        each_peer(n_z, z, lambda zk: slab_sum(zk, True).wait_send())
        each_peer(n_seq, seq, lambda s: piece_copy(s, True).wait_send())
        each_peer(n_dp, dp, lambda d: band_copy(d, True).wait_send())
        each_peer(n_dp, dp, lambda d: band_send(d, True).wait_send())
        each_peer(n_seq, seq, lambda s: piece_send(s, True).wait_send())
        for q in range(3):
            each_peer(GROUP, rank, lambda r: feed_piece(q, None, r, True).wait_send())
            each_peer(n_zz, zz, lambda g: each_peer(GROUP, rank, lambda r: feed_piece(q, g, r, True).wait_send()))
            each_peer(GROUP, rank, lambda r: grad_piece(q, r, True).wait_send())
            each_peer(n_zz, zz, lambda g: feed_along_z(q, g, True).wait_send())
            each_peer(n_zz, zz, lambda g: grad_along_z(q, g, True).wait_send())

            def left_along_y(h):
                loop(n_zz, lambda g: feed_along_y(q, h, g, True).wait_send())
                loop(n_zz, lambda g: grad_along_y(q, h, g, True).wait_send())

            each_peer(n_y, y, left_along_y)


def run_layer(plan, hidden, tokens, cotangent, *weights):
    p = plan
    n_seq, n_z, n_dp, B, D = p.n_seq, p.n_z, p.n_dp, p.block, p.width
    vmem = pl.BlockSpec(memory_space=pltpu.VMEM)
    grads = (n_seq, p.rows, p.cols) if p.inline else (D, p.cols)
    dma = pltpu.SemaphoreType.DMA

    def rows(width, kind=BF16):
        return pltpu.VMEM((n_seq, B, width), kind)

    def group(width):
        return pltpu.VMEM((GROUP, B, width), BF16)

    n_y, n_zz = p.n_y, p.n_zz
    feed_grads = (GROUP, p.rows, p.wide) if p.inline else (D, p.wide)
    feed_whole = (n_y, 2, n_zz, LANES, p.wide) if p.inline else (1, 1, 1, D, p.wide)
    section = (2, LANES, p.wide) if p.inline else (1, 16, LANES)
    feed_y = (n_y, n_zz) if p.inline else (1, 1)
    band = p.band if p.inline else 16
    n_gr = n_dp if p.inline else 1
    anywhere = pl.BlockSpec(memory_space=pl.ANY)
    whole = (n_dp, n_z, 2, p.rows, p.joined) if p.inline else (1, 1, 1, D, p.joined)
    slabs = (n_z, p.rows, p.joined) if p.inline else (1, 16, LANES)
    bands = (n_dp,) + slabs if p.inline else (1, 1, 16, LANES)
    outs = [((B, D), BF16), ((B, D), F32)]
    packed = []
    if p.inline:
        r = p.rows
        outs += [(grads, BF16), (feed_grads, BF16), ((r, p.joined), F32)]
        packed = [pltpu.VMEM(shape, BF16) for shape in (grads, feed_grads, (r, p.joined))]
        packed += [pltpu.VMEM((n_zz,) + feed_grads, BF16)]
        packed += [pltpu.VMEM(a.shape, a.dtype) for a in (tokens, cotangent) + weights]
        packed += [dma((11,))]
    else:
        outs += [(grads, BF16), (feed_grads, BF16), ((D, p.joined), BF16)]
    return pl.pallas_call(
        functools.partial(layer_kernel, plan),
        out_shape=[jax.ShapeDtypeStruct(shape, kind) for shape, kind in outs],
        in_specs=[anywhere if p.inline else vmem] * 2 + [anywhere] * len(weights),
        out_specs=[vmem, vmem] + [vmem if p.inline else anywhere] * (len(outs) - 2),
        scratch_shapes=packed + [
            rows(D), rows(D), group(D), group(D),
            pltpu.VMEM(whole, BF16), pltpu.VMEM(whole if p.inline else (1, 1, 1, 16, LANES), BF16), pltpu.VMEM(bands, BF16), pltpu.VMEM(bands, BF16),
            pltpu.VMEM(slabs, BF16), pltpu.VMEM(slabs, BF16),
            pltpu.VMEM((B, p.joined), BF16), pltpu.VMEM((B, p.joined), BF16), rows(p.vp),
            pltpu.VMEM((D, p.cols), BF16), pltpu.VMEM(feed_whole, BF16),
            pltpu.VMEM((D, p.cols), BF16), pltpu.VMEM(feed_whole, BF16),
            pltpu.VMEM(feed_y + section, BF16), pltpu.VMEM(feed_y[1:] + section, BF16),
            pltpu.VMEM((n_gr, band, p.cols), BF16), pltpu.VMEM((band, p.cols), BF16),
            rows(p.qk), rows(p.qk), rows(p.vp), rows(p.vp), rows(p.vp, F32), rows(p.vp, F32),
            rows(p.vp), rows(p.qk), rows(p.vp), rows(p.qk, F32), rows(p.vp, F32),
            group(p.fp), group(p.fp), group(p.fp),
            rows(D), group(D), group(D),
            pltpu.VMEM((n_z, B, D), BF16), pltpu.VMEM((n_z + 1, B, D), BF16),
            pltpu.VMEM((2, 4, B, D), BF16), pltpu.VMEM((2, 2, B, D), BF16), pltpu.VMEM((2, B, D), BF16),
            pltpu.VMEM((B, D), F32), pltpu.VMEM((B, D), F32),
            dma((3, n_seq)), dma((n_seq,)), dma((n_z,)), dma((n_z,)), dma((n_z,)), dma((n_z + 1,)),
            dma((n_seq,)), dma((n_seq,)), dma((n_dp,)), dma((n_dp,)),
            dma((n_dp,)), dma((n_dp,)), dma((n_seq,)), dma((n_seq,)), dma((1,)),
            dma((n_z,)), dma((n_z,)), dma((n_dp,)), dma((n_dp,)), dma((2,)), dma((2,)),
            dma((n_z,)), dma((n_z,)), dma((n_dp,)), dma((n_dp,)),
            dma((n_seq,)), dma((n_seq,)), dma((n_seq,)), dma((n_seq,)),
            dma((2, 3, GROUP)), dma((2, GROUP)), dma((2, 4)), dma((2, 4)), dma((2, 2)), dma((2, 2)), dma((2,)), dma((2,)),
            dma((3, n_zz, GROUP)), dma((3, n_zz, GROUP)), dma((3, n_zz)), dma((3, n_zz)), dma((3, n_y, n_zz)), dma((3, n_y, n_zz)),
            dma((3, GROUP)), dma((3, GROUP)), dma((3, n_zz)), dma((3, n_zz)), dma((3, n_y, n_zz)), dma((3, n_y, n_zz)),
        ],
        compiler_params=pltpu.CompilerParams(
            collective_id=0, has_side_effects=True, vmem_limit_bytes=66_000_000
        ),
    )(tokens, cotangent, *weights)


def finish_kernel(plan, *refs):
    p = plan
    ins, outs, held, made = refs[:5], refs[5:16], refs[16:21], refs[21:30]
    in_sem, out_sem = refs[30:]
    reading = [pltpu.make_async_copy(a, b, in_sem.at[i]) for i, (a, b) in enumerate(zip(ins, held))]
    for copy in reading:
        copy.start()
    sources = [held[0], held[1]] + list(made[:3]) + [held[4]] + list(made[3:])
    sources = sources[:11]
    writing = [pltpu.make_async_copy(a, b, out_sem.at[i]) for i, (a, b) in enumerate(zip(sources, outs))]
    g_query, g_key, g_value, g_gate, g_up, g_down, g_attn, g_mlp = made[:8]
    pieces, feed = held[2], held[3]
    for i in (0, 1, 4):
        reading[i].wait()
    for i in (0, 1, 5):
        writing[i].start()
    reading[3].wait()
    for q, to in enumerate((g_gate, g_up, g_down)):
        for r in range(GROUP):
            to[:, r * p.unit : (r + 1) * p.unit] = feed[r, :, q * p.fp : q * p.fp + p.unit].astype(F32)
        writing[6 + q].start()
    g_mlp[...] = jnp.sum(feed[:, :, p.fp + p.unit : p.fp + p.unit + 1].astype(F32), 0).T
    reading[2].wait()
    gain = jnp.zeros((p.rows, 1), F32)
    for c in range(p.n_seq):
        piece = pieces[c].astype(F32)
        g_query[:, c * p.feat : (c + 1) * p.feat] = piece[:, : p.feat]
        g_key[:, c * p.feat : (c + 1) * p.feat] = piece[:, p.feat : 2 * p.feat]
        g_value[:, c * p.value : (c + 1) * p.value] = piece[:, p.qk : p.qk + p.value]
        gain = gain + piece[:, 2 * p.feat : 2 * p.feat + 1]
    g_attn[...] = gain.T
    for i in (2, 3, 4, 9, 10):
        writing[i].start()
    for copy in writing:
        copy.wait()


def finish(plan, hidden, *owned):
    r = plan.rows
    shapes = [(r, HEADS * FEAT_DIM), (r, HEADS * FEAT_DIM), (r, HEADS * HEAD_V)]
    feeds = [(r, hidden)] * 3 + [(1, r)] * 2
    kinds = [(owned[0].shape, BF16), (owned[1].shape, F32)]
    kinds += [(shape, F32) for shape in shapes + [owned[4].shape] + feeds]
    anywhere = pl.BlockSpec(memory_space=pl.ANY)
    return pl.pallas_call(
        functools.partial(finish_kernel, plan),
        out_shape=[jax.ShapeDtypeStruct(shape, kind) for shape, kind in kinds],
        in_specs=[anywhere] * 5,
        out_specs=[anywhere] * 11,
        scratch_shapes=[pltpu.VMEM(a.shape, a.dtype) for a in owned]
        + [pltpu.VMEM(shape, F32) for shape in shapes + feeds + [(8, LANES)]]
        + [pltpu.SemaphoreType.DMA((5,)), pltpu.SemaphoreType.DMA((11,))],
    )(*owned)


def on_device(tokens, w_query, w_key, w_value, w_output, w_gate, w_up, w_down, norm_attn, norm_mlp, cotangent):
    plan = Plan(
        lax.axis_size("dp"), lax.axis_size("seq"), tokens.shape[0], tokens.shape[1], w_gate.shape[1]
    )
    hidden = w_gate.shape[1]
    if plan.inline:
        results = run_layer(
            plan, hidden, tokens, cotangent, w_query, w_key, w_value, w_output.T, w_gate, w_up, w_down.T,
            norm_attn[None], norm_mlp[None],
        )
        results = finish(plan, hidden, *results)
        layer_out, grad_tokens, g_query, g_key, g_value, g_output, g_gate, g_up, g_down, g_attn, g_mlp = results
        return (
            layer_out, grad_tokens, g_query, g_key, g_value, g_output.T, g_gate, g_up, g_down.T, g_attn[0], g_mlp[0]
        )
    axes = ("dp", "seq")
    dp, seq = lax.axis_index("dp"), lax.axis_index("seq")
    rank = 4 * (dp % 2) + seq % 4
    weights = pack_attention(plan, w_query, w_key, w_value, norm_attn, norm_mlp)
    weights = lax.all_to_all(weights, "seq", split_axis=0, concat_axis=0, tiled=True)
    weights = lax.all_gather(weights, "dp").reshape(plan.width, plan.cols)
    feed = lax.all_gather(pack_feed(plan, w_gate, w_up, w_down), axes, axis=1, tiled=True)
    feed = lax.dynamic_index_in_dim(feed, rank, 0, False)
    output_rows = lax.all_gather(pack_output(plan, w_output), axes, axis=0, tiled=True)
    layer_out, grad_tokens, grads, grads_feed, grad_output = run_layer(
        plan, hidden, tokens, cotangent, weights, feed, output_rows
    )
    grads = lax.psum_scatter(grads, "dp", scatter_dimension=0, tiled=True)
    grads = grads.reshape(plan.n_seq, plan.rows, plan.cols)
    grads = lax.all_to_all(grads, "seq", split_axis=0, concat_axis=0, tiled=True)
    spread = jnp.zeros((GROUP, plan.width, plan.wide), BF16)
    spread = lax.dynamic_update_index_in_dim(spread, grads_feed, rank, 0)
    grads_feed = lax.psum_scatter(spread, axes, scatter_dimension=1, tiled=True)
    grad_output = lax.psum_scatter(grad_output, axes, scatter_dimension=0, tiled=True).astype(F32)
    return (layer_out, grad_tokens) + unpack_grads(plan, grads, grads_feed, grad_output)


def solution(mesh):
    rows, cols, vec = P(("dp", "seq"), None), P(None, ("dp", "seq")), P(("dp", "seq"))
    return jax.shard_map(
        on_device,
        mesh=mesh,
        in_specs=(rows, rows, rows, rows, cols, rows, rows, cols, vec, vec, rows),
        out_specs=(rows, rows, rows, rows, rows, cols, rows, rows, cols, vec, vec),
        check_vma=False,
    )
```
